512 devices in a mesh: blk: 64 (over y, x, z_lo), rep: 8 (over z_hi, core).
Axes of the slice: x: 4, y: 8, z: 8 (z_hi: 4, z_lo: 2; z = z_hi * 2 + z_lo), core: 2. Of those that a mesh axis runs over, the one named last changes fastest.
Arguments:
- hidden_pre: bfloat16 [8192, 1024], P('blk'), may hold values from -6 to 6
- adj_vals: bfloat16 [64, 16, 128, 128], P('blk', 'rep'), may hold values from -0.125 to 0.125
- adj_cols: int32 [64, 16], P('blk', 'rep'), may hold values from 0 to 63, as said below
- w_out: bfloat16 [1024, 1024], replicated, may hold values from -0.1875 to 0.1875
- cotangent: bfloat16 [8192, 1024], P('blk'), may hold values from -6 to 6
Outputs:
- aggregated: bfloat16 [8192, 1024], P('blk', 'rep')
- grad_weight: float32 [1024, 1024], P('blk', 'rep')
- grad_pre: bfloat16 [8192, 1024], P('blk', 'rep')
The draws below stay inside these ranges and needn't reach their ends.
Inputs may be any that keep to these rules, and one draw needn't show every extreme that they name: For block-row i, let b = i // 1 and, for slot k, s = (b - adj_cols[i, k]) mod (64). Then s // 8 == k // 2, and the slots of one block-row with equal k // 2 have distinct s.
All inputs are finite; a program needn't handle non-finite values.
Results may differ from the reference program's by a relative error of at most 0.014.
Values may be sent and summed in bfloat16 or wider, within the bound.
A program may use at most 64 MiB of HBM per device.

```python
import jax
import jax.numpy as jnp
from jax import lax

D = 1024
TILE = 128
SLOTS = 16
RB = 1
NB = 64
ROWS = 8192
SPAN = 8
SLOTS_REP = 2


def draw_adj_cols(key, part):
    owner_count = NB // RB
    groups = SLOTS // SLOTS_REP
    first_key, second_key = jax.random.split(key)
    row_owner = jnp.arange(NB, dtype=jnp.int32) // RB
    scores = jax.random.randint(first_key, (NB, groups, SPAN), 0, 1 << 20) * SPAN + jnp.arange(SPAN, dtype=jnp.int32)
    order_idx = jnp.argsort(scores, axis=-1)[:, :, :SLOTS_REP].astype(jnp.int32)
    sections = jnp.arange(groups, dtype=jnp.int32)[None, :, None] * SPAN + order_idx
    target = jnp.mod(row_owner[:, None, None] - sections, owner_count)
    inner = jax.random.randint(second_key, (NB, groups, SLOTS_REP), 0, RB)
    return (target * RB + inner).reshape(NB, SLOTS).astype(jnp.int32)


def block_levels(key, dims, cuts, low, high):
    level = 1.0
    for position, parts in cuts:
        draws = jax.random.uniform(jax.random.fold_in(jax.random.fold_in(key, 6), position), (parts,), jnp.float32, low / len(cuts), high / len(cuts))
        level = level * jnp.repeat(jnp.exp(draws), dims[position] // parts).reshape((-1,) + (1,) * (len(dims) - 1 - position))
    return level


def scatter_about(own_key, shape, deviation, most, pieces=(), kind=jnp.bfloat16):
    factor_of = block_levels(own_key, shape, pieces, -0.22, 0.18) if pieces else 1.0
    drawn = jax.random.normal(own_key, shape, jnp.float32) * deviation * factor_of
    return jnp.minimum(jnp.maximum(drawn, -most), most).astype(kind)


def setup_inputs(seed: int = 0) -> dict:
    key_of = jax.random.split(jax.random.key(seed), 6)
    return {
        "hidden_pre": scatter_about(key_of[0], (ROWS, D), 1.0, 6.0, ((0, 64),)),
        "adj_vals": scatter_about(key_of[1], (NB, SLOTS, TILE, TILE), (TILE * SLOTS) ** -0.5, 0.125, ((0, 64), (1, 8))),
        "adj_cols": draw_adj_cols(jax.random.fold_in(key_of[5], 71), 0),
        "w_out": scatter_about(key_of[3], (D, D), D ** -0.5, 0.1875),
        "cotangent": scatter_about(key_of[4], (ROWS, D), 1.0, 6.0, ((0, 64),)),
    }


def aggregate(adj_vals, adj_cols, features):
    blocks = features.reshape(NB, TILE, D)

    def one_row(row_pair):
        tile_vals, columns = row_pair
        picked = blocks[columns].astype(jnp.float32)
        return jnp.einsum('kab,kbd->ad', tile_vals.astype(jnp.float32), picked)

    return lax.map(one_row, (adj_vals, adj_cols)).reshape(ROWS, D)


def transposed(adj_vals, adj_cols, features):
    blocks = features.reshape(NB, TILE, D)

    def one_row(row_pair):
        tile_vals, grad_block = row_pair
        return jnp.einsum('kab,ad->kbd', tile_vals.astype(jnp.float32), grad_block.astype(jnp.float32))

    contribution = lax.map(one_row, (adj_vals, blocks))
    summed = jax.ops.segment_sum(contribution.reshape(NB * SLOTS, TILE, D), adj_cols.reshape(-1).astype(jnp.int32), num_segments=NB)
    return summed.reshape(ROWS, D)


def reference(hidden_pre, adj_vals, adj_cols, w_out, cotangent):
    hidden_act = jnp.maximum(hidden_pre, 0)
    projected = jnp.dot(hidden_act, w_out, preferred_element_type=jnp.float32).astype(jnp.bfloat16)
    aggregated = aggregate(adj_vals, adj_cols, projected).astype(jnp.bfloat16)
    back_grad = transposed(adj_vals, adj_cols, cotangent).astype(jnp.bfloat16)
    grad_weight = jnp.dot(hidden_act.T, back_grad, preferred_element_type=jnp.float32)
    grad_in = jnp.dot(back_grad, w_out.T, preferred_element_type=jnp.float32)
    grad_pre = jnp.where(hidden_pre > 0, grad_in, 0.0).astype(jnp.bfloat16)
    return aggregated, grad_weight, grad_pre
```

```python
import math

import jax
import jax.numpy as jnp
from jax import lax
from jax.sharding import Mesh
from jax.sharding import PartitionSpec as P

BLK = ("by", "bx", "bz")
REP = ("rz", "rc")
EVERY = BLK + REP


def shifted_pairs(blk_count, rep_count, per_rep):
    pairs = []
    for b in range(blk_count):
        for r in range(rep_count):
            pairs.append((b * rep_count + r, ((b + per_rep * r) % blk_count) * rep_count + r))
    return pairs


def ring_pairs(count, steps):
    return [(source, (source + steps) % count) for source in range(count)]


def staged_scatter(value, axes, dim):
    sizes = [lax.axis_size(a) for a in axes]
    full = value.shape[dim]
    rest = full // math.prod(sizes)
    shape = value.shape[:dim] + tuple(sizes) + (rest,) + value.shape[dim + 1 :]
    moved = value.reshape(shape)
    order = list(range(dim)) + [dim + i for i in reversed(range(len(axes)))]
    order += list(range(dim + len(axes), len(shape)))
    moved = jnp.transpose(moved, order).reshape(value.shape)
    for a in reversed(axes):
        moved = lax.psum_scatter(moved, a, scatter_dimension=dim, tiled=True)
    return moved


def shards(hidden_pre, adj_vals, adj_cols, w_out, cotangent):
    row_count, feature_width = hidden_pre.shape
    blk_count = lax.axis_size(BLK)
    rep_count = lax.axis_size(REP)
    span = blk_count // rep_count
    blk_pos = lax.axis_index(BLK)
    rep_pos = lax.axis_index(REP)
    cols_here = feature_width // rep_count
    slots = adj_vals.shape[1]

    hidden_act = jnp.maximum(hidden_pre, 0)
    projected = jnp.dot(hidden_act, w_out, preferred_element_type=jnp.float32).astype(jnp.bfloat16)
    own_vals = adj_vals[0]
    own_cols = adj_cols[0]
    section = jnp.mod(blk_pos - own_cols, blk_count) - rep_pos * span

    visiting = lax.ppermute(projected, EVERY, shifted_pairs(blk_count, rep_count, span))
    back = shifted_pairs(blk_count, rep_count, -span)
    cot_cur = lax.ppermute(cotangent, EVERY, back)
    vals_cur = lax.ppermute(own_vals, EVERY, back)
    cols_cur = lax.ppermute(own_cols, EVERY, back)

    out_sum = jnp.zeros((row_count, feature_width), jnp.float32)
    back_sum = jnp.zeros((row_count, feature_width), jnp.float32)
    for turn in range(span):
        chosen = jnp.zeros_like(own_vals[0])
        for k in range(slots):
            chosen = chosen + jnp.where(section[k] == turn, own_vals[k], 0)
        out_sum = out_sum + jnp.dot(chosen, visiting, preferred_element_type=jnp.float32)
        chosen_back = jnp.zeros_like(own_vals[0])
        for k in range(slots):
            chosen_back = chosen_back + jnp.where(cols_cur[k] == blk_pos, vals_cur[k], 0)
        back_sum = back_sum + lax.dot_general(
            chosen_back, cot_cur, (((0,), (0,)), ((), ())), preferred_element_type=jnp.float32
        )
        if turn < span - 1:
            visiting = lax.ppermute(visiting, BLK, ring_pairs(blk_count, 1))
            cot_cur = lax.ppermute(cot_cur, BLK, ring_pairs(blk_count, -1))
            vals_cur = lax.ppermute(vals_cur, BLK, ring_pairs(blk_count, -1))
            cols_cur = lax.ppermute(cols_cur, BLK, ring_pairs(blk_count, -1))

    out_part = staged_scatter(out_sum.astype(jnp.bfloat16), REP, 1)
    back_part = staged_scatter(back_sum, REP, 1)
    back_grad = back_part.astype(jnp.bfloat16)
    term = lax.dot_general(
        hidden_act, back_grad, (((0,), (0,)), ((), ())), preferred_element_type=jnp.float32
    )
    grad_weight = staged_scatter(term, BLK, 0)
    back_full = lax.all_gather(back_grad, REP, axis=1, tiled=True)
    w_rows = lax.dynamic_slice_in_dim(w_out, rep_pos * cols_here, cols_here, 0)
    grad_in = lax.dot_general(
        back_full, w_rows, (((1,), (1,)), ((), ())), preferred_element_type=jnp.float32
    )
    pre_part = lax.dynamic_slice_in_dim(hidden_pre, rep_pos * cols_here, cols_here, 1)
    grad_pre = jnp.where(pre_part > 0, grad_in, 0.0).astype(jnp.bfloat16)
    return (out_part, grad_weight, grad_pre)


def solution(mesh):
    blk_count, rep_count = mesh.devices.shape
    fine = Mesh(mesh.devices.reshape(8, blk_count // 16, 2, rep_count // 2, 2), EVERY)
    placed = (P(BLK, None), P(BLK, REP, None, None), P(BLK, REP), P(), P(BLK, None))
    return jax.shard_map(
        shards,
        mesh=fine,
        in_specs=placed,
        out_specs=(P(BLK, REP), P(BLK, REP), P(BLK, REP)),
        check_vma=False,
    )
```

```python
import functools
import math

import jax
import jax.numpy as jnp
from jax import lax
from jax.experimental import pallas as pl
from jax.experimental.pallas import tpu as pltpu
from jax.sharding import Mesh
from jax.sharding import PartitionSpec as P

MESH_IDS = pl.DeviceIdType.MESH

BLK = ("by", "bx", "bz")
REP = ("rz", "rc")
EVERY = BLK + REP


def shifted_pairs(blk_count, rep_count, per_rep):
    pairs = []
    for b in range(blk_count):
        for r in range(rep_count):
            pairs.append((b * rep_count + r, ((b + per_rep * r) % blk_count) * rep_count + r))
    return pairs


def ring_pairs(count, steps):
    return [(source, (source + steps) % count) for source in range(count)]


def staged_scatter(value, axes, dim):
    sizes = [lax.axis_size(a) for a in axes]
    full = value.shape[dim]
    rest = full // math.prod(sizes)
    shape = value.shape[:dim] + tuple(sizes) + (rest,) + value.shape[dim + 1 :]
    moved = value.reshape(shape)
    order = list(range(dim)) + [dim + i for i in reversed(range(len(axes)))]
    order += list(range(dim + len(axes), len(shape)))
    moved = jnp.transpose(moved, order).reshape(value.shape)
    for a in reversed(axes):
        moved = lax.psum_scatter(moved, a, scatter_dimension=dim, tiled=True)
    return moved


def exchange_kernel(group, sizes, every, broadcast, src_ref, out_ref, landed, send_sem, recv_sem):
    count = math.prod(sizes)
    me = 0
    for a, s in zip(group, sizes):
        me = me * s + lax.axis_index(a)

    def target(d):
        coords = {}
        rest = d
        for a, s in reversed(list(zip(group, sizes))):
            coords[a] = rest % s
            rest = rest // s
        return tuple(coords[a] if a in coords else lax.axis_index(a) for a in every)

    def source(d):
        return src_ref if broadcast else src_ref.at[d]

    def copy_to(d, o):
        return pltpu.make_async_remote_copy(
            src_ref=source(d),
            dst_ref=landed.at[me],
            send_sem=send_sem.at[o],
            recv_sem=recv_sem.at[me],
            device_id=target(d),
            device_id_type=MESH_IDS,
        )

    barrier = pltpu.get_barrier_semaphore()

    def greet(o, carry):
        pl.semaphore_signal(barrier, inc=1, device_id=target((me + o) % count), device_id_type=MESH_IDS)
        return carry

    lax.fori_loop(1, count, greet, 0)
    pl.semaphore_wait(barrier, count - 1)

    def send(o, carry):
        copy_to((me + o) % count, o).start()
        return carry

    lax.fori_loop(1, count, send, 0)
    out_ref[me] = src_ref[...] if broadcast else src_ref[me]

    def finish(o, carry):
        copy_to((me + o) % count, o).wait_send()
        sender = (me + count - o) % count
        incoming = pltpu.make_async_remote_copy(
            src_ref=source(sender),
            dst_ref=landed.at[sender],
            send_sem=send_sem.at[o],
            recv_sem=recv_sem.at[sender],
            device_id=target(sender),
            device_id_type=MESH_IDS,
        )
        incoming.wait_recv()
        out_ref[sender] = landed[sender]
        return carry

    lax.fori_loop(1, count, finish, 0)


def exchange(blocks, group, every, collective, broadcast=False):
    sizes = tuple(lax.axis_size(a) for a in group)
    count = math.prod(sizes)
    shape = (count,) + (blocks.shape if broadcast else blocks.shape[1:])
    size = math.prod(shape) * blocks.dtype.itemsize
    return pl.pallas_call(
        functools.partial(exchange_kernel, group, sizes, every, broadcast),
        out_shape=jax.ShapeDtypeStruct(shape, blocks.dtype),
        in_specs=[pl.BlockSpec(memory_space=pltpu.VMEM)],
        out_specs=pl.BlockSpec(memory_space=pltpu.VMEM),
        scratch_shapes=[
            pltpu.VMEM(shape, blocks.dtype),
            pltpu.SemaphoreType.DMA((count,)),
            pltpu.SemaphoreType.DMA((count,)),
        ],
        compiler_params=pltpu.CompilerParams(collective_id=collective, has_side_effects=True),
        cost_estimate=pl.CostEstimate(flops=0, transcendentals=0, bytes_accessed=3 * size),
    )(blocks)


def shards(hidden_pre, adj_vals, adj_cols, w_out, cotangent):
    row_count, feature_width = hidden_pre.shape
    blk_count = lax.axis_size(BLK)
    rep_count = lax.axis_size(REP)
    span = blk_count // rep_count
    blk_pos = lax.axis_index(BLK)
    rep_pos = lax.axis_index(REP)
    cols_here = feature_width // rep_count
    slots = adj_vals.shape[1]

    hidden_act = jnp.maximum(hidden_pre, 0)
    projected = jnp.dot(hidden_act, w_out, preferred_element_type=jnp.float32).astype(jnp.bfloat16)
    own_vals = adj_vals[0]
    own_cols = adj_cols[0]
    section = jnp.mod(blk_pos - own_cols, blk_count) - rep_pos * span

    visiting = lax.ppermute(projected, EVERY, shifted_pairs(blk_count, rep_count, span))
    back = shifted_pairs(blk_count, rep_count, -span)
    cot_cur = lax.ppermute(cotangent, EVERY, back)
    vals_cur = lax.ppermute(own_vals, EVERY, back)
    cols_cur = lax.ppermute(own_cols, EVERY, back)

    out_sum = jnp.zeros((row_count, feature_width), jnp.float32)
    back_sum = jnp.zeros((row_count, feature_width), jnp.float32)
    for turn in range(span):
        chosen = jnp.zeros_like(own_vals[0])
        for k in range(slots):
            chosen = chosen + jnp.where(section[k] == turn, own_vals[k], 0)
        out_sum = out_sum + jnp.dot(chosen, visiting, preferred_element_type=jnp.float32)
        chosen_back = jnp.zeros_like(own_vals[0])
        for k in range(slots):
            chosen_back = chosen_back + jnp.where(cols_cur[k] == blk_pos, vals_cur[k], 0)
        back_sum = back_sum + lax.dot_general(
            chosen_back, cot_cur, (((0,), (0,)), ((), ())), preferred_element_type=jnp.float32
        )
        if turn < span - 1:
            visiting = lax.ppermute(visiting, BLK, ring_pairs(blk_count, 1))
            cot_cur = lax.ppermute(cot_cur, BLK, ring_pairs(blk_count, -1))
            vals_cur = lax.ppermute(vals_cur, BLK, ring_pairs(blk_count, -1))
            cols_cur = lax.ppermute(cols_cur, BLK, ring_pairs(blk_count, -1))

    rows = out_sum.shape[0]
    both = jnp.stack([out_sum, back_sum]).reshape(2, rows, rep_count, cols_here)
    summed = exchange(jnp.transpose(both, (2, 0, 1, 3)), REP, EVERY, 0).sum(0)
    out_part = summed[0].astype(jnp.bfloat16)
    back_grad = summed[1].astype(jnp.bfloat16)
    term = lax.dot_general(
        hidden_act, back_grad, (((0,), (0,)), ((), ())), preferred_element_type=jnp.float32
    )
    grad_weight = exchange(term.reshape(blk_count, -1, cols_here), BLK, EVERY, 1).sum(0)
    gathered = exchange(back_grad, REP, EVERY, 2, broadcast=True)
    back_full = jnp.transpose(gathered, (1, 0, 2)).reshape(rows, feature_width)
    w_rows = lax.dynamic_slice_in_dim(w_out, rep_pos * cols_here, cols_here, 0)
    grad_in = lax.dot_general(
        back_full, w_rows, (((1,), (1,)), ((), ())), preferred_element_type=jnp.float32
    )
    pre_part = lax.dynamic_slice_in_dim(hidden_pre, rep_pos * cols_here, cols_here, 1)
    grad_pre = jnp.where(pre_part > 0, grad_in, 0.0).astype(jnp.bfloat16)
    return (out_part, grad_weight, grad_pre)


def solution(mesh):
    blk_count, rep_count = mesh.devices.shape
    fine = Mesh(mesh.devices.reshape(8, blk_count // 16, 2, rep_count // 2, 2), EVERY)
    placed = (P(BLK, None), P(BLK, REP, None, None), P(BLK, REP), P(), P(BLK, None))
    return jax.shard_map(
        shards,
        mesh=fine,
        in_specs=placed,
        out_specs=(P(BLK, REP), P(BLK, REP), P(BLK, REP)),
        check_vma=False,
    )
```

```python
import functools
import math

import jax
import jax.numpy as jnp
from jax import lax
from jax.experimental import pallas as pl
from jax.experimental.pallas import tpu as pltpu
from jax.sharding import Mesh
from jax.sharding import PartitionSpec as P

MESH_IDS = pl.DeviceIdType.MESH

BLK = ("by", "bx", "bz")
REP = ("rz", "rc")
EVERY = BLK + REP


def shifted_pairs(blk_count, rep_count, per_rep):
    pairs = []
    for b in range(blk_count):
        for r in range(rep_count):
            pairs.append((b * rep_count + r, ((b + per_rep * r) % blk_count) * rep_count + r))
    return pairs


def ring_pairs(count, steps):
    return [(source, (source + steps) % count) for source in range(count)]


def staged_scatter(value, axes, dim):
    sizes = [lax.axis_size(a) for a in axes]
    full = value.shape[dim]
    rest = full // math.prod(sizes)
    shape = value.shape[:dim] + tuple(sizes) + (rest,) + value.shape[dim + 1 :]
    moved = value.reshape(shape)
    order = list(range(dim)) + [dim + i for i in reversed(range(len(axes)))]
    order += list(range(dim + len(axes), len(shape)))
    moved = jnp.transpose(moved, order).reshape(value.shape)
    for a in reversed(axes):
        moved = lax.psum_scatter(moved, a, scatter_dimension=dim, tiled=True)
    return moved


def exchange_kernel(group, sizes, every, broadcast, src_ref, out_ref, landed, send_sem, recv_sem):
    count = math.prod(sizes)
    me = 0
    for a, s in zip(group, sizes):
        me = me * s + lax.axis_index(a)

    def target(d):
        coords = {}
        rest = d
        for a, s in reversed(list(zip(group, sizes))):
            coords[a] = rest % s
            rest = rest // s
        return tuple(coords[a] if a in coords else lax.axis_index(a) for a in every)

    def source(d):
        return src_ref if broadcast else src_ref.at[d]

    def copy_to(d, o):
        return pltpu.make_async_remote_copy(
            src_ref=source(d),
            dst_ref=landed.at[me],
            send_sem=send_sem.at[o],
            recv_sem=recv_sem.at[me],
            device_id=target(d),
            device_id_type=MESH_IDS,
        )

    barrier = pltpu.get_barrier_semaphore()

    def greet(o, carry):
        pl.semaphore_signal(barrier, inc=1, device_id=target((me + o) % count), device_id_type=MESH_IDS)
        return carry

    lax.fori_loop(1, count, greet, 0)
    pl.semaphore_wait(barrier, count - 1)

    def send(o, carry):
        copy_to((me + o) % count, o).start()
        return carry

    lax.fori_loop(1, count, send, 0)
    out_ref[me] = src_ref[...] if broadcast else src_ref[me]

    def finish(o, carry):
        copy_to((me + o) % count, o).wait_send()
        sender = (me + count - o) % count
        incoming = pltpu.make_async_remote_copy(
            src_ref=source(sender),
            dst_ref=landed.at[sender],
            send_sem=send_sem.at[o],
            recv_sem=recv_sem.at[sender],
            device_id=target(sender),
            device_id_type=MESH_IDS,
        )
        incoming.wait_recv()
        out_ref[sender] = landed[sender]
        return carry

    lax.fori_loop(1, count, finish, 0)


def exchange(blocks, group, every, collective, broadcast=False):
    sizes = tuple(lax.axis_size(a) for a in group)
    count = math.prod(sizes)
    shape = (count,) + (blocks.shape if broadcast else blocks.shape[1:])
    size = math.prod(shape) * blocks.dtype.itemsize
    return pl.pallas_call(
        functools.partial(exchange_kernel, group, sizes, every, broadcast),
        out_shape=jax.ShapeDtypeStruct(shape, blocks.dtype),
        in_specs=[pl.BlockSpec(memory_space=pltpu.VMEM)],
        out_specs=pl.BlockSpec(memory_space=pltpu.VMEM),
        scratch_shapes=[
            pltpu.VMEM(shape, blocks.dtype),
            pltpu.SemaphoreType.DMA((count,)),
            pltpu.SemaphoreType.DMA((count,)),
        ],
        compiler_params=pltpu.CompilerParams(collective_id=collective, has_side_effects=True),
        cost_estimate=pl.CostEstimate(flops=0, transcendentals=0, bytes_accessed=3 * size),
    )(blocks)


def window_kernel(blk_sizes, rep_sizes, every, proj_ref, cot_ref, chosen_ref, sent_ref, out_ref, back_ref,
                  p_got, cot_got, ch_got, send_sem, recv_sem, local_sem):
    blk_count = math.prod(blk_sizes)
    span = chosen_ref.shape[0]
    blk_axes, rep_axes = every[: len(blk_sizes)], every[len(blk_sizes) :]
    b = 0
    for a, s in zip(blk_axes, blk_sizes):
        b = b * s + lax.axis_index(a)
    r = 0
    for a, s in zip(rep_axes, rep_sizes):
        r = r * s + lax.axis_index(a)

    def target(j):
        coords = []
        rest = j
        for s in reversed(blk_sizes):
            coords.append(rest % s)
            rest = rest // s
        return tuple(reversed(coords)) + tuple(lax.axis_index(a) for a in rep_axes)

    def copies(t):
        ahead = target((b + span * r + t) % blk_count)
        behind = target((b + blk_count - span * r - t) % blk_count)
        return (
            pltpu.make_async_remote_copy(proj_ref, p_got.at[t], send_sem.at[0, t], recv_sem.at[0, t],
                                         device_id=ahead, device_id_type=MESH_IDS),
            pltpu.make_async_remote_copy(cot_ref, cot_got.at[t], send_sem.at[1, t], recv_sem.at[1, t],
                                         device_id=behind, device_id_type=MESH_IDS),
            pltpu.make_async_remote_copy(sent_ref.at[t], ch_got.at[t], send_sem.at[2, t], recv_sem.at[2, t],
                                         device_id=behind, device_id_type=MESH_IDS),
        )

    def local_copies():
        return (
            pltpu.make_async_copy(proj_ref, p_got.at[0], local_sem.at[0]),
            pltpu.make_async_copy(cot_ref, cot_got.at[0], local_sem.at[1]),
            pltpu.make_async_copy(sent_ref.at[0], ch_got.at[0], local_sem.at[2]),
        )

    barrier = pltpu.get_barrier_semaphore()
    for t in range(span):
        ahead = target((b + span * r + t) % blk_count)
        behind = target((b + blk_count - span * r - t) % blk_count)

        def greet(ahead=ahead, behind=behind):
            pl.semaphore_signal(barrier, inc=1, device_id=ahead, device_id_type=MESH_IDS)
            pl.semaphore_signal(barrier, inc=1, device_id=behind, device_id_type=MESH_IDS)

        if t == 0:
            pl.when(r != 0)(greet)
        else:
            greet()

    @pl.when(r != 0)
    def _():
        pl.semaphore_wait(barrier, 2 * span)
        for c in copies(0):
            c.start()

    @pl.when(r == 0)
    def _():
        pl.semaphore_wait(barrier, 2 * span - 2)
        for c in local_copies():
            c.start()

    for t in range(1, span):
        for c in copies(t):
            c.start()

    @pl.when(r != 0)
    def _():
        for c in copies(0):
            c.wait_recv()

    @pl.when(r == 0)
    def _():
        for c in local_copies():
            c.wait()

    for t in range(span):
        if t > 0:
            for c in copies(t):
                c.wait_recv()
        part = jnp.dot(chosen_ref[t], p_got[t], preferred_element_type=jnp.float32)
        back = jnp.dot(ch_got[t], cot_got[t], preferred_element_type=jnp.float32)
        if t == 0:
            out_ref[...] = part
            back_ref[...] = back
        else:
            out_ref[...] += part
            back_ref[...] += back

    @pl.when(r != 0)
    def _():
        for c in copies(0):
            c.wait_send()

    for t in range(1, span):
        for c in copies(t):
            c.wait_send()


def window(projected, cotangent, chosen, chosen_t, blk_sizes, rep_sizes, every, collective):
    span = chosen.shape[0]
    rows, width = projected.shape
    vmem = pl.BlockSpec(memory_space=pltpu.VMEM)
    moved = (2 * rows * width * 2 + rows * rows * 2) * span
    return pl.pallas_call(
        functools.partial(window_kernel, blk_sizes, rep_sizes, every),
        out_shape=(
            jax.ShapeDtypeStruct((rows, width), jnp.float32),
            jax.ShapeDtypeStruct((rows, width), jnp.float32),
        ),
        in_specs=[vmem, vmem, vmem, vmem],
        out_specs=(vmem, vmem),
        scratch_shapes=[
            pltpu.VMEM((span, rows, width), projected.dtype),
            pltpu.VMEM((span, rows, width), cotangent.dtype),
            pltpu.VMEM((span, rows, rows), chosen.dtype),
            pltpu.SemaphoreType.DMA((3, span)),
            pltpu.SemaphoreType.DMA((3, span)),
            pltpu.SemaphoreType.DMA((3,)),
        ],
        compiler_params=pltpu.CompilerParams(collective_id=collective, has_side_effects=True),
        cost_estimate=pl.CostEstimate(
            flops=4 * span * rows * rows * width, transcendentals=0, bytes_accessed=2 * moved
        ),
    )(projected, cotangent, chosen, chosen_t)


def shards(hidden_pre, adj_vals, adj_cols, w_out, cotangent):
    row_count, feature_width = hidden_pre.shape
    blk_count = lax.axis_size(BLK)
    rep_count = lax.axis_size(REP)
    span = blk_count // rep_count
    blk_pos = lax.axis_index(BLK)
    rep_pos = lax.axis_index(REP)
    cols_here = feature_width // rep_count
    slots = adj_vals.shape[1]

    hidden_act = jnp.maximum(hidden_pre, 0)
    projected = jnp.dot(hidden_act, w_out, preferred_element_type=jnp.float32).astype(jnp.bfloat16)
    own_vals = adj_vals[0]
    own_cols = adj_cols[0]
    section = jnp.mod(blk_pos - own_cols, blk_count) - rep_pos * span

    chosen = jnp.stack(
        [
            sum(jnp.where(section[k] == turn, own_vals[k], 0) for k in range(slots))
            for turn in range(span)
        ]
    )
    blk_sizes = tuple(lax.axis_size(a) for a in BLK)
    rep_sizes = tuple(lax.axis_size(a) for a in REP)
    out_sum, back_sum = window(
        projected, cotangent, chosen, jnp.transpose(chosen, (0, 2, 1)), blk_sizes, rep_sizes, EVERY, 3
    )

    rows = out_sum.shape[0]
    both = jnp.stack([out_sum, back_sum]).reshape(2, rows, rep_count, cols_here)
    summed = exchange(jnp.transpose(both, (2, 0, 1, 3)), REP, EVERY, 0).sum(0)
    out_part = summed[0].astype(jnp.bfloat16)
    back_grad = summed[1].astype(jnp.bfloat16)
    term = lax.dot_general(
        hidden_act, back_grad, (((0,), (0,)), ((), ())), preferred_element_type=jnp.float32
    )
    grad_weight = exchange(term.reshape(blk_count, -1, cols_here), BLK, EVERY, 1).sum(0)
    gathered = exchange(back_grad, REP, EVERY, 2, broadcast=True)
    back_full = jnp.transpose(gathered, (1, 0, 2)).reshape(rows, feature_width)
    w_rows = lax.dynamic_slice_in_dim(w_out, rep_pos * cols_here, cols_here, 0)
    grad_in = lax.dot_general(
        back_full, w_rows, (((1,), (1,)), ((), ())), preferred_element_type=jnp.float32
    )
    pre_part = lax.dynamic_slice_in_dim(hidden_pre, rep_pos * cols_here, cols_here, 1)
    grad_pre = jnp.where(pre_part > 0, grad_in, 0.0).astype(jnp.bfloat16)
    return (out_part, grad_weight, grad_pre)


def solution(mesh):
    blk_count, rep_count = mesh.devices.shape
    fine = Mesh(mesh.devices.reshape(8, blk_count // 16, 2, rep_count // 2, 2), EVERY)
    placed = (P(BLK, None), P(BLK, REP, None, None), P(BLK, REP), P(), P(BLK, None))
    return jax.shard_map(
        shards,
        mesh=fine,
        in_specs=placed,
        out_specs=(P(BLK, REP), P(BLK, REP), P(BLK, REP)),
        check_vma=False,
    )
```

```python
import functools
import math

import jax
import jax.numpy as jnp
from jax import lax
from jax.experimental import pallas as pl
from jax.experimental.pallas import tpu as pltpu
from jax.sharding import Mesh
from jax.sharding import PartitionSpec as P

MESH_IDS = pl.DeviceIdType.MESH

BLK = ("by", "bx", "bz")
REP = ("rz", "rc")
EVERY = BLK + REP


def shifted_pairs(blk_count, rep_count, per_rep):
    pairs = []
    for b in range(blk_count):
        for r in range(rep_count):
            pairs.append((b * rep_count + r, ((b + per_rep * r) % blk_count) * rep_count + r))
    return pairs


def ring_pairs(count, steps):
    return [(source, (source + steps) % count) for source in range(count)]


def staged_scatter(value, axes, dim):
    sizes = [lax.axis_size(a) for a in axes]
    full = value.shape[dim]
    rest = full // math.prod(sizes)
    shape = value.shape[:dim] + tuple(sizes) + (rest,) + value.shape[dim + 1 :]
    moved = value.reshape(shape)
    order = list(range(dim)) + [dim + i for i in reversed(range(len(axes)))]
    order += list(range(dim + len(axes), len(shape)))
    moved = jnp.transpose(moved, order).reshape(value.shape)
    for a in reversed(axes):
        moved = lax.psum_scatter(moved, a, scatter_dimension=dim, tiled=True)
    return moved


def exchange_kernel(group, sizes, every, broadcast, src_ref, out_ref, landed, send_sem, recv_sem):
    count = math.prod(sizes)
    me = 0
    for a, s in zip(group, sizes):
        me = me * s + lax.axis_index(a)

    def target(d):
        coords = {}
        rest = d
        for a, s in reversed(list(zip(group, sizes))):
            coords[a] = rest % s
            rest = rest // s
        return tuple(coords[a] if a in coords else lax.axis_index(a) for a in every)

    def source(d):
        return src_ref if broadcast else src_ref.at[d]

    def copy_to(d, o):
        return pltpu.make_async_remote_copy(
            src_ref=source(d),
            dst_ref=landed.at[me],
            send_sem=send_sem.at[o],
            recv_sem=recv_sem.at[me],
            device_id=target(d),
            device_id_type=MESH_IDS,
        )

    barrier = pltpu.get_barrier_semaphore()

    def greet(o, carry):
        pl.semaphore_signal(barrier, inc=1, device_id=target((me + o) % count), device_id_type=MESH_IDS)
        return carry

    lax.fori_loop(1, count, greet, 0)
    pl.semaphore_wait(barrier, count - 1)

    def send(o, carry):
        copy_to((me + o) % count, o).start()
        return carry

    lax.fori_loop(1, count, send, 0)
    out_ref[me] = src_ref[...] if broadcast else src_ref[me]

    def finish(o, carry):
        copy_to((me + o) % count, o).wait_send()
        sender = (me + count - o) % count
        incoming = pltpu.make_async_remote_copy(
            src_ref=source(sender),
            dst_ref=landed.at[sender],
            send_sem=send_sem.at[o],
            recv_sem=recv_sem.at[sender],
            device_id=target(sender),
            device_id_type=MESH_IDS,
        )
        incoming.wait_recv()
        out_ref[sender] = landed[sender]
        return carry

    lax.fori_loop(1, count, finish, 0)


def exchange(blocks, group, every, collective, broadcast=False):
    sizes = tuple(lax.axis_size(a) for a in group)
    count = math.prod(sizes)
    shape = (count,) + (blocks.shape if broadcast else blocks.shape[1:])
    size = math.prod(shape) * blocks.dtype.itemsize
    return pl.pallas_call(
        functools.partial(exchange_kernel, group, sizes, every, broadcast),
        out_shape=jax.ShapeDtypeStruct(shape, blocks.dtype),
        in_specs=[pl.BlockSpec(memory_space=pltpu.VMEM)],
        out_specs=pl.BlockSpec(memory_space=pltpu.VMEM),
        scratch_shapes=[
            pltpu.VMEM(shape, blocks.dtype),
            pltpu.SemaphoreType.DMA((count,)),
            pltpu.SemaphoreType.DMA((count,)),
        ],
        compiler_params=pltpu.CompilerParams(collective_id=collective, has_side_effects=True),
        cost_estimate=pl.CostEstimate(flops=0, transcendentals=0, bytes_accessed=3 * size),
    )(blocks)


def window_kernel(blk_sizes, rep_sizes, every, proj_ref, cot_ref, chosen_ref, sent_ref, out_ref, back_ref,
                  p_got, cot_got, ch_got, send_sem, recv_sem, local_sem):
    blk_count = math.prod(blk_sizes)
    span = chosen_ref.shape[0]
    blk_axes, rep_axes = every[: len(blk_sizes)], every[len(blk_sizes) :]
    b = 0
    for a, s in zip(blk_axes, blk_sizes):
        b = b * s + lax.axis_index(a)
    r = 0
    for a, s in zip(rep_axes, rep_sizes):
        r = r * s + lax.axis_index(a)
    far = span * r

    def target(offset):
        rest = (b + offset + blk_count) % blk_count
        coords = []
        for s in reversed(blk_sizes):
            coords.append(rest % s)
            rest = rest // s
        return tuple(reversed(coords)) + tuple(lax.axis_index(a) for a in rep_axes)

    def remote(src, dst, kind, t, offset):
        return pltpu.make_async_remote_copy(src, dst, send_sem.at[kind, t], recv_sem.at[kind, t],
                                            device_id=target(offset), device_id_type=MESH_IDS)

    def relay_moves():
        return (
            remote(proj_ref, p_got.at[0], 0, 0, far),
            remote(cot_ref, cot_got.at[0], 1, 0, -far),
            remote(sent_ref.at[0], ch_got.at[0], 2, 0, -far),
        )

    def local_moves():
        return (
            pltpu.make_async_copy(proj_ref, p_got.at[0], local_sem.at[0]),
            pltpu.make_async_copy(cot_ref, cot_got.at[0], local_sem.at[1]),
            pltpu.make_async_copy(sent_ref.at[0], ch_got.at[0], local_sem.at[2]),
        )

    def chosen_move(t):
        return remote(sent_ref.at[t], ch_got.at[t], 2, t, -far - t)

    def forwards(t):
        return (
            remote(p_got.at[0], p_got.at[t], 0, t, t),
            remote(cot_got.at[0], cot_got.at[t], 1, t, -t),
        )

    barrier = pltpu.get_barrier_semaphore()

    def greet(offset):
        pl.semaphore_signal(barrier, inc=1, device_id=target(offset), device_id_type=MESH_IDS)
        pl.semaphore_signal(barrier, inc=1, device_id=target(-offset), device_id_type=MESH_IDS)

    for t in range(1, span):
        greet(far + t)
        greet(t)

    @pl.when(r != 0)
    def _():
        greet(far)
        greet(far)
        pl.semaphore_wait(barrier, 4 * span)
        for c in relay_moves():
            c.start()

    @pl.when(r == 0)
    def _():
        pl.semaphore_wait(barrier, 4 * span - 4)
        for c in local_moves():
            c.start()

    for t in range(1, span):
        chosen_move(t).start()

    @pl.when(r != 0)
    def _():
        for c in relay_moves():
            c.wait_recv()

    @pl.when(r == 0)
    def _():
        for c in local_moves():
            c.wait()

    for t in range(1, span):
        for c in forwards(t):
            c.start()

    for t in range(span):
        if t > 0:
            for c in forwards(t):
                c.wait_recv()
            chosen_move(t).wait_recv()
        part = jnp.dot(chosen_ref[t], p_got[t], preferred_element_type=jnp.float32)
        back = jnp.dot(ch_got[t], cot_got[t], preferred_element_type=jnp.float32)
        if t == 0:
            out_ref[...] = part
            back_ref[...] = back
        else:
            out_ref[...] += part
            back_ref[...] += back

    @pl.when(r != 0)
    def _():
        for c in relay_moves():
            c.wait_send()

    for t in range(1, span):
        chosen_move(t).wait_send()
        for c in forwards(t):
            c.wait_send()


def window(projected, cotangent, chosen, chosen_t, blk_sizes, rep_sizes, every, collective):
    span = chosen.shape[0]
    rows, width = projected.shape
    vmem = pl.BlockSpec(memory_space=pltpu.VMEM)
    moved = (2 * rows * width * 2 + rows * rows * 2) * span
    return pl.pallas_call(
        functools.partial(window_kernel, blk_sizes, rep_sizes, every),
        out_shape=(
            jax.ShapeDtypeStruct((rows, width), jnp.float32),
            jax.ShapeDtypeStruct((rows, width), jnp.float32),
        ),
        in_specs=[vmem, vmem, vmem, vmem],
        out_specs=(vmem, vmem),
        scratch_shapes=[
            pltpu.VMEM((span, rows, width), projected.dtype),
            pltpu.VMEM((span, rows, width), cotangent.dtype),
            pltpu.VMEM((span, rows, rows), chosen.dtype),
            pltpu.SemaphoreType.DMA((3, span)),
            pltpu.SemaphoreType.DMA((3, span)),
            pltpu.SemaphoreType.DMA((3,)),
        ],
        compiler_params=pltpu.CompilerParams(collective_id=collective, has_side_effects=True),
        cost_estimate=pl.CostEstimate(
            flops=4 * span * rows * rows * width, transcendentals=0, bytes_accessed=2 * moved
        ),
    )(projected, cotangent, chosen, chosen_t)


def shards(hidden_pre, adj_vals, adj_cols, w_out, cotangent):
    row_count, feature_width = hidden_pre.shape
    blk_count = lax.axis_size(BLK)
    rep_count = lax.axis_size(REP)
    span = blk_count // rep_count
    blk_pos = lax.axis_index(BLK)
    rep_pos = lax.axis_index(REP)
    cols_here = feature_width // rep_count
    slots = adj_vals.shape[1]

    hidden_act = jnp.maximum(hidden_pre, 0)
    projected = jnp.dot(hidden_act, w_out, preferred_element_type=jnp.float32).astype(jnp.bfloat16)
    own_vals = adj_vals[0]
    own_cols = adj_cols[0]
    section = jnp.mod(blk_pos - own_cols, blk_count) - rep_pos * span

    chosen = jnp.stack(
        [
            sum(jnp.where(section[k] == turn, own_vals[k], 0) for k in range(slots))
            for turn in range(span)
        ]
    )
    blk_sizes = tuple(lax.axis_size(a) for a in BLK)
    rep_sizes = tuple(lax.axis_size(a) for a in REP)
    out_sum, back_sum = window(
        projected, cotangent, chosen, jnp.transpose(chosen, (0, 2, 1)), blk_sizes, rep_sizes, EVERY, 3
    )

    rows = out_sum.shape[0]
    both = jnp.stack([out_sum, back_sum]).reshape(2, rows, rep_count, cols_here)
    summed = exchange(jnp.transpose(both, (2, 0, 1, 3)), REP, EVERY, 0).sum(0)
    out_part = summed[0].astype(jnp.bfloat16)
    back_grad = summed[1].astype(jnp.bfloat16)
    term = lax.dot_general(
        hidden_act, back_grad, (((0,), (0,)), ((), ())), preferred_element_type=jnp.float32
    )
    grad_weight = exchange(term.reshape(blk_count, -1, cols_here), BLK, EVERY, 1).sum(0)
    gathered = exchange(back_grad, REP, EVERY, 2, broadcast=True)
    back_full = jnp.transpose(gathered, (1, 0, 2)).reshape(rows, feature_width)
    w_rows = lax.dynamic_slice_in_dim(w_out, rep_pos * cols_here, cols_here, 0)
    grad_in = lax.dot_general(
        back_full, w_rows, (((1,), (1,)), ((), ())), preferred_element_type=jnp.float32
    )
    pre_part = lax.dynamic_slice_in_dim(hidden_pre, rep_pos * cols_here, cols_here, 1)
    grad_pre = jnp.where(pre_part > 0, grad_in, 0.0).astype(jnp.bfloat16)
    return (out_part, grad_weight, grad_pre)


def solution(mesh):
    blk_count, rep_count = mesh.devices.shape
    fine = Mesh(mesh.devices.reshape(8, blk_count // 16, 2, rep_count // 2, 2), EVERY)
    placed = (P(BLK, None), P(BLK, REP, None, None), P(BLK, REP), P(), P(BLK, None))
    return jax.shard_map(
        shards,
        mesh=fine,
        in_specs=placed,
        out_specs=(P(BLK, REP), P(BLK, REP), P(BLK, REP)),
        check_vma=False,
    )
```

```python
import functools
import math

import jax
import jax.numpy as jnp
from jax import lax
from jax.experimental import pallas as pl
from jax.experimental.pallas import tpu as pltpu
from jax.sharding import Mesh
from jax.sharding import PartitionSpec as P

MESH_IDS = pl.DeviceIdType.MESH

BLK = ("by", "bx", "bz")
REP = ("rz", "rc")
EVERY = BLK + REP


def shifted_pairs(blk_count, rep_count, per_rep):
    pairs = []
    for b in range(blk_count):
        for r in range(rep_count):
            pairs.append((b * rep_count + r, ((b + per_rep * r) % blk_count) * rep_count + r))
    return pairs


def ring_pairs(count, steps):
    return [(source, (source + steps) % count) for source in range(count)]


def staged_scatter(value, axes, dim):
    sizes = [lax.axis_size(a) for a in axes]
    full = value.shape[dim]
    rest = full // math.prod(sizes)
    shape = value.shape[:dim] + tuple(sizes) + (rest,) + value.shape[dim + 1 :]
    moved = value.reshape(shape)
    order = list(range(dim)) + [dim + i for i in reversed(range(len(axes)))]
    order += list(range(dim + len(axes), len(shape)))
    moved = jnp.transpose(moved, order).reshape(value.shape)
    for a in reversed(axes):
        moved = lax.psum_scatter(moved, a, scatter_dimension=dim, tiled=True)
    return moved


def exchange_kernel(plans, every, *refs):
    count_of = [math.prod(sizes) for _, sizes, _ in plans]
    n = len(plans)
    srcs, outs = refs[:n], refs[n : 2 * n]
    landed, send_sems, recv_sems = refs[2 * n : 3 * n], refs[3 * n : 4 * n], refs[4 * n : 5 * n]
    barrier = pltpu.get_barrier_semaphore()

    def position(group, sizes):
        me = 0
        for a, s in zip(group, sizes):
            me = me * s + lax.axis_index(a)
        return me

    def target(group, sizes, d):
        coords = {}
        rest = d
        for a, s in reversed(list(zip(group, sizes))):
            coords[a] = rest % s
            rest = rest // s
        return tuple(coords[a] if a in coords else lax.axis_index(a) for a in every)

    def copy(i, d, slot, o):
        group, sizes, broadcast = plans[i]
        return pltpu.make_async_remote_copy(
            src_ref=srcs[i] if broadcast else srcs[i].at[d],
            dst_ref=landed[i].at[slot],
            send_sem=send_sems[i].at[o],
            recv_sem=recv_sems[i].at[slot],
            device_id=target(group, sizes, d),
            device_id_type=MESH_IDS,
        )

    for i, (group, sizes, _) in enumerate(plans):
        me, count = position(group, sizes), count_of[i]

        def greet(o, carry, group=group, sizes=sizes, me=me, count=count):
            pl.semaphore_signal(barrier, inc=1, device_id=target(group, sizes, (me + o) % count),
                                device_id_type=MESH_IDS)
            return carry

        lax.fori_loop(1, count, greet, 0)
    pl.semaphore_wait(barrier, sum(count_of) - n)

    for i, (group, sizes, broadcast) in enumerate(plans):
        me, count = position(group, sizes), count_of[i]

        def send(o, carry, i=i, me=me, count=count):
            copy(i, (me + o) % count, me, o).start()
            return carry

        lax.fori_loop(1, count, send, 0)
        outs[i][me] = srcs[i][...] if broadcast else srcs[i][me]

    for i, (group, sizes, broadcast) in enumerate(plans):
        me, count = position(group, sizes), count_of[i]

        def finish(o, carry, i=i, me=me, count=count):
            copy(i, (me + o) % count, me, o).wait_send()
            sender = (me + count - o) % count
            copy(i, sender, sender, o).wait_recv()
            outs[i][sender] = landed[i][sender]
            return carry

        lax.fori_loop(1, count, finish, 0)


def exchange_many(items, every, collective):
    plans, shapes, total = [], [], 0
    for blocks, group, broadcast in items:
        sizes = tuple(lax.axis_size(a) for a in group)
        count = math.prod(sizes)
        shape = (count,) + (blocks.shape if broadcast else blocks.shape[1:])
        plans.append((group, sizes, broadcast))
        shapes.append(jax.ShapeDtypeStruct(shape, blocks.dtype))
        total += math.prod(shape) * blocks.dtype.itemsize
    vmem = pl.BlockSpec(memory_space=pltpu.VMEM)
    return pl.pallas_call(
        functools.partial(exchange_kernel, tuple(plans), every),
        out_shape=tuple(shapes),
        in_specs=[vmem] * len(items),
        out_specs=tuple([vmem] * len(items)),
        scratch_shapes=[pltpu.VMEM(x.shape, x.dtype) for x in shapes]
        + [pltpu.SemaphoreType.DMA((x.shape[0],)) for x in shapes]
        + [pltpu.SemaphoreType.DMA((x.shape[0],)) for x in shapes],
        compiler_params=pltpu.CompilerParams(collective_id=collective, has_side_effects=True),
        cost_estimate=pl.CostEstimate(flops=0, transcendentals=0, bytes_accessed=3 * total),
    )(*[blocks for blocks, _, _ in items])


def exchange(blocks, group, every, collective, broadcast=False):
    return exchange_many([(blocks, group, broadcast)], every, collective)[0]


def window_kernel(blk_sizes, rep_sizes, every, proj_ref, cot_ref, chosen_ref, sent_ref, out_ref, back_ref,
                  p_got, cot_got, ch_got, send_sem, recv_sem, local_sem):
    blk_count = math.prod(blk_sizes)
    span = chosen_ref.shape[0]
    blk_axes, rep_axes = every[: len(blk_sizes)], every[len(blk_sizes) :]
    b = 0
    for a, s in zip(blk_axes, blk_sizes):
        b = b * s + lax.axis_index(a)
    r = 0
    for a, s in zip(rep_axes, rep_sizes):
        r = r * s + lax.axis_index(a)
    far = span * r

    def target(offset):
        rest = (b + offset + blk_count) % blk_count
        coords = []
        for s in reversed(blk_sizes):
            coords.append(rest % s)
            rest = rest // s
        return tuple(reversed(coords)) + tuple(lax.axis_index(a) for a in rep_axes)

    def remote(src, dst, kind, t, offset):
        return pltpu.make_async_remote_copy(src, dst, send_sem.at[kind, t], recv_sem.at[kind, t],
                                            device_id=target(offset), device_id_type=MESH_IDS)

    def relay_moves():
        return (
            remote(proj_ref, p_got.at[0], 0, 0, far),
            remote(cot_ref, cot_got.at[0], 1, 0, -far),
            remote(sent_ref.at[0], ch_got.at[0], 2, 0, -far),
        )

    def local_moves():
        return (
            pltpu.make_async_copy(proj_ref, p_got.at[0], local_sem.at[0]),
            pltpu.make_async_copy(cot_ref, cot_got.at[0], local_sem.at[1]),
            pltpu.make_async_copy(sent_ref.at[0], ch_got.at[0], local_sem.at[2]),
        )

    def chosen_move(t):
        return remote(sent_ref.at[t], ch_got.at[t], 2, t, -far - t)

    def forwards(t):
        return (
            remote(p_got.at[0], p_got.at[t], 0, t, t),
            remote(cot_got.at[0], cot_got.at[t], 1, t, -t),
        )

    barrier = pltpu.get_barrier_semaphore()

    def greet(offset):
        pl.semaphore_signal(barrier, inc=1, device_id=target(offset), device_id_type=MESH_IDS)
        pl.semaphore_signal(barrier, inc=1, device_id=target(-offset), device_id_type=MESH_IDS)

    for t in range(1, span):
        greet(far + t)
        greet(t)

    @pl.when(r != 0)
    def _():
        greet(far)
        greet(far)
        pl.semaphore_wait(barrier, 4 * span)
        for c in relay_moves():
            c.start()

    @pl.when(r == 0)
    def _():
        pl.semaphore_wait(barrier, 4 * span - 4)
        for c in local_moves():
            c.start()

    for t in range(1, span):
        chosen_move(t).start()

    @pl.when(r != 0)
    def _():
        for c in relay_moves():
            c.wait_recv()

    @pl.when(r == 0)
    def _():
        for c in local_moves():
            c.wait()

    for t in range(1, span):
        for c in forwards(t):
            c.start()

    for t in range(span):
        if t > 0:
            for c in forwards(t):
                c.wait_recv()
            chosen_move(t).wait_recv()
        part = jnp.dot(chosen_ref[t], p_got[t], preferred_element_type=jnp.float32)
        back = jnp.dot(ch_got[t], cot_got[t], preferred_element_type=jnp.float32)
        if t == 0:
            out_ref[...] = part
            back_ref[...] = back
        else:
            out_ref[...] += part
            back_ref[...] += back

    @pl.when(r != 0)
    def _():
        for c in relay_moves():
            c.wait_send()

    for t in range(1, span):
        chosen_move(t).wait_send()
        for c in forwards(t):
            c.wait_send()


def window(projected, cotangent, chosen, chosen_t, blk_sizes, rep_sizes, every, collective):
    span = chosen.shape[0]
    rows, width = projected.shape
    vmem = pl.BlockSpec(memory_space=pltpu.VMEM)
    moved = (2 * rows * width * 2 + rows * rows * 2) * span
    return pl.pallas_call(
        functools.partial(window_kernel, blk_sizes, rep_sizes, every),
        out_shape=(
            jax.ShapeDtypeStruct((rows, width), jnp.float32),
            jax.ShapeDtypeStruct((rows, width), jnp.float32),
        ),
        in_specs=[vmem, vmem, vmem, vmem],
        out_specs=(vmem, vmem),
        scratch_shapes=[
            pltpu.VMEM((span, rows, width), projected.dtype),
            pltpu.VMEM((span, rows, width), cotangent.dtype),
            pltpu.VMEM((span, rows, rows), chosen.dtype),
            pltpu.SemaphoreType.DMA((3, span)),
            pltpu.SemaphoreType.DMA((3, span)),
            pltpu.SemaphoreType.DMA((3,)),
        ],
        compiler_params=pltpu.CompilerParams(collective_id=collective, has_side_effects=True),
        cost_estimate=pl.CostEstimate(
            flops=4 * span * rows * rows * width, transcendentals=0, bytes_accessed=2 * moved
        ),
    )(projected, cotangent, chosen, chosen_t)


def shards(hidden_pre, adj_vals, adj_cols, w_out, cotangent):
    row_count, feature_width = hidden_pre.shape
    blk_count = lax.axis_size(BLK)
    rep_count = lax.axis_size(REP)
    span = blk_count // rep_count
    blk_pos = lax.axis_index(BLK)
    rep_pos = lax.axis_index(REP)
    cols_here = feature_width // rep_count
    slots = adj_vals.shape[1]

    hidden_act = jnp.maximum(hidden_pre, 0)
    projected = jnp.dot(hidden_act, w_out, preferred_element_type=jnp.float32).astype(jnp.bfloat16)
    own_vals = adj_vals[0]
    own_cols = adj_cols[0]
    section = jnp.mod(blk_pos - own_cols, blk_count) - rep_pos * span

    chosen = jnp.stack(
        [
            sum(jnp.where(section[k] == turn, own_vals[k], 0) for k in range(slots))
            for turn in range(span)
        ]
    )
    blk_sizes = tuple(lax.axis_size(a) for a in BLK)
    rep_sizes = tuple(lax.axis_size(a) for a in REP)
    out_sum, back_sum = window(
        projected, cotangent, chosen, jnp.transpose(chosen, (0, 2, 1)), blk_sizes, rep_sizes, EVERY, 3
    )

    rows = out_sum.shape[0]
    both = jnp.stack([out_sum, back_sum]).reshape(2, rows, rep_count, cols_here)
    summed = exchange(jnp.transpose(both, (2, 0, 1, 3)), REP, EVERY, 0).sum(0)
    out_part = summed[0].astype(jnp.bfloat16)
    back_grad = summed[1].astype(jnp.bfloat16)
    term = lax.dot_general(
        hidden_act, back_grad, (((0,), (0,)), ((), ())), preferred_element_type=jnp.float32
    )
    weight_parts, gathered = exchange_many(
        [(term.reshape(blk_count, -1, cols_here), BLK, False), (back_grad, REP, True)], EVERY, 1
    )
    grad_weight = weight_parts.sum(0)
    back_full = jnp.transpose(gathered, (1, 0, 2)).reshape(rows, feature_width)
    w_rows = lax.dynamic_slice_in_dim(w_out, rep_pos * cols_here, cols_here, 0)
    grad_in = lax.dot_general(
        back_full, w_rows, (((1,), (1,)), ((), ())), preferred_element_type=jnp.float32
    )
    pre_part = lax.dynamic_slice_in_dim(hidden_pre, rep_pos * cols_here, cols_here, 1)
    grad_pre = jnp.where(pre_part > 0, grad_in, 0.0).astype(jnp.bfloat16)
    return (out_part, grad_weight, grad_pre)


def solution(mesh):
    blk_count, rep_count = mesh.devices.shape
    fine = Mesh(mesh.devices.reshape(8, blk_count // 16, 2, rep_count // 2, 2), EVERY)
    placed = (P(BLK, None), P(BLK, REP, None, None), P(BLK, REP), P(), P(BLK, None))
    return jax.shard_map(
        shards,
        mesh=fine,
        in_specs=placed,
        out_specs=(P(BLK, REP), P(BLK, REP), P(BLK, REP)),
        check_vma=False,
    )
```

```python
import functools
import math

import jax
import jax.numpy as jnp
from jax import lax
from jax.experimental import pallas as pl
from jax.experimental.pallas import tpu as pltpu
from jax.sharding import Mesh
from jax.sharding import PartitionSpec as P

MESH_IDS = pl.DeviceIdType.MESH

BLK = ("by", "bx", "bz")
REP = ("rz", "rc")
EVERY = BLK + REP


def shifted_pairs(blk_count, rep_count, per_rep):
    pairs = []
    for b in range(blk_count):
        for r in range(rep_count):
            pairs.append((b * rep_count + r, ((b + per_rep * r) % blk_count) * rep_count + r))
    return pairs


def ring_pairs(count, steps):
    return [(source, (source + steps) % count) for source in range(count)]


def staged_scatter(value, axes, dim):
    sizes = [lax.axis_size(a) for a in axes]
    full = value.shape[dim]
    rest = full // math.prod(sizes)
    shape = value.shape[:dim] + tuple(sizes) + (rest,) + value.shape[dim + 1 :]
    moved = value.reshape(shape)
    order = list(range(dim)) + [dim + i for i in reversed(range(len(axes)))]
    order += list(range(dim + len(axes), len(shape)))
    moved = jnp.transpose(moved, order).reshape(value.shape)
    for a in reversed(axes):
        moved = lax.psum_scatter(moved, a, scatter_dimension=dim, tiled=True)
    return moved


def exchange_kernel(plans, every, *refs):
    count_of = [math.prod(sizes) for _, sizes, _ in plans]
    n = len(plans)
    srcs, outs = refs[:n], refs[n : 2 * n]
    landed, send_sems, recv_sems = refs[2 * n : 3 * n], refs[3 * n : 4 * n], refs[4 * n : 5 * n]
    totals = refs[5 * n : 6 * n]
    barrier = pltpu.get_barrier_semaphore()

    def position(group, sizes):
        me = 0
        for a, s in zip(group, sizes):
            me = me * s + lax.axis_index(a)
        return me

    def target(group, sizes, d):
        coords = {}
        rest = d
        for a, s in reversed(list(zip(group, sizes))):
            coords[a] = rest % s
            rest = rest // s
        return tuple(coords[a] if a in coords else lax.axis_index(a) for a in every)

    def copy(i, d, slot, o):
        group, sizes, mode = plans[i]
        broadcast = mode == "concat"
        return pltpu.make_async_remote_copy(
            src_ref=srcs[i] if broadcast else srcs[i].at[d],
            dst_ref=landed[i].at[slot],
            send_sem=send_sems[i].at[o],
            recv_sem=recv_sems[i].at[slot],
            device_id=target(group, sizes, d),
            device_id_type=MESH_IDS,
        )

    for i, (group, sizes, _) in enumerate(plans):
        me, count = position(group, sizes), count_of[i]

        def greet(o, carry, group=group, sizes=sizes, me=me, count=count):
            pl.semaphore_signal(barrier, inc=1, device_id=target(group, sizes, (me + o) % count),
                                device_id_type=MESH_IDS)
            return carry

        lax.fori_loop(1, count, greet, 0)
    pl.semaphore_wait(barrier, sum(count_of) - n)

    for i, (group, sizes, mode) in enumerate(plans):
        me, count = position(group, sizes), count_of[i]

        def send(o, carry, i=i, me=me, count=count):
            copy(i, (me + o) % count, me, o).start()
            return carry

        lax.fori_loop(1, count, send, 0)
        if mode == "concat":
            width = srcs[i].shape[-1]
            outs[i][:, pl.ds(pl.multiple_of(me * width, width), width)] = srcs[i][...]
        else:
            totals[i][...] = srcs[i][me].astype(jnp.float32)

    for i, (group, sizes, mode) in enumerate(plans):
        me, count = position(group, sizes), count_of[i]

        def finish(o, carry, i=i, me=me, count=count, mode=mode):
            copy(i, (me + o) % count, me, o).wait_send()
            sender = (me + count - o) % count
            copy(i, sender, sender, o).wait_recv()
            if mode == "concat":
                width = srcs[i].shape[-1]
                outs[i][:, pl.ds(pl.multiple_of(sender * width, width), width)] = landed[i][sender]
            else:
                totals[i][...] += landed[i][sender].astype(jnp.float32)
            return carry

        lax.fori_loop(1, count, finish, 0)
        if mode != "concat":
            outs[i][...] = totals[i][...].astype(outs[i].dtype)


def exchange_many(items, every, collective):
    plans, shapes, landings, totals, counts, total = [], [], [], [], [], 0
    for blocks, group, mode, dtype in items:
        sizes = tuple(lax.axis_size(a) for a in group)
        count = math.prod(sizes)
        if mode == "concat":
            slot_shape = blocks.shape
            shapes.append(jax.ShapeDtypeStruct(blocks.shape[:-1] + (count * blocks.shape[-1],), dtype))
        else:
            slot_shape = blocks.shape[1:]
            shapes.append(jax.ShapeDtypeStruct(slot_shape, dtype))
        plans.append((group, sizes, mode))
        counts.append(count)
        landings.append(pltpu.VMEM((count,) + slot_shape, blocks.dtype))
        totals.append(pltpu.VMEM(slot_shape, jnp.float32))
        total += count * math.prod(slot_shape) * blocks.dtype.itemsize
    vmem = pl.BlockSpec(memory_space=pltpu.VMEM)
    return pl.pallas_call(
        functools.partial(exchange_kernel, tuple(plans), every),
        out_shape=tuple(shapes),
        in_specs=[vmem] * len(items),
        out_specs=tuple([vmem] * len(items)),
        scratch_shapes=landings
        + [pltpu.SemaphoreType.DMA((c,)) for c in counts]
        + [pltpu.SemaphoreType.DMA((c,)) for c in counts]
        + totals,
        compiler_params=pltpu.CompilerParams(collective_id=collective, has_side_effects=True),
        cost_estimate=pl.CostEstimate(flops=0, transcendentals=0, bytes_accessed=3 * total),
    )(*[item[0] for item in items])


def window_kernel(blk_sizes, rep_sizes, every, proj_ref, cot_ref, chosen_ref, sent_ref, out_ref, back_ref,
                  p_got, cot_got, ch_got, send_sem, recv_sem, local_sem):
    blk_count = math.prod(blk_sizes)
    span = chosen_ref.shape[0]
    blk_axes, rep_axes = every[: len(blk_sizes)], every[len(blk_sizes) :]
    b = 0
    for a, s in zip(blk_axes, blk_sizes):
        b = b * s + lax.axis_index(a)
    r = 0
    for a, s in zip(rep_axes, rep_sizes):
        r = r * s + lax.axis_index(a)
    far = span * r

    def target(offset):
        rest = (b + offset + blk_count) % blk_count
        coords = []
        for s in reversed(blk_sizes):
            coords.append(rest % s)
            rest = rest // s
        return tuple(reversed(coords)) + tuple(lax.axis_index(a) for a in rep_axes)

    def remote(src, dst, kind, t, offset):
        return pltpu.make_async_remote_copy(src, dst, send_sem.at[kind, t], recv_sem.at[kind, t],
                                            device_id=target(offset), device_id_type=MESH_IDS)

    def relay_moves():
        return (
            remote(proj_ref, p_got.at[0], 0, 0, far),
            remote(cot_ref, cot_got.at[0], 1, 0, -far),
            remote(sent_ref.at[0], ch_got.at[0], 2, 0, -far),
        )

    def local_moves():
        return (
            pltpu.make_async_copy(proj_ref, p_got.at[0], local_sem.at[0]),
            pltpu.make_async_copy(cot_ref, cot_got.at[0], local_sem.at[1]),
            pltpu.make_async_copy(sent_ref.at[0], ch_got.at[0], local_sem.at[2]),
        )

    def chosen_move(t):
        return remote(sent_ref.at[t], ch_got.at[t], 2, t, -far - t)

    def forwards(t):
        return (
            remote(p_got.at[0], p_got.at[t], 0, t, t),
            remote(cot_got.at[0], cot_got.at[t], 1, t, -t),
        )

    barrier = pltpu.get_barrier_semaphore()

    def greet(offset):
        pl.semaphore_signal(barrier, inc=1, device_id=target(offset), device_id_type=MESH_IDS)
        pl.semaphore_signal(barrier, inc=1, device_id=target(-offset), device_id_type=MESH_IDS)

    for t in range(1, span):
        greet(far + t)
        greet(t)

    @pl.when(r != 0)
    def _():
        greet(far)
        greet(far)
        pl.semaphore_wait(barrier, 4 * span)
        for c in relay_moves():
            c.start()

    @pl.when(r == 0)
    def _():
        pl.semaphore_wait(barrier, 4 * span - 4)
        for c in local_moves():
            c.start()

    for t in range(1, span):
        chosen_move(t).start()

    @pl.when(r != 0)
    def _():
        for c in relay_moves():
            c.wait_recv()

    @pl.when(r == 0)
    def _():
        for c in local_moves():
            c.wait()

    for t in range(1, span):
        for c in forwards(t):
            c.start()

    for t in range(span):
        if t > 0:
            for c in forwards(t):
                c.wait_recv()
            chosen_move(t).wait_recv()
        part = jnp.dot(chosen_ref[t], p_got[t], preferred_element_type=jnp.float32)
        back = jnp.dot(ch_got[t], cot_got[t], preferred_element_type=jnp.float32)
        width = out_ref.shape[-1]
        for q in range(out_ref.shape[0]):
            columns = slice(q * width, (q + 1) * width)
            if t == 0:
                out_ref[q] = part[:, columns]
                back_ref[q] = back[:, columns]
            else:
                out_ref[q] += part[:, columns]
                back_ref[q] += back[:, columns]

    @pl.when(r != 0)
    def _():
        for c in relay_moves():
            c.wait_send()

    for t in range(1, span):
        chosen_move(t).wait_send()
        for c in forwards(t):
            c.wait_send()


def window(projected, cotangent, chosen, chosen_t, blk_sizes, rep_sizes, every, collective):
    pieces = math.prod(rep_sizes)
    span = chosen.shape[0]
    rows, width = projected.shape
    vmem = pl.BlockSpec(memory_space=pltpu.VMEM)
    moved = (2 * rows * width * 2 + rows * rows * 2) * span
    return pl.pallas_call(
        functools.partial(window_kernel, blk_sizes, rep_sizes, every),
        out_shape=(
            jax.ShapeDtypeStruct((pieces, rows, width // pieces), jnp.float32),
            jax.ShapeDtypeStruct((pieces, rows, width // pieces), jnp.float32),
        ),
        in_specs=[vmem, vmem, vmem, vmem],
        out_specs=(vmem, vmem),
        scratch_shapes=[
            pltpu.VMEM((span, rows, width), projected.dtype),
            pltpu.VMEM((span, rows, width), cotangent.dtype),
            pltpu.VMEM((span, rows, rows), chosen.dtype),
            pltpu.SemaphoreType.DMA((3, span)),
            pltpu.SemaphoreType.DMA((3, span)),
            pltpu.SemaphoreType.DMA((3,)),
        ],
        compiler_params=pltpu.CompilerParams(collective_id=collective, has_side_effects=True),
        cost_estimate=pl.CostEstimate(
            flops=4 * span * rows * rows * width, transcendentals=0, bytes_accessed=2 * moved
        ),
    )(projected, cotangent, chosen, chosen_t)


def shards(hidden_pre, adj_vals, adj_cols, w_out, cotangent):
    row_count, feature_width = hidden_pre.shape
    blk_count = lax.axis_size(BLK)
    rep_count = lax.axis_size(REP)
    span = blk_count // rep_count
    blk_pos = lax.axis_index(BLK)
    rep_pos = lax.axis_index(REP)
    cols_here = feature_width // rep_count
    slots = adj_vals.shape[1]

    hidden_act = jnp.maximum(hidden_pre, 0)
    projected = jnp.dot(hidden_act, w_out, preferred_element_type=jnp.float32).astype(jnp.bfloat16)
    own_vals = adj_vals[0]
    own_cols = adj_cols[0]
    section = jnp.mod(blk_pos - own_cols, blk_count) - rep_pos * span

    chosen = jnp.stack(
        [
            sum(jnp.where(section[k] == turn, own_vals[k], 0) for k in range(slots))
            for turn in range(span)
        ]
    )
    blk_sizes = tuple(lax.axis_size(a) for a in BLK)
    rep_sizes = tuple(lax.axis_size(a) for a in REP)
    out_sum, back_sum = window(
        projected, cotangent, chosen, jnp.transpose(chosen, (0, 2, 1)), blk_sizes, rep_sizes, EVERY, 3
    )

    rows = projected.shape[0]
    out_part, back_grad = exchange_many(
        [(out_sum, REP, "sum", jnp.bfloat16), (back_sum, REP, "sum", jnp.bfloat16)], EVERY, 0
    )
    term = lax.dot_general(
        hidden_act, back_grad, (((0,), (0,)), ((), ())), preferred_element_type=jnp.float32
    )
    grad_weight, back_full = exchange_many(
        [
            (term.reshape(blk_count, -1, cols_here), BLK, "sum", jnp.float32),
            (back_grad, REP, "concat", jnp.bfloat16),
        ],
        EVERY,
        1,
    )
    w_rows = lax.dynamic_slice_in_dim(w_out, rep_pos * cols_here, cols_here, 0)
    grad_in = lax.dot_general(
        back_full, w_rows, (((1,), (1,)), ((), ())), preferred_element_type=jnp.float32
    )
    pre_part = lax.dynamic_slice_in_dim(hidden_pre, rep_pos * cols_here, cols_here, 1)
    grad_pre = jnp.where(pre_part > 0, grad_in, 0.0).astype(jnp.bfloat16)
    return (out_part, grad_weight, grad_pre)


def solution(mesh):
    blk_count, rep_count = mesh.devices.shape
    fine = Mesh(mesh.devices.reshape(8, blk_count // 16, 2, rep_count // 2, 2), EVERY)
    placed = (P(BLK, None), P(BLK, REP, None, None), P(BLK, REP), P(), P(BLK, None))
    return jax.shard_map(
        shards,
        mesh=fine,
        in_specs=placed,
        out_specs=(P(BLK, REP), P(BLK, REP), P(BLK, REP)),
        check_vma=False,
    )
```

```python
import functools
import math

import jax
import jax.numpy as jnp
from jax import lax
from jax.experimental import pallas as pl
from jax.experimental.pallas import tpu as pltpu
from jax.sharding import Mesh
from jax.sharding import PartitionSpec as P

MESH_IDS = pl.DeviceIdType.MESH

BLK = ("by", "bx", "bz")
REP = ("rz", "rc")
EVERY = BLK + REP


def shifted_pairs(blk_count, rep_count, per_rep):
    pairs = []
    for b in range(blk_count):
        for r in range(rep_count):
            pairs.append((b * rep_count + r, ((b + per_rep * r) % blk_count) * rep_count + r))
    return pairs


def ring_pairs(count, steps):
    return [(source, (source + steps) % count) for source in range(count)]


def staged_scatter(value, axes, dim):
    sizes = [lax.axis_size(a) for a in axes]
    full = value.shape[dim]
    rest = full // math.prod(sizes)
    shape = value.shape[:dim] + tuple(sizes) + (rest,) + value.shape[dim + 1 :]
    moved = value.reshape(shape)
    order = list(range(dim)) + [dim + i for i in reversed(range(len(axes)))]
    order += list(range(dim + len(axes), len(shape)))
    moved = jnp.transpose(moved, order).reshape(value.shape)
    for a in reversed(axes):
        moved = lax.psum_scatter(moved, a, scatter_dimension=dim, tiled=True)
    return moved


def exchange_kernel(plans, every, *refs):
    count_of = [math.prod(sizes) for _, sizes, _ in plans]
    n = len(plans)
    srcs, outs = refs[:n], refs[n : 2 * n]
    landed, send_sems, recv_sems = refs[2 * n : 3 * n], refs[3 * n : 4 * n], refs[4 * n : 5 * n]
    totals = refs[5 * n : 6 * n]
    barrier = pltpu.get_barrier_semaphore()

    def position(group, sizes):
        me = 0
        for a, s in zip(group, sizes):
            me = me * s + lax.axis_index(a)
        return me

    def target(group, sizes, d):
        coords = {}
        rest = d
        for a, s in reversed(list(zip(group, sizes))):
            coords[a] = rest % s
            rest = rest // s
        return tuple(coords[a] if a in coords else lax.axis_index(a) for a in every)

    def copy(i, d, slot, o):
        group, sizes, mode = plans[i]
        broadcast = mode == "concat"
        return pltpu.make_async_remote_copy(
            src_ref=srcs[i] if broadcast else srcs[i].at[d],
            dst_ref=landed[i].at[slot],
            send_sem=send_sems[i].at[o],
            recv_sem=recv_sems[i].at[slot],
            device_id=target(group, sizes, d),
            device_id_type=MESH_IDS,
        )

    for i, (group, sizes, _) in enumerate(plans):
        me, count = position(group, sizes), count_of[i]

        def greet(o, carry, group=group, sizes=sizes, me=me, count=count):
            pl.semaphore_signal(barrier, inc=1, device_id=target(group, sizes, (me + o) % count),
                                device_id_type=MESH_IDS)
            return carry

        lax.fori_loop(1, count, greet, 0)
    pl.semaphore_wait(barrier, sum(count_of) - n)

    for i, (group, sizes, mode) in enumerate(plans):
        me, count = position(group, sizes), count_of[i]

        def send(o, carry, i=i, me=me, count=count):
            copy(i, (me + o) % count, me, o).start()
            return carry

        lax.fori_loop(1, count, send, 0)
        if mode == "concat":
            width = srcs[i].shape[-1]
            outs[i][:, pl.ds(pl.multiple_of(me * width, width), width)] = srcs[i][...]
        else:
            totals[i][...] = srcs[i][me].astype(jnp.float32)

    for i, (group, sizes, mode) in enumerate(plans):
        me, count = position(group, sizes), count_of[i]

        def finish(o, carry, i=i, me=me, count=count, mode=mode):
            copy(i, (me + o) % count, me, o).wait_send()
            sender = (me + count - o) % count
            copy(i, sender, sender, o).wait_recv()
            if mode == "concat":
                width = srcs[i].shape[-1]
                outs[i][:, pl.ds(pl.multiple_of(sender * width, width), width)] = landed[i][sender]
            else:
                totals[i][...] += landed[i][sender].astype(jnp.float32)
            return carry

        lax.fori_loop(1, count, finish, 0)
        if mode != "concat":
            outs[i][...] = totals[i][...].astype(outs[i].dtype)


def exchange_many(items, every, collective):
    plans, shapes, landings, totals, counts, total = [], [], [], [], [], 0
    for blocks, group, mode, dtype in items:
        sizes = tuple(lax.axis_size(a) for a in group)
        count = math.prod(sizes)
        if mode == "concat":
            slot_shape = blocks.shape
            shapes.append(jax.ShapeDtypeStruct(blocks.shape[:-1] + (count * blocks.shape[-1],), dtype))
        else:
            slot_shape = blocks.shape[1:]
            shapes.append(jax.ShapeDtypeStruct(slot_shape, dtype))
        plans.append((group, sizes, mode))
        counts.append(count)
        landings.append(pltpu.VMEM((count,) + slot_shape, blocks.dtype))
        totals.append(pltpu.VMEM(slot_shape, jnp.float32))
        total += count * math.prod(slot_shape) * blocks.dtype.itemsize
    vmem = pl.BlockSpec(memory_space=pltpu.VMEM)
    return pl.pallas_call(
        functools.partial(exchange_kernel, tuple(plans), every),
        out_shape=tuple(shapes),
        in_specs=[vmem] * len(items),
        out_specs=tuple([vmem] * len(items)),
        scratch_shapes=landings
        + [pltpu.SemaphoreType.DMA((c,)) for c in counts]
        + [pltpu.SemaphoreType.DMA((c,)) for c in counts]
        + totals,
        compiler_params=pltpu.CompilerParams(collective_id=collective, has_side_effects=True),
        cost_estimate=pl.CostEstimate(flops=0, transcendentals=0, bytes_accessed=3 * total),
    )(*[item[0] for item in items])


def window_kernel(blk_sizes, rep_sizes, every, proj_ref, cot_ref, chosen_ref, sent_ref, out_ref, back_ref,
                  p_got, cot_got, ch_got, send_sem, recv_sem, local_sem):
    blk_count = math.prod(blk_sizes)
    span = chosen_ref.shape[0]
    blk_axes, rep_axes = every[: len(blk_sizes)], every[len(blk_sizes) :]
    b = 0
    for a, s in zip(blk_axes, blk_sizes):
        b = b * s + lax.axis_index(a)
    r = 0
    for a, s in zip(rep_axes, rep_sizes):
        r = r * s + lax.axis_index(a)
    far = span * r

    def target(offset):
        rest = (b + offset + blk_count) % blk_count
        coords = []
        for s in reversed(blk_sizes):
            coords.append(rest % s)
            rest = rest // s
        return tuple(reversed(coords)) + tuple(lax.axis_index(a) for a in rep_axes)

    def remote(src, dst, kind, h, t, offset):
        return pltpu.make_async_remote_copy(src, dst, send_sem.at[kind, h, t], recv_sem.at[kind, h, t],
                                            device_id=target(offset), device_id_type=MESH_IDS)

    half = proj_ref.shape[0] // 2

    def rows(h):
        return pl.ds(h * half, half)

    def relay_moves(h):
        moves = (
            remote(proj_ref.at[rows(h)], p_got.at[0, rows(h)], 0, h, 0, far),
            remote(cot_ref.at[rows(h)], cot_got.at[0, rows(h)], 1, h, 0, -far),
        )
        if h == 0:
            moves += (remote(sent_ref.at[0], ch_got.at[0], 2, 0, 0, -far),)
        return moves

    def local_moves(h):
        moves = (
            pltpu.make_async_copy(proj_ref.at[rows(h)], p_got.at[0, rows(h)], local_sem.at[0, h]),
            pltpu.make_async_copy(cot_ref.at[rows(h)], cot_got.at[0, rows(h)], local_sem.at[1, h]),
        )
        if h == 0:
            moves += (pltpu.make_async_copy(sent_ref.at[0], ch_got.at[0], local_sem.at[2, 0]),)
        return moves

    def chosen_move(t):
        return remote(sent_ref.at[t], ch_got.at[t], 2, 0, t, -far - t)

    def forwards(t, h):
        return (
            remote(p_got.at[0, rows(h)], p_got.at[t, rows(h)], 0, h, t, t),
            remote(cot_got.at[0, rows(h)], cot_got.at[t, rows(h)], 1, h, t, -t),
        )

    barrier = pltpu.get_barrier_semaphore()

    def greet(offset):
        pl.semaphore_signal(barrier, inc=1, device_id=target(offset), device_id_type=MESH_IDS)
        pl.semaphore_signal(barrier, inc=1, device_id=target(-offset), device_id_type=MESH_IDS)

    for t in range(1, span):
        greet(far + t)
        greet(t)

    @pl.when(r != 0)
    def _():
        greet(far)
        greet(far)
        pl.semaphore_wait(barrier, 4 * span)
        for h in range(2):
            for c in relay_moves(h):
                c.start()

    @pl.when(r == 0)
    def _():
        pl.semaphore_wait(barrier, 4 * span - 4)
        for h in range(2):
            for c in local_moves(h):
                c.start()

    for t in range(1, span):
        chosen_move(t).start()

    for h in range(2):

        @pl.when(r != 0)
        def _():
            for c in relay_moves(h):
                c.wait_recv()

        @pl.when(r == 0)
        def _():
            for c in local_moves(h):
                c.wait()

        for t in range(1, span):
            for c in forwards(t, h):
                c.start()

    for t in range(span):
        if t > 0:
            for h in range(2):
                for c in forwards(t, h):
                    c.wait_recv()
            chosen_move(t).wait_recv()
        part = jnp.dot(chosen_ref[t], p_got[t], preferred_element_type=jnp.float32)
        back = jnp.dot(ch_got[t], cot_got[t], preferred_element_type=jnp.float32)
        width = out_ref.shape[-1]
        for q in range(out_ref.shape[0]):
            columns = slice(q * width, (q + 1) * width)
            if t == 0:
                out_ref[q] = part[:, columns]
                back_ref[q] = back[:, columns]
            else:
                out_ref[q] += part[:, columns]
                back_ref[q] += back[:, columns]

    @pl.when(r != 0)
    def _():
        for h in range(2):
            for c in relay_moves(h):
                c.wait_send()

    for t in range(1, span):
        chosen_move(t).wait_send()
        for h in range(2):
            for c in forwards(t, h):
                c.wait_send()


def window(projected, cotangent, chosen, chosen_t, blk_sizes, rep_sizes, every, collective):
    pieces = math.prod(rep_sizes)
    span = chosen.shape[0]
    rows, width = projected.shape
    vmem = pl.BlockSpec(memory_space=pltpu.VMEM)
    moved = (2 * rows * width * 2 + rows * rows * 2) * span
    return pl.pallas_call(
        functools.partial(window_kernel, blk_sizes, rep_sizes, every),
        out_shape=(
            jax.ShapeDtypeStruct((pieces, rows, width // pieces), jnp.float32),
            jax.ShapeDtypeStruct((pieces, rows, width // pieces), jnp.float32),
        ),
        in_specs=[vmem, vmem, vmem, vmem],
        out_specs=(vmem, vmem),
        scratch_shapes=[
            pltpu.VMEM((span, rows, width), projected.dtype),
            pltpu.VMEM((span, rows, width), cotangent.dtype),
            pltpu.VMEM((span, rows, rows), chosen.dtype),
            pltpu.SemaphoreType.DMA((3, 2, span)),
            pltpu.SemaphoreType.DMA((3, 2, span)),
            pltpu.SemaphoreType.DMA((3, 2)),
        ],
        compiler_params=pltpu.CompilerParams(collective_id=collective, has_side_effects=True),
        cost_estimate=pl.CostEstimate(
            flops=4 * span * rows * rows * width, transcendentals=0, bytes_accessed=2 * moved
        ),
    )(projected, cotangent, chosen, chosen_t)


def shards(hidden_pre, adj_vals, adj_cols, w_out, cotangent):
    row_count, feature_width = hidden_pre.shape
    blk_count = lax.axis_size(BLK)
    rep_count = lax.axis_size(REP)
    span = blk_count // rep_count
    blk_pos = lax.axis_index(BLK)
    rep_pos = lax.axis_index(REP)
    cols_here = feature_width // rep_count
    slots = adj_vals.shape[1]

    hidden_act = jnp.maximum(hidden_pre, 0)
    projected = jnp.dot(hidden_act, w_out, preferred_element_type=jnp.float32).astype(jnp.bfloat16)
    own_vals = adj_vals[0]
    own_cols = adj_cols[0]
    section = jnp.mod(blk_pos - own_cols, blk_count) - rep_pos * span

    chosen = jnp.stack(
        [
            sum(jnp.where(section[k] == turn, own_vals[k], 0) for k in range(slots))
            for turn in range(span)
        ]
    )
    blk_sizes = tuple(lax.axis_size(a) for a in BLK)
    rep_sizes = tuple(lax.axis_size(a) for a in REP)
    out_sum, back_sum = window(
        projected, cotangent, chosen, jnp.transpose(chosen, (0, 2, 1)), blk_sizes, rep_sizes, EVERY, 3
    )

    rows = projected.shape[0]
    out_part, back_grad = exchange_many(
        [(out_sum, REP, "sum", jnp.bfloat16), (back_sum, REP, "sum", jnp.bfloat16)], EVERY, 0
    )
    term = lax.dot_general(
        hidden_act, back_grad, (((0,), (0,)), ((), ())), preferred_element_type=jnp.float32
    )
    grad_weight, back_full = exchange_many(
        [
            (term.reshape(blk_count, -1, cols_here), BLK, "sum", jnp.float32),
            (back_grad, REP, "concat", jnp.bfloat16),
        ],
        EVERY,
        1,
    )
    w_rows = lax.dynamic_slice_in_dim(w_out, rep_pos * cols_here, cols_here, 0)
    grad_in = lax.dot_general(
        back_full, w_rows, (((1,), (1,)), ((), ())), preferred_element_type=jnp.float32
    )
    pre_part = lax.dynamic_slice_in_dim(hidden_pre, rep_pos * cols_here, cols_here, 1)
    grad_pre = jnp.where(pre_part > 0, grad_in, 0.0).astype(jnp.bfloat16)
    return (out_part, grad_weight, grad_pre)


def solution(mesh):
    blk_count, rep_count = mesh.devices.shape
    fine = Mesh(mesh.devices.reshape(8, blk_count // 16, 2, rep_count // 2, 2), EVERY)
    placed = (P(BLK, None), P(BLK, REP, None, None), P(BLK, REP), P(), P(BLK, None))
    return jax.shard_map(
        shards,
        mesh=fine,
        in_specs=placed,
        out_specs=(P(BLK, REP), P(BLK, REP), P(BLK, REP)),
        check_vma=False,
    )
```

```python
import functools
import math

import jax
import jax.numpy as jnp
from jax import lax
from jax.experimental import pallas as pl
from jax.experimental.pallas import tpu as pltpu
from jax.sharding import Mesh
from jax.sharding import PartitionSpec as P

MESH_IDS = pl.DeviceIdType.MESH

BLK = ("by", "bx", "bz")
REP = ("rz", "rc")
EVERY = BLK + REP


def shifted_pairs(blk_count, rep_count, per_rep):
    pairs = []
    for b in range(blk_count):
        for r in range(rep_count):
            pairs.append((b * rep_count + r, ((b + per_rep * r) % blk_count) * rep_count + r))
    return pairs


def ring_pairs(count, steps):
    return [(source, (source + steps) % count) for source in range(count)]


def staged_scatter(value, axes, dim):
    sizes = [lax.axis_size(a) for a in axes]
    full = value.shape[dim]
    rest = full // math.prod(sizes)
    shape = value.shape[:dim] + tuple(sizes) + (rest,) + value.shape[dim + 1 :]
    moved = value.reshape(shape)
    order = list(range(dim)) + [dim + i for i in reversed(range(len(axes)))]
    order += list(range(dim + len(axes), len(shape)))
    moved = jnp.transpose(moved, order).reshape(value.shape)
    for a in reversed(axes):
        moved = lax.psum_scatter(moved, a, scatter_dimension=dim, tiled=True)
    return moved


def exchange_kernel(plans, every, *refs):
    count_of = [math.prod(sizes) for _, sizes, _ in plans]
    n = len(plans)
    srcs, outs = refs[:n], refs[n : 2 * n]
    landed, send_sems, recv_sems = refs[2 * n : 3 * n], refs[3 * n : 4 * n], refs[4 * n : 5 * n]
    totals = refs[5 * n : 6 * n]
    barrier = pltpu.get_barrier_semaphore()

    def position(group, sizes):
        me = 0
        for a, s in zip(group, sizes):
            me = me * s + lax.axis_index(a)
        return me

    def target(group, sizes, d):
        coords = {}
        rest = d
        for a, s in reversed(list(zip(group, sizes))):
            coords[a] = rest % s
            rest = rest // s
        return tuple(coords[a] if a in coords else lax.axis_index(a) for a in every)

    def copy(i, d, slot, o):
        group, sizes, mode = plans[i]
        broadcast = mode == "concat"
        return pltpu.make_async_remote_copy(
            src_ref=srcs[i] if broadcast else srcs[i].at[d],
            dst_ref=landed[i].at[slot],
            send_sem=send_sems[i].at[o],
            recv_sem=recv_sems[i].at[slot],
            device_id=target(group, sizes, d),
            device_id_type=MESH_IDS,
        )

    for i, (group, sizes, _) in enumerate(plans):
        me, count = position(group, sizes), count_of[i]

        def greet(o, carry, group=group, sizes=sizes, me=me, count=count):
            pl.semaphore_signal(barrier, inc=1, device_id=target(group, sizes, (me + o) % count),
                                device_id_type=MESH_IDS)
            return carry

        lax.fori_loop(1, count, greet, 0)
    pl.semaphore_wait(barrier, sum(count_of) - n)

    for i, (group, sizes, mode) in enumerate(plans):
        me, count = position(group, sizes), count_of[i]

        def send(o, carry, i=i, me=me, count=count):
            copy(i, (me + o) % count, me, o).start()
            return carry

        lax.fori_loop(1, count, send, 0)
        if mode == "concat":
            width = srcs[i].shape[-1]
            outs[i][:, pl.ds(pl.multiple_of(me * width, width), width)] = srcs[i][...]
        else:
            totals[i][...] = srcs[i][me].astype(jnp.float32)

    for i, (group, sizes, mode) in enumerate(plans):
        me, count = position(group, sizes), count_of[i]

        def finish(o, carry, i=i, me=me, count=count, mode=mode):
            copy(i, (me + o) % count, me, o).wait_send()
            sender = (me + count - o) % count
            copy(i, sender, sender, o).wait_recv()
            if mode == "concat":
                width = srcs[i].shape[-1]
                outs[i][:, pl.ds(pl.multiple_of(sender * width, width), width)] = landed[i][sender]
            else:
                totals[i][...] += landed[i][sender].astype(jnp.float32)
            return carry

        lax.fori_loop(1, count, finish, 0)
        if mode != "concat":
            outs[i][...] = totals[i][...].astype(outs[i].dtype)


def exchange_many(items, every, collective):
    plans, shapes, landings, totals, counts, total = [], [], [], [], [], 0
    for blocks, group, mode, dtype in items:
        sizes = tuple(lax.axis_size(a) for a in group)
        count = math.prod(sizes)
        if mode == "concat":
            slot_shape = blocks.shape
            shapes.append(jax.ShapeDtypeStruct(blocks.shape[:-1] + (count * blocks.shape[-1],), dtype))
        else:
            slot_shape = blocks.shape[1:]
            shapes.append(jax.ShapeDtypeStruct(slot_shape, dtype))
        plans.append((group, sizes, mode))
        counts.append(count)
        landings.append(pltpu.VMEM((count,) + slot_shape, blocks.dtype))
        totals.append(pltpu.VMEM(slot_shape, jnp.float32))
        total += count * math.prod(slot_shape) * blocks.dtype.itemsize
    vmem = pl.BlockSpec(memory_space=pltpu.VMEM)
    return pl.pallas_call(
        functools.partial(exchange_kernel, tuple(plans), every),
        out_shape=tuple(shapes),
        in_specs=[vmem] * len(items),
        out_specs=tuple([vmem] * len(items)),
        scratch_shapes=landings
        + [pltpu.SemaphoreType.DMA((c,)) for c in counts]
        + [pltpu.SemaphoreType.DMA((c,)) for c in counts]
        + totals,
        compiler_params=pltpu.CompilerParams(collective_id=collective, has_side_effects=True),
        cost_estimate=pl.CostEstimate(flops=0, transcendentals=0, bytes_accessed=3 * total),
    )(*[item[0] for item in items])


def window_kernel(blk_sizes, rep_sizes, every, proj_ref, cot_ref, chosen_ref, sent_ref, out_ref, back_ref,
                  p_got, cot_got, ch_got, send_sem, recv_sem, local_sem):
    blk_count = math.prod(blk_sizes)
    span = chosen_ref.shape[0]
    blk_axes, rep_axes = every[: len(blk_sizes)], every[len(blk_sizes) :]
    b = 0
    for a, s in zip(blk_axes, blk_sizes):
        b = b * s + lax.axis_index(a)
    r = 0
    for a, s in zip(rep_axes, rep_sizes):
        r = r * s + lax.axis_index(a)
    far = span * r

    def target(offset):
        rest = (b + offset + blk_count) % blk_count
        coords = []
        for s in reversed(blk_sizes):
            coords.append(rest % s)
            rest = rest // s
        return tuple(reversed(coords)) + tuple(lax.axis_index(a) for a in rep_axes)

    def remote(src, dst, kind, h, t, offset):
        return pltpu.make_async_remote_copy(src, dst, send_sem.at[kind, h, t], recv_sem.at[kind, h, t],
                                            device_id=target(offset), device_id_type=MESH_IDS)

    splits = 4
    half = proj_ref.shape[0] // splits

    def rows(h):
        return pl.ds(h * half, half)

    def relay_moves(h):
        moves = (
            remote(proj_ref.at[rows(h)], p_got.at[0, rows(h)], 0, h, 0, far),
            remote(cot_ref.at[rows(h)], cot_got.at[0, rows(h)], 1, h, 0, -far),
        )
        if h == 0:
            moves += (remote(sent_ref.at[0], ch_got.at[0], 2, 0, 0, -far),)
        return moves

    def local_moves(h):
        moves = (
            pltpu.make_async_copy(proj_ref.at[rows(h)], p_got.at[0, rows(h)], local_sem.at[0, h]),
            pltpu.make_async_copy(cot_ref.at[rows(h)], cot_got.at[0, rows(h)], local_sem.at[1, h]),
        )
        if h == 0:
            moves += (pltpu.make_async_copy(sent_ref.at[0], ch_got.at[0], local_sem.at[2, 0]),)
        return moves

    def chosen_move(t):
        return remote(sent_ref.at[t], ch_got.at[t], 2, 0, t, -far - t)

    def forwards(t, h):
        return (
            remote(p_got.at[0, rows(h)], p_got.at[t, rows(h)], 0, h, t, t),
            remote(cot_got.at[0, rows(h)], cot_got.at[t, rows(h)], 1, h, t, -t),
        )

    barrier = pltpu.get_barrier_semaphore()

    def greet(offset):
        pl.semaphore_signal(barrier, inc=1, device_id=target(offset), device_id_type=MESH_IDS)
        pl.semaphore_signal(barrier, inc=1, device_id=target(-offset), device_id_type=MESH_IDS)

    for t in range(1, span):
        greet(far + t)
        greet(t)

    @pl.when(r != 0)
    def _():
        greet(far)
        greet(far)
        pl.semaphore_wait(barrier, 4 * span)
        for h in range(splits):
            for c in relay_moves(h):
                c.start()

    @pl.when(r == 0)
    def _():
        pl.semaphore_wait(barrier, 4 * span - 4)
        for h in range(splits):
            for c in local_moves(h):
                c.start()

    for t in range(1, span):
        chosen_move(t).start()

    for h in range(splits):

        @pl.when(r != 0)
        def _():
            for c in relay_moves(h):
                c.wait_recv()

        @pl.when(r == 0)
        def _():
            for c in local_moves(h):
                c.wait()

        for t in range(1, span):
            for c in forwards(t, h):
                c.start()

    for t in range(span):
        if t > 0:
            for h in range(splits):
                for c in forwards(t, h):
                    c.wait_recv()
            chosen_move(t).wait_recv()
        part = jnp.dot(chosen_ref[t], p_got[t], preferred_element_type=jnp.float32)
        back = jnp.dot(ch_got[t], cot_got[t], preferred_element_type=jnp.float32)
        width = out_ref.shape[-1]
        for q in range(out_ref.shape[0]):
            columns = slice(q * width, (q + 1) * width)
            if t == 0:
                out_ref[q] = part[:, columns]
                back_ref[q] = back[:, columns]
            else:
                out_ref[q] += part[:, columns]
                back_ref[q] += back[:, columns]

    @pl.when(r != 0)
    def _():
        for h in range(splits):
            for c in relay_moves(h):
                c.wait_send()

    for t in range(1, span):
        chosen_move(t).wait_send()
        for h in range(splits):
            for c in forwards(t, h):
                c.wait_send()


def window(projected, cotangent, chosen, chosen_t, blk_sizes, rep_sizes, every, collective):
    pieces = math.prod(rep_sizes)
    span = chosen.shape[0]
    rows, width = projected.shape
    vmem = pl.BlockSpec(memory_space=pltpu.VMEM)
    moved = (2 * rows * width * 2 + rows * rows * 2) * span
    return pl.pallas_call(
        functools.partial(window_kernel, blk_sizes, rep_sizes, every),
        out_shape=(
            jax.ShapeDtypeStruct((pieces, rows, width // pieces), jnp.float32),
            jax.ShapeDtypeStruct((pieces, rows, width // pieces), jnp.float32),
        ),
        in_specs=[vmem, vmem, vmem, vmem],
        out_specs=(vmem, vmem),
        scratch_shapes=[
            pltpu.VMEM((span, rows, width), projected.dtype),
            pltpu.VMEM((span, rows, width), cotangent.dtype),
            pltpu.VMEM((span, rows, rows), chosen.dtype),
            pltpu.SemaphoreType.DMA((3, 4, span)),
            pltpu.SemaphoreType.DMA((3, 4, span)),
            pltpu.SemaphoreType.DMA((3, 4)),
        ],
        compiler_params=pltpu.CompilerParams(collective_id=collective, has_side_effects=True),
        cost_estimate=pl.CostEstimate(
            flops=4 * span * rows * rows * width, transcendentals=0, bytes_accessed=2 * moved
        ),
    )(projected, cotangent, chosen, chosen_t)


def shards(hidden_pre, adj_vals, adj_cols, w_out, cotangent):
    row_count, feature_width = hidden_pre.shape
    blk_count = lax.axis_size(BLK)
    rep_count = lax.axis_size(REP)
    span = blk_count // rep_count
    blk_pos = lax.axis_index(BLK)
    rep_pos = lax.axis_index(REP)
    cols_here = feature_width // rep_count
    slots = adj_vals.shape[1]

    hidden_act = jnp.maximum(hidden_pre, 0)
    projected = jnp.dot(hidden_act, w_out, preferred_element_type=jnp.float32).astype(jnp.bfloat16)
    own_vals = adj_vals[0]
    own_cols = adj_cols[0]
    section = jnp.mod(blk_pos - own_cols, blk_count) - rep_pos * span

    chosen = jnp.stack(
        [
            sum(jnp.where(section[k] == turn, own_vals[k], 0) for k in range(slots))
            for turn in range(span)
        ]
    )
    blk_sizes = tuple(lax.axis_size(a) for a in BLK)
    rep_sizes = tuple(lax.axis_size(a) for a in REP)
    out_sum, back_sum = window(
        projected, cotangent, chosen, jnp.transpose(chosen, (0, 2, 1)), blk_sizes, rep_sizes, EVERY, 3
    )

    rows = projected.shape[0]
    out_part, back_grad = exchange_many(
        [(out_sum, REP, "sum", jnp.bfloat16), (back_sum, REP, "sum", jnp.bfloat16)], EVERY, 0
    )
    term = lax.dot_general(
        hidden_act, back_grad, (((0,), (0,)), ((), ())), preferred_element_type=jnp.float32
    )
    grad_weight, back_full = exchange_many(
        [
            (term.reshape(blk_count, -1, cols_here), BLK, "sum", jnp.float32),
            (back_grad, REP, "concat", jnp.bfloat16),
        ],
        EVERY,
        1,
    )
    w_rows = lax.dynamic_slice_in_dim(w_out, rep_pos * cols_here, cols_here, 0)
    grad_in = lax.dot_general(
        back_full, w_rows, (((1,), (1,)), ((), ())), preferred_element_type=jnp.float32
    )
    pre_part = lax.dynamic_slice_in_dim(hidden_pre, rep_pos * cols_here, cols_here, 1)
    grad_pre = jnp.where(pre_part > 0, grad_in, 0.0).astype(jnp.bfloat16)
    return (out_part, grad_weight, grad_pre)


def solution(mesh):
    blk_count, rep_count = mesh.devices.shape
    fine = Mesh(mesh.devices.reshape(8, blk_count // 16, 2, rep_count // 2, 2), EVERY)
    placed = (P(BLK, None), P(BLK, REP, None, None), P(BLK, REP), P(), P(BLK, None))
    return jax.shard_map(
        shards,
        mesh=fine,
        in_specs=placed,
        out_specs=(P(BLK, REP), P(BLK, REP), P(BLK, REP)),
        check_vma=False,
    )
```

```python
import functools
import math

import jax
import jax.numpy as jnp
from jax import lax
from jax.experimental import pallas as pl
from jax.experimental.pallas import tpu as pltpu
from jax.sharding import Mesh
from jax.sharding import PartitionSpec as P

MESH_IDS = pl.DeviceIdType.MESH

BLK = ("by", "bx", "bz")
REP = ("rz", "rc")
EVERY = BLK + REP


def shifted_pairs(blk_count, rep_count, per_rep):
    pairs = []
    for b in range(blk_count):
        for r in range(rep_count):
            pairs.append((b * rep_count + r, ((b + per_rep * r) % blk_count) * rep_count + r))
    return pairs


def ring_pairs(count, steps):
    return [(source, (source + steps) % count) for source in range(count)]


def staged_scatter(value, axes, dim):
    sizes = [lax.axis_size(a) for a in axes]
    full = value.shape[dim]
    rest = full // math.prod(sizes)
    shape = value.shape[:dim] + tuple(sizes) + (rest,) + value.shape[dim + 1 :]
    moved = value.reshape(shape)
    order = list(range(dim)) + [dim + i for i in reversed(range(len(axes)))]
    order += list(range(dim + len(axes), len(shape)))
    moved = jnp.transpose(moved, order).reshape(value.shape)
    for a in reversed(axes):
        moved = lax.psum_scatter(moved, a, scatter_dimension=dim, tiled=True)
    return moved


def exchange_kernel(plans, every, *refs):
    count_of = [math.prod(sizes) for _, sizes, _ in plans]
    n = len(plans)
    srcs, outs = refs[:n], refs[n : 2 * n]
    landed, send_sems, recv_sems = refs[2 * n : 3 * n], refs[3 * n : 4 * n], refs[4 * n : 5 * n]
    totals = refs[5 * n : 6 * n]
    barrier = pltpu.get_barrier_semaphore()

    def position(group, sizes):
        me = 0
        for a, s in zip(group, sizes):
            me = me * s + lax.axis_index(a)
        return me

    def target(group, sizes, d):
        coords = {}
        rest = d
        for a, s in reversed(list(zip(group, sizes))):
            coords[a] = rest % s
            rest = rest // s
        return tuple(coords[a] if a in coords else lax.axis_index(a) for a in every)

    def copy(i, d, slot, o):
        group, sizes, mode = plans[i]
        broadcast = mode == "concat"
        return pltpu.make_async_remote_copy(
            src_ref=srcs[i] if broadcast else srcs[i].at[d],
            dst_ref=landed[i].at[slot],
            send_sem=send_sems[i].at[o],
            recv_sem=recv_sems[i].at[slot],
            device_id=target(group, sizes, d),
            device_id_type=MESH_IDS,
        )

    for i, (group, sizes, _) in enumerate(plans):
        me, count = position(group, sizes), count_of[i]

        def greet(o, carry, group=group, sizes=sizes, me=me, count=count):
            pl.semaphore_signal(barrier, inc=1, device_id=target(group, sizes, (me + o) % count),
                                device_id_type=MESH_IDS)
            return carry

        lax.fori_loop(1, count, greet, 0)
    pl.semaphore_wait(barrier, sum(count_of) - n)

    for i, (group, sizes, mode) in enumerate(plans):
        me, count = position(group, sizes), count_of[i]

        def send(o, carry, i=i, me=me, count=count):
            copy(i, (me + o) % count, me, o).start()
            return carry

        lax.fori_loop(1, count, send, 0)
        if mode == "concat":
            width = srcs[i].shape[-1]
            outs[i][:, pl.ds(pl.multiple_of(me * width, width), width)] = srcs[i][...]
        else:
            totals[i][...] = srcs[i][me].astype(jnp.float32)

    for i, (group, sizes, mode) in enumerate(plans):
        me, count = position(group, sizes), count_of[i]

        def finish(o, carry, i=i, me=me, count=count, mode=mode):
            copy(i, (me + o) % count, me, o).wait_send()
            sender = (me + count - o) % count
            copy(i, sender, sender, o).wait_recv()
            if mode == "concat":
                width = srcs[i].shape[-1]
                outs[i][:, pl.ds(pl.multiple_of(sender * width, width), width)] = landed[i][sender]
            else:
                totals[i][...] += landed[i][sender].astype(jnp.float32)
            return carry

        lax.fori_loop(1, count, finish, 0)
        if mode != "concat":
            outs[i][...] = totals[i][...].astype(outs[i].dtype)


def exchange_many(items, every, collective):
    plans, shapes, landings, totals, counts, total = [], [], [], [], [], 0
    for blocks, group, mode, dtype in items:
        sizes = tuple(lax.axis_size(a) for a in group)
        count = math.prod(sizes)
        if mode == "concat":
            slot_shape = blocks.shape
            shapes.append(jax.ShapeDtypeStruct(blocks.shape[:-1] + (count * blocks.shape[-1],), dtype))
        else:
            slot_shape = blocks.shape[1:]
            shapes.append(jax.ShapeDtypeStruct(slot_shape, dtype))
        plans.append((group, sizes, mode))
        counts.append(count)
        landings.append(pltpu.VMEM((count,) + slot_shape, blocks.dtype))
        totals.append(pltpu.VMEM(slot_shape, jnp.float32))
        total += count * math.prod(slot_shape) * blocks.dtype.itemsize
    vmem = pl.BlockSpec(memory_space=pltpu.VMEM)
    return pl.pallas_call(
        functools.partial(exchange_kernel, tuple(plans), every),
        out_shape=tuple(shapes),
        in_specs=[vmem] * len(items),
        out_specs=tuple([vmem] * len(items)),
        scratch_shapes=landings
        + [pltpu.SemaphoreType.DMA((c,)) for c in counts]
        + [pltpu.SemaphoreType.DMA((c,)) for c in counts]
        + totals,
        compiler_params=pltpu.CompilerParams(collective_id=collective, has_side_effects=True),
        cost_estimate=pl.CostEstimate(flops=0, transcendentals=0, bytes_accessed=3 * total),
    )(*[item[0] for item in items])


def window_kernel(blk_sizes, rep_sizes, every, proj_ref, cot_ref, chosen_ref, sent_ref, out_ref, back_ref,
                  p_got, cot_got, ch_got, send_sem, recv_sem, local_sem, acc):
    blk_count = math.prod(blk_sizes)
    span = chosen_ref.shape[0]
    blk_axes, rep_axes = every[: len(blk_sizes)], every[len(blk_sizes) :]
    b = 0
    for a, s in zip(blk_axes, blk_sizes):
        b = b * s + lax.axis_index(a)
    r = 0
    for a, s in zip(rep_axes, rep_sizes):
        r = r * s + lax.axis_index(a)
    far = span * r

    def target(offset):
        rest = (b + offset + blk_count) % blk_count
        coords = []
        for s in reversed(blk_sizes):
            coords.append(rest % s)
            rest = rest // s
        return tuple(reversed(coords)) + tuple(lax.axis_index(a) for a in rep_axes)

    def remote(src, dst, kind, h, t, offset):
        return pltpu.make_async_remote_copy(src, dst, send_sem.at[kind, h, t], recv_sem.at[kind, h, t],
                                            device_id=target(offset), device_id_type=MESH_IDS)

    splits = 4
    half = proj_ref.shape[0] // splits

    def rows(h):
        return pl.ds(h * half, half)

    def relay_moves(h):
        moves = (
            remote(proj_ref.at[rows(h)], p_got.at[0, rows(h)], 0, h, 0, far),
            remote(cot_ref.at[rows(h)], cot_got.at[0, rows(h)], 1, h, 0, -far),
        )
        if h == 0:
            moves += (remote(sent_ref.at[0], ch_got.at[0], 2, 0, 0, -far),)
        return moves

    def local_moves(h):
        moves = (
            pltpu.make_async_copy(proj_ref.at[rows(h)], p_got.at[0, rows(h)], local_sem.at[0, h]),
            pltpu.make_async_copy(cot_ref.at[rows(h)], cot_got.at[0, rows(h)], local_sem.at[1, h]),
        )
        if h == 0:
            moves += (pltpu.make_async_copy(sent_ref.at[0], ch_got.at[0], local_sem.at[2, 0]),)
        return moves

    def chosen_move(t):
        return remote(sent_ref.at[t], ch_got.at[t], 2, 0, t, -far - t)

    def forwards(t, h):
        return (
            remote(p_got.at[0, rows(h)], p_got.at[t, rows(h)], 0, h, t, t),
            remote(cot_got.at[0, rows(h)], cot_got.at[t, rows(h)], 1, h, t, -t),
        )

    barrier = pltpu.get_barrier_semaphore()

    def greet(offset):
        pl.semaphore_signal(barrier, inc=1, device_id=target(offset), device_id_type=MESH_IDS)
        pl.semaphore_signal(barrier, inc=1, device_id=target(-offset), device_id_type=MESH_IDS)

    for t in range(1, span):
        greet(far + t)
        greet(t)

    @pl.when(r != 0)
    def _():
        greet(far)
        greet(far)
        pl.semaphore_wait(barrier, 4 * span)
        for h in range(splits):
            for c in relay_moves(h):
                c.start()

    @pl.when(r == 0)
    def _():
        pl.semaphore_wait(barrier, 4 * span - 4)
        for h in range(splits):
            for c in local_moves(h):
                c.start()

    for t in range(1, span):
        chosen_move(t).start()

    for h in range(splits):

        @pl.when(r != 0)
        def _():
            for c in relay_moves(h):
                c.wait_recv()

        @pl.when(r == 0)
        def _():
            for c in local_moves(h):
                c.wait()

        for t in range(1, span):
            for c in forwards(t, h):
                c.start()

    for t in range(span):
        if t > 0:
            for h in range(splits):
                for c in forwards(t, h):
                    c.wait_recv()
            chosen_move(t).wait_recv()
        part = jnp.dot(chosen_ref[t], p_got[t], preferred_element_type=jnp.float32)
        back = jnp.dot(ch_got[t], cot_got[t], preferred_element_type=jnp.float32)
        if t == 0:
            acc[0] = part
            acc[1] = back
        else:
            acc[0] += part
            acc[1] += back

    width = out_ref.shape[-1]
    for q in range(out_ref.shape[0]):
        columns = pl.ds(q * width, width)
        out_ref[q] = acc[0, :, columns].astype(out_ref.dtype)
        back_ref[q] = acc[1, :, columns].astype(back_ref.dtype)

    @pl.when(r != 0)
    def _():
        for h in range(splits):
            for c in relay_moves(h):
                c.wait_send()

    for t in range(1, span):
        chosen_move(t).wait_send()
        for h in range(splits):
            for c in forwards(t, h):
                c.wait_send()


def window(projected, cotangent, chosen, chosen_t, blk_sizes, rep_sizes, every, collective):
    pieces = math.prod(rep_sizes)
    span = chosen.shape[0]
    rows, width = projected.shape
    vmem = pl.BlockSpec(memory_space=pltpu.VMEM)
    moved = (2 * rows * width * 2 + rows * rows * 2) * span
    return pl.pallas_call(
        functools.partial(window_kernel, blk_sizes, rep_sizes, every),
        out_shape=(
            jax.ShapeDtypeStruct((pieces, rows, width // pieces), jnp.bfloat16),
            jax.ShapeDtypeStruct((pieces, rows, width // pieces), jnp.bfloat16),
        ),
        in_specs=[vmem, vmem, vmem, vmem],
        out_specs=(vmem, vmem),
        scratch_shapes=[
            pltpu.VMEM((span, rows, width), projected.dtype),
            pltpu.VMEM((span, rows, width), cotangent.dtype),
            pltpu.VMEM((span, rows, rows), chosen.dtype),
            pltpu.SemaphoreType.DMA((3, 4, span)),
            pltpu.SemaphoreType.DMA((3, 4, span)),
            pltpu.SemaphoreType.DMA((3, 4)),
            pltpu.VMEM((2, rows, width), jnp.float32),
        ],
        compiler_params=pltpu.CompilerParams(collective_id=collective, has_side_effects=True),
        cost_estimate=pl.CostEstimate(
            flops=4 * span * rows * rows * width, transcendentals=0, bytes_accessed=2 * moved
        ),
    )(projected, cotangent, chosen, chosen_t)


def shards(hidden_pre, adj_vals, adj_cols, w_out, cotangent):
    row_count, feature_width = hidden_pre.shape
    blk_count = lax.axis_size(BLK)
    rep_count = lax.axis_size(REP)
    span = blk_count // rep_count
    blk_pos = lax.axis_index(BLK)
    rep_pos = lax.axis_index(REP)
    cols_here = feature_width // rep_count
    slots = adj_vals.shape[1]

    hidden_act = jnp.maximum(hidden_pre, 0)
    projected = jnp.dot(hidden_act, w_out, preferred_element_type=jnp.float32).astype(jnp.bfloat16)
    own_vals = adj_vals[0]
    own_cols = adj_cols[0]
    section = jnp.mod(blk_pos - own_cols, blk_count) - rep_pos * span

    chosen = jnp.stack(
        [
            sum(jnp.where(section[k] == turn, own_vals[k], 0) for k in range(slots))
            for turn in range(span)
        ]
    )
    blk_sizes = tuple(lax.axis_size(a) for a in BLK)
    rep_sizes = tuple(lax.axis_size(a) for a in REP)
    out_sum, back_sum = window(
        projected, cotangent, chosen, jnp.transpose(chosen, (0, 2, 1)), blk_sizes, rep_sizes, EVERY, 3
    )

    rows = projected.shape[0]
    out_part, back_grad = exchange_many(
        [(out_sum, REP, "sum", jnp.bfloat16), (back_sum, REP, "sum", jnp.bfloat16)], EVERY, 0
    )
    term = lax.dot_general(
        hidden_act, back_grad, (((0,), (0,)), ((), ())), preferred_element_type=jnp.float32
    )
    grad_weight, back_full = exchange_many(
        [
            (term.reshape(blk_count, -1, cols_here), BLK, "sum", jnp.float32),
            (back_grad, REP, "concat", jnp.bfloat16),
        ],
        EVERY,
        1,
    )
    w_rows = lax.dynamic_slice_in_dim(w_out, rep_pos * cols_here, cols_here, 0)
    grad_in = lax.dot_general(
        back_full, w_rows, (((1,), (1,)), ((), ())), preferred_element_type=jnp.float32
    )
    pre_part = lax.dynamic_slice_in_dim(hidden_pre, rep_pos * cols_here, cols_here, 1)
    grad_pre = jnp.where(pre_part > 0, grad_in, 0.0).astype(jnp.bfloat16)
    return (out_part, grad_weight, grad_pre)


def solution(mesh):
    blk_count, rep_count = mesh.devices.shape
    fine = Mesh(mesh.devices.reshape(8, blk_count // 16, 2, rep_count // 2, 2), EVERY)
    placed = (P(BLK, None), P(BLK, REP, None, None), P(BLK, REP), P(), P(BLK, None))
    return jax.shard_map(
        shards,
        mesh=fine,
        in_specs=placed,
        out_specs=(P(BLK, REP), P(BLK, REP), P(BLK, REP)),
        check_vma=False,
    )
```

```python
import functools
import math

import jax
import jax.numpy as jnp
from jax import lax
from jax.experimental import pallas as pl
from jax.experimental.pallas import tpu as pltpu
from jax.sharding import Mesh
from jax.sharding import PartitionSpec as P

MESH_IDS = pl.DeviceIdType.MESH

BLK = ("by", "bx", "bz")
REP = ("rz", "rc")
EVERY = BLK + REP


def shifted_pairs(blk_count, rep_count, per_rep):
    pairs = []
    for b in range(blk_count):
        for r in range(rep_count):
            pairs.append((b * rep_count + r, ((b + per_rep * r) % blk_count) * rep_count + r))
    return pairs


def ring_pairs(count, steps):
    return [(source, (source + steps) % count) for source in range(count)]


def staged_scatter(value, axes, dim):
    sizes = [lax.axis_size(a) for a in axes]
    full = value.shape[dim]
    rest = full // math.prod(sizes)
    shape = value.shape[:dim] + tuple(sizes) + (rest,) + value.shape[dim + 1 :]
    moved = value.reshape(shape)
    order = list(range(dim)) + [dim + i for i in reversed(range(len(axes)))]
    order += list(range(dim + len(axes), len(shape)))
    moved = jnp.transpose(moved, order).reshape(value.shape)
    for a in reversed(axes):
        moved = lax.psum_scatter(moved, a, scatter_dimension=dim, tiled=True)
    return moved


def exchange_kernel(plans, every, *refs):
    count_of = [math.prod(sizes) for _, sizes, _ in plans]
    n = len(plans)
    srcs, outs = refs[:n], refs[n : 2 * n]
    landed, send_sems, recv_sems = refs[2 * n : 3 * n], refs[3 * n : 4 * n], refs[4 * n : 5 * n]
    totals = refs[5 * n : 6 * n]
    barrier = pltpu.get_barrier_semaphore()

    def position(group, sizes):
        me = 0
        for a, s in zip(group, sizes):
            me = me * s + lax.axis_index(a)
        return me

    def target(group, sizes, d):
        coords = {}
        rest = d
        for a, s in reversed(list(zip(group, sizes))):
            coords[a] = rest % s
            rest = rest // s
        return tuple(coords[a] if a in coords else lax.axis_index(a) for a in every)

    def copy(i, d, slot, o):
        group, sizes, mode = plans[i]
        broadcast = mode == "concat"
        return pltpu.make_async_remote_copy(
            src_ref=srcs[i] if broadcast else srcs[i].at[d],
            dst_ref=landed[i].at[slot],
            send_sem=send_sems[i].at[o],
            recv_sem=recv_sems[i].at[slot],
            device_id=target(group, sizes, d),
            device_id_type=MESH_IDS,
        )

    for i, (group, sizes, _) in enumerate(plans):
        me, count = position(group, sizes), count_of[i]

        def greet(o, carry, group=group, sizes=sizes, me=me, count=count):
            pl.semaphore_signal(barrier, inc=1, device_id=target(group, sizes, (me + o) % count),
                                device_id_type=MESH_IDS)
            return carry

        lax.fori_loop(1, count, greet, 0)
    pl.semaphore_wait(barrier, sum(count_of) - n)

    for i, (group, sizes, mode) in enumerate(plans):
        me, count = position(group, sizes), count_of[i]

        def send(o, carry, i=i, me=me, count=count):
            copy(i, (me + o) % count, me, o).start()
            return carry

        lax.fori_loop(1, count, send, 0)
        if mode == "concat":
            width = srcs[i].shape[-1]
            outs[i][:, pl.ds(pl.multiple_of(me * width, width), width)] = srcs[i][...]
        else:
            totals[i][...] = srcs[i][me].astype(jnp.float32)

    for i, (group, sizes, mode) in enumerate(plans):
        me, count = position(group, sizes), count_of[i]

        def finish(o, carry, i=i, me=me, count=count, mode=mode):
            copy(i, (me + o) % count, me, o).wait_send()
            sender = (me + count - o) % count
            copy(i, sender, sender, o).wait_recv()
            if mode == "concat":
                width = srcs[i].shape[-1]
                outs[i][:, pl.ds(pl.multiple_of(sender * width, width), width)] = landed[i][sender]
            else:
                totals[i][...] += landed[i][sender].astype(jnp.float32)
            return carry

        lax.fori_loop(1, count, finish, 0)
        if mode != "concat":
            outs[i][...] = totals[i][...].astype(outs[i].dtype)


def exchange_many(items, every, collective):
    plans, shapes, landings, totals, counts, total = [], [], [], [], [], 0
    for blocks, group, mode, dtype in items:
        sizes = tuple(lax.axis_size(a) for a in group)
        count = math.prod(sizes)
        if mode == "concat":
            slot_shape = blocks.shape
            shapes.append(jax.ShapeDtypeStruct(blocks.shape[:-1] + (count * blocks.shape[-1],), dtype))
        else:
            slot_shape = blocks.shape[1:]
            shapes.append(jax.ShapeDtypeStruct(slot_shape, dtype))
        plans.append((group, sizes, mode))
        counts.append(count)
        landings.append(pltpu.VMEM((count,) + slot_shape, blocks.dtype))
        totals.append(pltpu.VMEM(slot_shape, jnp.float32))
        total += count * math.prod(slot_shape) * blocks.dtype.itemsize
    vmem = pl.BlockSpec(memory_space=pltpu.VMEM)
    return pl.pallas_call(
        functools.partial(exchange_kernel, tuple(plans), every),
        out_shape=tuple(shapes),
        in_specs=[vmem] * len(items),
        out_specs=tuple([vmem] * len(items)),
        scratch_shapes=landings
        + [pltpu.SemaphoreType.DMA((c,)) for c in counts]
        + [pltpu.SemaphoreType.DMA((c,)) for c in counts]
        + totals,
        compiler_params=pltpu.CompilerParams(collective_id=collective, has_side_effects=True),
        cost_estimate=pl.CostEstimate(flops=0, transcendentals=0, bytes_accessed=3 * total),
    )(*[item[0] for item in items])


def window_kernel(blk_sizes, rep_sizes, every, proj_ref, cot_ref, chosen_ref, sent_ref, out_ref, back_ref,
                  p_got, cot_got, ch_got, send_sem, recv_sem, local_sem, acc):
    blk_count = math.prod(blk_sizes)
    span = chosen_ref.shape[0]
    blk_axes, rep_axes = every[: len(blk_sizes)], every[len(blk_sizes) :]
    b = 0
    for a, s in zip(blk_axes, blk_sizes):
        b = b * s + lax.axis_index(a)
    r = 0
    for a, s in zip(rep_axes, rep_sizes):
        r = r * s + lax.axis_index(a)
    far = span * r

    def target(offset):
        rest = (b + offset + blk_count) % blk_count
        coords = []
        for s in reversed(blk_sizes):
            coords.append(rest % s)
            rest = rest // s
        return tuple(reversed(coords)) + tuple(lax.axis_index(a) for a in rep_axes)

    def remote(src, dst, kind, h, t, offset):
        return pltpu.make_async_remote_copy(src, dst, send_sem.at[kind, h, t], recv_sem.at[kind, h, t],
                                            device_id=target(offset), device_id_type=MESH_IDS)

    splits = 4
    half = proj_ref.shape[0] // splits

    def rows(h):
        return pl.ds(h * half, half)

    def relay_moves(h):
        moves = (
            remote(proj_ref.at[rows(h)], p_got.at[0, rows(h)], 0, h, 0, far),
            remote(cot_ref.at[rows(h)], cot_got.at[0, rows(h)], 1, h, 0, -far),
        )
        if h == 0:
            moves += (remote(sent_ref.at[0], ch_got.at[0], 2, 0, 0, -far),)
        return moves

    def local_moves(h):
        moves = (
            pltpu.make_async_copy(proj_ref.at[rows(h)], p_got.at[0, rows(h)], local_sem.at[0, h]),
            pltpu.make_async_copy(cot_ref.at[rows(h)], cot_got.at[0, rows(h)], local_sem.at[1, h]),
        )
        if h == 0:
            moves += (pltpu.make_async_copy(sent_ref.at[0], ch_got.at[0], local_sem.at[2, 0]),)
        return moves

    def chosen_move(t):
        return remote(sent_ref.at[t], ch_got.at[t], 2, 0, t, -far - t)

    def forwards(t, h):
        return (
            remote(p_got.at[0, rows(h)], p_got.at[t, rows(h)], 0, h, t, t),
            remote(cot_got.at[0, rows(h)], cot_got.at[t, rows(h)], 1, h, t, -t),
        )

    barrier = pltpu.get_barrier_semaphore()

    def greet(offset):
        pl.semaphore_signal(barrier, inc=1, device_id=target(offset), device_id_type=MESH_IDS)
        pl.semaphore_signal(barrier, inc=1, device_id=target(-offset), device_id_type=MESH_IDS)

    for t in range(1, span):
        greet(far + t)
        greet(t)

    @pl.when(r != 0)
    def _():
        greet(far)
        greet(far)
        pl.semaphore_wait(barrier, 4 * span)
        for h in range(splits):
            for c in relay_moves(h):
                c.start()

    @pl.when(r == 0)
    def _():
        pl.semaphore_wait(barrier, 4 * span - 4)
        for h in range(splits):
            for c in local_moves(h):
                c.start()

    for t in range(1, span):
        chosen_move(t).start()

    for h in range(splits):

        @pl.when(r != 0)
        def _():
            for c in relay_moves(h):
                c.wait_recv()

        @pl.when(r == 0)
        def _():
            for c in local_moves(h):
                c.wait()

        for t in range(1, span):
            for c in forwards(t, h):
                c.start()

    for t in range(span):
        if t > 0:
            for h in range(splits):
                for c in forwards(t, h):
                    c.wait_recv()
            chosen_move(t).wait_recv()
        part = jnp.dot(chosen_ref[t], p_got[t], preferred_element_type=jnp.float32)
        back = jnp.dot(ch_got[t], cot_got[t], preferred_element_type=jnp.float32)
        if t == 0:
            acc[0] = part
            acc[1] = back
        else:
            acc[0] += part
            acc[1] += back

    width = out_ref.shape[-1]
    for q in range(out_ref.shape[0]):
        columns = pl.ds(q * width, width)
        out_ref[q] = acc[0, :, columns].astype(out_ref.dtype)
        back_ref[q] = acc[1, :, columns].astype(back_ref.dtype)

    @pl.when(r != 0)
    def _():
        for h in range(splits):
            for c in relay_moves(h):
                c.wait_send()

    for t in range(1, span):
        chosen_move(t).wait_send()
        for h in range(splits):
            for c in forwards(t, h):
                c.wait_send()


def window(projected, cotangent, chosen, chosen_t, blk_sizes, rep_sizes, every, collective):
    pieces = math.prod(rep_sizes)
    span = chosen.shape[0]
    rows, width = projected.shape
    vmem = pl.BlockSpec(memory_space=pltpu.VMEM)
    moved = (2 * rows * width * 2 + rows * rows * 2) * span
    return pl.pallas_call(
        functools.partial(window_kernel, blk_sizes, rep_sizes, every),
        out_shape=(
            jax.ShapeDtypeStruct((pieces, rows, width // pieces), jnp.bfloat16),
            jax.ShapeDtypeStruct((pieces, rows, width // pieces), jnp.bfloat16),
        ),
        in_specs=[vmem, vmem, vmem, vmem],
        out_specs=(vmem, vmem),
        scratch_shapes=[
            pltpu.VMEM((span, rows, width), projected.dtype),
            pltpu.VMEM((span, rows, width), cotangent.dtype),
            pltpu.VMEM((span, rows, rows), chosen.dtype),
            pltpu.SemaphoreType.DMA((3, 4, span)),
            pltpu.SemaphoreType.DMA((3, 4, span)),
            pltpu.SemaphoreType.DMA((3, 4)),
            pltpu.VMEM((2, rows, width), jnp.float32),
        ],
        compiler_params=pltpu.CompilerParams(collective_id=collective, has_side_effects=True),
        cost_estimate=pl.CostEstimate(
            flops=4 * span * rows * rows * width, transcendentals=0, bytes_accessed=2 * moved
        ),
    )(projected, cotangent, chosen, chosen_t)


def shards(hidden_pre, adj_vals, adj_cols, w_out, cotangent):
    row_count, feature_width = hidden_pre.shape
    blk_count = lax.axis_size(BLK)
    rep_count = lax.axis_size(REP)
    span = blk_count // rep_count
    blk_pos = lax.axis_index(BLK)
    rep_pos = lax.axis_index(REP)
    cols_here = feature_width // rep_count
    slots = adj_vals.shape[1]

    hidden_act = jnp.maximum(hidden_pre, 0)
    projected = jnp.dot(hidden_act, w_out, preferred_element_type=jnp.float32).astype(jnp.bfloat16)
    own_vals = adj_vals[0]
    own_cols = adj_cols[0]
    section = jnp.mod(blk_pos - own_cols, blk_count) - rep_pos * span

    picks = (section[None, :] == jnp.arange(span, dtype=section.dtype)[:, None]).astype(own_vals.dtype)
    chosen = jnp.einsum("tk,kab->tab", picks, own_vals, preferred_element_type=jnp.float32).astype(own_vals.dtype)
    chosen_t = jnp.einsum("tk,kab->tba", picks, own_vals, preferred_element_type=jnp.float32).astype(own_vals.dtype)
    blk_sizes = tuple(lax.axis_size(a) for a in BLK)
    rep_sizes = tuple(lax.axis_size(a) for a in REP)
    out_sum, back_sum = window(
        projected, cotangent, chosen, chosen_t, blk_sizes, rep_sizes, EVERY, 3
    )

    rows = projected.shape[0]
    out_part, back_grad = exchange_many(
        [(out_sum, REP, "sum", jnp.bfloat16), (back_sum, REP, "sum", jnp.bfloat16)], EVERY, 0
    )
    term = lax.dot_general(
        hidden_act, back_grad, (((0,), (0,)), ((), ())), preferred_element_type=jnp.float32
    )
    grad_weight, back_full = exchange_many(
        [
            (term.reshape(blk_count, -1, cols_here), BLK, "sum", jnp.float32),
            (back_grad, REP, "concat", jnp.bfloat16),
        ],
        EVERY,
        1,
    )
    w_rows = lax.dynamic_slice_in_dim(w_out, rep_pos * cols_here, cols_here, 0)
    grad_in = lax.dot_general(
        back_full, w_rows, (((1,), (1,)), ((), ())), preferred_element_type=jnp.float32
    )
    pre_part = lax.dynamic_slice_in_dim(hidden_pre, rep_pos * cols_here, cols_here, 1)
    grad_pre = jnp.where(pre_part > 0, grad_in, 0.0).astype(jnp.bfloat16)
    return (out_part, grad_weight, grad_pre)


def solution(mesh):
    blk_count, rep_count = mesh.devices.shape
    fine = Mesh(mesh.devices.reshape(8, blk_count // 16, 2, rep_count // 2, 2), EVERY)
    placed = (P(BLK, None), P(BLK, REP, None, None), P(BLK, REP), P(), P(BLK, None))
    return jax.shard_map(
        shards,
        mesh=fine,
        in_specs=placed,
        out_specs=(P(BLK, REP), P(BLK, REP), P(BLK, REP)),
        check_vma=False,
    )
```

```python
import functools
import math

import jax
import jax.numpy as jnp
from jax import lax
from jax.experimental import pallas as pl
from jax.experimental.pallas import tpu as pltpu
from jax.sharding import Mesh
from jax.sharding import PartitionSpec as P

MESH_IDS = pl.DeviceIdType.MESH

BLK = ("by", "bx", "bz")
REP = ("rz", "rc")
EVERY = BLK + REP


def shifted_pairs(blk_count, rep_count, per_rep):
    pairs = []
    for b in range(blk_count):
        for r in range(rep_count):
            pairs.append((b * rep_count + r, ((b + per_rep * r) % blk_count) * rep_count + r))
    return pairs


def ring_pairs(count, steps):
    return [(source, (source + steps) % count) for source in range(count)]


def staged_scatter(value, axes, dim):
    sizes = [lax.axis_size(a) for a in axes]
    full = value.shape[dim]
    rest = full // math.prod(sizes)
    shape = value.shape[:dim] + tuple(sizes) + (rest,) + value.shape[dim + 1 :]
    moved = value.reshape(shape)
    order = list(range(dim)) + [dim + i for i in reversed(range(len(axes)))]
    order += list(range(dim + len(axes), len(shape)))
    moved = jnp.transpose(moved, order).reshape(value.shape)
    for a in reversed(axes):
        moved = lax.psum_scatter(moved, a, scatter_dimension=dim, tiled=True)
    return moved


def exchange_kernel(plans, every, *refs):
    count_of = [math.prod(sizes) for _, sizes, _ in plans]
    n = len(plans)
    srcs, outs = refs[:n], refs[n : 2 * n]
    landed, send_sems, recv_sems = refs[2 * n : 3 * n], refs[3 * n : 4 * n], refs[4 * n : 5 * n]
    totals = refs[5 * n : 6 * n]
    barrier = pltpu.get_barrier_semaphore()

    def position(group, sizes):
        me = 0
        for a, s in zip(group, sizes):
            me = me * s + lax.axis_index(a)
        return me

    def target(group, sizes, d):
        coords = {}
        rest = d
        for a, s in reversed(list(zip(group, sizes))):
            coords[a] = rest % s
            rest = rest // s
        return tuple(coords[a] if a in coords else lax.axis_index(a) for a in every)

    def copy(i, d, slot, o):
        group, sizes, mode = plans[i]
        broadcast = mode == "concat"
        return pltpu.make_async_remote_copy(
            src_ref=srcs[i] if broadcast else srcs[i].at[d],
            dst_ref=landed[i].at[slot],
            send_sem=send_sems[i].at[o],
            recv_sem=recv_sems[i].at[slot],
            device_id=target(group, sizes, d),
            device_id_type=MESH_IDS,
        )

    for i, (group, sizes, _) in enumerate(plans):
        me, count = position(group, sizes), count_of[i]

        def greet(o, carry, group=group, sizes=sizes, me=me, count=count):
            pl.semaphore_signal(barrier, inc=1, device_id=target(group, sizes, (me + o) % count),
                                device_id_type=MESH_IDS)
            return carry

        lax.fori_loop(1, count, greet, 0)
    pl.semaphore_wait(barrier, sum(count_of) - n)

    for i, (group, sizes, mode) in enumerate(plans):
        me, count = position(group, sizes), count_of[i]

        def send(o, carry, i=i, me=me, count=count):
            copy(i, (me + o) % count, me, o).start()
            return carry

        lax.fori_loop(1, count, send, 0)
        if mode == "concat":
            width = srcs[i].shape[-1]
            outs[i][:, pl.ds(pl.multiple_of(me * width, width), width)] = srcs[i][...]
        else:
            totals[i][...] = srcs[i][me].astype(jnp.float32)

    for i, (group, sizes, mode) in enumerate(plans):
        me, count = position(group, sizes), count_of[i]

        def finish(o, carry, i=i, me=me, count=count, mode=mode):
            copy(i, (me + o) % count, me, o).wait_send()
            sender = (me + count - o) % count
            copy(i, sender, sender, o).wait_recv()
            if mode == "concat":
                width = srcs[i].shape[-1]
                outs[i][:, pl.ds(pl.multiple_of(sender * width, width), width)] = landed[i][sender]
            else:
                totals[i][...] += landed[i][sender].astype(jnp.float32)
            return carry

        lax.fori_loop(1, count, finish, 0)
        if mode != "concat":
            outs[i][...] = totals[i][...].astype(outs[i].dtype)


def exchange_many(items, every, collective):
    plans, shapes, landings, totals, counts, total = [], [], [], [], [], 0
    for blocks, group, mode, dtype in items:
        sizes = tuple(lax.axis_size(a) for a in group)
        count = math.prod(sizes)
        if mode == "concat":
            slot_shape = blocks.shape
            shapes.append(jax.ShapeDtypeStruct(blocks.shape[:-1] + (count * blocks.shape[-1],), dtype))
        else:
            slot_shape = blocks.shape[1:]
            shapes.append(jax.ShapeDtypeStruct(slot_shape, dtype))
        plans.append((group, sizes, mode))
        counts.append(count)
        landings.append(pltpu.VMEM((count,) + slot_shape, blocks.dtype))
        totals.append(pltpu.VMEM(slot_shape, jnp.float32))
        total += count * math.prod(slot_shape) * blocks.dtype.itemsize
    vmem = pl.BlockSpec(memory_space=pltpu.VMEM)
    return pl.pallas_call(
        functools.partial(exchange_kernel, tuple(plans), every),
        out_shape=tuple(shapes),
        in_specs=[vmem] * len(items),
        out_specs=tuple([vmem] * len(items)),
        scratch_shapes=landings
        + [pltpu.SemaphoreType.DMA((c,)) for c in counts]
        + [pltpu.SemaphoreType.DMA((c,)) for c in counts]
        + totals,
        compiler_params=pltpu.CompilerParams(collective_id=collective, has_side_effects=True),
        cost_estimate=pl.CostEstimate(flops=0, transcendentals=0, bytes_accessed=3 * total),
    )(*[item[0] for item in items])


def window_kernel(blk_sizes, rep_sizes, every, proj_ref, cot_ref, chosen_ref, sent_ref, out_ref, back_ref,
                  p_got, cot_got, ch_got, send_sem, recv_sem, local_sem, acc):
    blk_count = math.prod(blk_sizes)
    span = chosen_ref.shape[0]
    blk_axes, rep_axes = every[: len(blk_sizes)], every[len(blk_sizes) :]
    b = 0
    for a, s in zip(blk_axes, blk_sizes):
        b = b * s + lax.axis_index(a)
    r = 0
    for a, s in zip(rep_axes, rep_sizes):
        r = r * s + lax.axis_index(a)
    far = span * r

    def target(offset):
        rest = (b + offset + blk_count) % blk_count
        coords = []
        for s in reversed(blk_sizes):
            coords.append(rest % s)
            rest = rest // s
        return tuple(reversed(coords)) + tuple(lax.axis_index(a) for a in rep_axes)

    def remote(src, dst, kind, h, t, offset):
        return pltpu.make_async_remote_copy(src, dst, send_sem.at[kind, h, t], recv_sem.at[kind, h, t],
                                            device_id=target(offset), device_id_type=MESH_IDS)

    splits = 8
    half = proj_ref.shape[0] // splits

    def rows(h):
        return pl.ds(h * half, half)

    def relay_moves(h):
        moves = (
            remote(proj_ref.at[rows(h)], p_got.at[0, rows(h)], 0, h, 0, far),
            remote(cot_ref.at[rows(h)], cot_got.at[0, rows(h)], 1, h, 0, -far),
        )
        if h == 0:
            moves += (remote(sent_ref.at[0], ch_got.at[0], 2, 0, 0, -far),)
        return moves

    def local_moves(h):
        moves = (
            pltpu.make_async_copy(proj_ref.at[rows(h)], p_got.at[0, rows(h)], local_sem.at[0, h]),
            pltpu.make_async_copy(cot_ref.at[rows(h)], cot_got.at[0, rows(h)], local_sem.at[1, h]),
        )
        if h == 0:
            moves += (pltpu.make_async_copy(sent_ref.at[0], ch_got.at[0], local_sem.at[2, 0]),)
        return moves

    def chosen_move(t):
        return remote(sent_ref.at[t], ch_got.at[t], 2, 0, t, -far - t)

    def forwards(t, h):
        return (
            remote(p_got.at[0, rows(h)], p_got.at[t, rows(h)], 0, h, t, t),
            remote(cot_got.at[0, rows(h)], cot_got.at[t, rows(h)], 1, h, t, -t),
        )

    barrier = pltpu.get_barrier_semaphore()

    def greet(offset):
        pl.semaphore_signal(barrier, inc=1, device_id=target(offset), device_id_type=MESH_IDS)
        pl.semaphore_signal(barrier, inc=1, device_id=target(-offset), device_id_type=MESH_IDS)

    for t in range(1, span):
        greet(far + t)
        greet(t)

    @pl.when(r != 0)
    def _():
        greet(far)
        greet(far)
        pl.semaphore_wait(barrier, 4 * span)
        for h in range(splits):
            for c in relay_moves(h):
                c.start()

    @pl.when(r == 0)
    def _():
        pl.semaphore_wait(barrier, 4 * span - 4)
        for h in range(splits):
            for c in local_moves(h):
                c.start()

    for t in range(1, span):
        chosen_move(t).start()

    for h in range(splits):

        @pl.when(r != 0)
        def _():
            for c in relay_moves(h):
                c.wait_recv()

        @pl.when(r == 0)
        def _():
            for c in local_moves(h):
                c.wait()

        for t in range(1, span):
            for c in forwards(t, h):
                c.start()

    for t in range(span):
        if t > 0:
            for h in range(splits):
                for c in forwards(t, h):
                    c.wait_recv()
            chosen_move(t).wait_recv()
        part = jnp.dot(chosen_ref[t], p_got[t], preferred_element_type=jnp.float32)
        back = jnp.dot(ch_got[t], cot_got[t], preferred_element_type=jnp.float32)
        if t == 0:
            acc[0] = part
            acc[1] = back
        else:
            acc[0] += part
            acc[1] += back

    width = out_ref.shape[-1]
    for q in range(out_ref.shape[0]):
        columns = pl.ds(q * width, width)
        out_ref[q] = acc[0, :, columns].astype(out_ref.dtype)
        back_ref[q] = acc[1, :, columns].astype(back_ref.dtype)

    @pl.when(r != 0)
    def _():
        for h in range(splits):
            for c in relay_moves(h):
                c.wait_send()

    for t in range(1, span):
        chosen_move(t).wait_send()
        for h in range(splits):
            for c in forwards(t, h):
                c.wait_send()


def window(projected, cotangent, chosen, chosen_t, blk_sizes, rep_sizes, every, collective):
    pieces = math.prod(rep_sizes)
    span = chosen.shape[0]
    rows, width = projected.shape
    vmem = pl.BlockSpec(memory_space=pltpu.VMEM)
    moved = (2 * rows * width * 2 + rows * rows * 2) * span
    return pl.pallas_call(
        functools.partial(window_kernel, blk_sizes, rep_sizes, every),
        out_shape=(
            jax.ShapeDtypeStruct((pieces, rows, width // pieces), jnp.bfloat16),
            jax.ShapeDtypeStruct((pieces, rows, width // pieces), jnp.bfloat16),
        ),
        in_specs=[vmem, vmem, vmem, vmem],
        out_specs=(vmem, vmem),
        scratch_shapes=[
            pltpu.VMEM((span, rows, width), projected.dtype),
            pltpu.VMEM((span, rows, width), cotangent.dtype),
            pltpu.VMEM((span, rows, rows), chosen.dtype),
            pltpu.SemaphoreType.DMA((3, 8, span)),
            pltpu.SemaphoreType.DMA((3, 8, span)),
            pltpu.SemaphoreType.DMA((3, 8)),
            pltpu.VMEM((2, rows, width), jnp.float32),
        ],
        compiler_params=pltpu.CompilerParams(collective_id=collective, has_side_effects=True),
        cost_estimate=pl.CostEstimate(
            flops=4 * span * rows * rows * width, transcendentals=0, bytes_accessed=2 * moved
        ),
    )(projected, cotangent, chosen, chosen_t)


def shards(hidden_pre, adj_vals, adj_cols, w_out, cotangent):
    row_count, feature_width = hidden_pre.shape
    blk_count = lax.axis_size(BLK)
    rep_count = lax.axis_size(REP)
    span = blk_count // rep_count
    blk_pos = lax.axis_index(BLK)
    rep_pos = lax.axis_index(REP)
    cols_here = feature_width // rep_count
    slots = adj_vals.shape[1]

    hidden_act = jnp.maximum(hidden_pre, 0)
    projected = jnp.dot(hidden_act, w_out, preferred_element_type=jnp.float32).astype(jnp.bfloat16)
    own_vals = adj_vals[0]
    own_cols = adj_cols[0]
    section = jnp.mod(blk_pos - own_cols, blk_count) - rep_pos * span

    picks = (section[None, :] == jnp.arange(span, dtype=section.dtype)[:, None]).astype(own_vals.dtype)
    chosen = jnp.einsum("tk,kab->tab", picks, own_vals, preferred_element_type=jnp.float32).astype(own_vals.dtype)
    chosen_t = jnp.einsum("tk,kab->tba", picks, own_vals, preferred_element_type=jnp.float32).astype(own_vals.dtype)
    blk_sizes = tuple(lax.axis_size(a) for a in BLK)
    rep_sizes = tuple(lax.axis_size(a) for a in REP)
    out_sum, back_sum = window(
        projected, cotangent, chosen, chosen_t, blk_sizes, rep_sizes, EVERY, 3
    )

    rows = projected.shape[0]
    out_part, back_grad = exchange_many(
        [(out_sum, REP, "sum", jnp.bfloat16), (back_sum, REP, "sum", jnp.bfloat16)], EVERY, 0
    )
    term = lax.dot_general(
        hidden_act, back_grad, (((0,), (0,)), ((), ())), preferred_element_type=jnp.float32
    )
    grad_weight, back_full = exchange_many(
        [
            (term.reshape(blk_count, -1, cols_here), BLK, "sum", jnp.float32),
            (back_grad, REP, "concat", jnp.bfloat16),
        ],
        EVERY,
        1,
    )
    w_rows = lax.dynamic_slice_in_dim(w_out, rep_pos * cols_here, cols_here, 0)
    grad_in = lax.dot_general(
        back_full, w_rows, (((1,), (1,)), ((), ())), preferred_element_type=jnp.float32
    )
    pre_part = lax.dynamic_slice_in_dim(hidden_pre, rep_pos * cols_here, cols_here, 1)
    grad_pre = jnp.where(pre_part > 0, grad_in, 0.0).astype(jnp.bfloat16)
    return (out_part, grad_weight, grad_pre)


def solution(mesh):
    blk_count, rep_count = mesh.devices.shape
    fine = Mesh(mesh.devices.reshape(8, blk_count // 16, 2, rep_count // 2, 2), EVERY)
    placed = (P(BLK, None), P(BLK, REP, None, None), P(BLK, REP), P(), P(BLK, None))
    return jax.shard_map(
        shards,
        mesh=fine,
        in_specs=placed,
        out_specs=(P(BLK, REP), P(BLK, REP), P(BLK, REP)),
        check_vma=False,
    )
```

```python
import functools
import math

import jax
import jax.numpy as jnp
from jax import lax
from jax.experimental import pallas as pl
from jax.experimental.pallas import tpu as pltpu
from jax.sharding import Mesh
from jax.sharding import PartitionSpec as P

MESH_IDS = pl.DeviceIdType.MESH

BLK = ("by", "bx", "bz")
REP = ("rz", "rc")
EVERY = BLK + REP


def shifted_pairs(blk_count, rep_count, per_rep):
    pairs = []
    for b in range(blk_count):
        for r in range(rep_count):
            pairs.append((b * rep_count + r, ((b + per_rep * r) % blk_count) * rep_count + r))
    return pairs


def ring_pairs(count, steps):
    return [(source, (source + steps) % count) for source in range(count)]


def staged_scatter(value, axes, dim):
    sizes = [lax.axis_size(a) for a in axes]
    full = value.shape[dim]
    rest = full // math.prod(sizes)
    shape = value.shape[:dim] + tuple(sizes) + (rest,) + value.shape[dim + 1 :]
    moved = value.reshape(shape)
    order = list(range(dim)) + [dim + i for i in reversed(range(len(axes)))]
    order += list(range(dim + len(axes), len(shape)))
    moved = jnp.transpose(moved, order).reshape(value.shape)
    for a in reversed(axes):
        moved = lax.psum_scatter(moved, a, scatter_dimension=dim, tiled=True)
    return moved


def exchange_kernel(plans, every, *refs):
    count_of = [math.prod(sizes) for _, sizes, _ in plans]
    n = len(plans)
    srcs, outs = refs[:n], refs[n : 2 * n]
    landed, send_sems, recv_sems = refs[2 * n : 3 * n], refs[3 * n : 4 * n], refs[4 * n : 5 * n]
    totals = refs[5 * n : 6 * n]
    barrier = pltpu.get_barrier_semaphore()

    def position(group, sizes):
        me = 0
        for a, s in zip(group, sizes):
            me = me * s + lax.axis_index(a)
        return me

    def target(group, sizes, d):
        coords = {}
        rest = d
        for a, s in reversed(list(zip(group, sizes))):
            coords[a] = rest % s
            rest = rest // s
        return tuple(coords[a] if a in coords else lax.axis_index(a) for a in every)

    def copy(i, d, slot, o):
        group, sizes, mode = plans[i]
        broadcast = mode == "concat"
        return pltpu.make_async_remote_copy(
            src_ref=srcs[i] if broadcast else srcs[i].at[d],
            dst_ref=landed[i].at[slot],
            send_sem=send_sems[i].at[o],
            recv_sem=recv_sems[i].at[slot],
            device_id=target(group, sizes, d),
            device_id_type=MESH_IDS,
        )

    for i, (group, sizes, _) in enumerate(plans):
        me, count = position(group, sizes), count_of[i]

        def greet(o, carry, group=group, sizes=sizes, me=me, count=count):
            pl.semaphore_signal(barrier, inc=1, device_id=target(group, sizes, (me + o) % count),
                                device_id_type=MESH_IDS)
            return carry

        lax.fori_loop(1, count, greet, 0)
    pl.semaphore_wait(barrier, sum(count_of) - n)

    for i, (group, sizes, mode) in enumerate(plans):
        me, count = position(group, sizes), count_of[i]

        def send(o, carry, i=i, me=me, count=count):
            copy(i, (me + o) % count, me, o).start()
            return carry

        lax.fori_loop(1, count, send, 0)
        if mode == "concat":
            width = srcs[i].shape[-1]
            outs[i][:, pl.ds(pl.multiple_of(me * width, width), width)] = srcs[i][...]
        else:
            totals[i][...] = srcs[i][me].astype(jnp.float32)

    for i, (group, sizes, mode) in enumerate(plans):
        me, count = position(group, sizes), count_of[i]

        def finish(o, carry, i=i, me=me, count=count, mode=mode):
            copy(i, (me + o) % count, me, o).wait_send()
            sender = (me + count - o) % count
            copy(i, sender, sender, o).wait_recv()
            if mode == "concat":
                width = srcs[i].shape[-1]
                outs[i][:, pl.ds(pl.multiple_of(sender * width, width), width)] = landed[i][sender]
            else:
                totals[i][...] += landed[i][sender].astype(jnp.float32)
            return carry

        lax.fori_loop(1, count, finish, 0)
        if mode != "concat":
            outs[i][...] = totals[i][...].astype(outs[i].dtype)


def exchange_many(items, every, collective):
    plans, shapes, landings, totals, counts, total = [], [], [], [], [], 0
    for blocks, group, mode, dtype in items:
        sizes = tuple(lax.axis_size(a) for a in group)
        count = math.prod(sizes)
        if mode == "concat":
            slot_shape = blocks.shape
            shapes.append(jax.ShapeDtypeStruct(blocks.shape[:-1] + (count * blocks.shape[-1],), dtype))
        else:
            slot_shape = blocks.shape[1:]
            shapes.append(jax.ShapeDtypeStruct(slot_shape, dtype))
        plans.append((group, sizes, mode))
        counts.append(count)
        landings.append(pltpu.VMEM((count,) + slot_shape, blocks.dtype))
        totals.append(pltpu.VMEM(slot_shape, jnp.float32))
        total += count * math.prod(slot_shape) * blocks.dtype.itemsize
    vmem = pl.BlockSpec(memory_space=pltpu.VMEM)
    return pl.pallas_call(
        functools.partial(exchange_kernel, tuple(plans), every),
        out_shape=tuple(shapes),
        in_specs=[vmem] * len(items),
        out_specs=tuple([vmem] * len(items)),
        scratch_shapes=landings
        + [pltpu.SemaphoreType.DMA((c,)) for c in counts]
        + [pltpu.SemaphoreType.DMA((c,)) for c in counts]
        + totals,
        compiler_params=pltpu.CompilerParams(collective_id=collective, has_side_effects=True),
        cost_estimate=pl.CostEstimate(flops=0, transcendentals=0, bytes_accessed=3 * total),
    )(*[item[0] for item in items])


def window_kernel(blk_sizes, rep_sizes, every, proj_ref, cot_ref, chosen_ref, sent_ref, out_ref, back_ref,
                  p_got, cot_got, ch_got, send_sem, recv_sem, local_sem, acc):
    blk_count = math.prod(blk_sizes)
    span = chosen_ref.shape[0]
    blk_axes, rep_axes = every[: len(blk_sizes)], every[len(blk_sizes) :]
    b = 0
    for a, s in zip(blk_axes, blk_sizes):
        b = b * s + lax.axis_index(a)
    r = 0
    for a, s in zip(rep_axes, rep_sizes):
        r = r * s + lax.axis_index(a)
    far = span * r

    def target(offset):
        rest = (b + offset + blk_count) % blk_count
        coords = []
        for s in reversed(blk_sizes):
            coords.append(rest % s)
            rest = rest // s
        return tuple(reversed(coords)) + tuple(lax.axis_index(a) for a in rep_axes)

    def remote(src, dst, kind, h, t, offset):
        return pltpu.make_async_remote_copy(src, dst, send_sem.at[kind, h, t], recv_sem.at[kind, h, t],
                                            device_id=target(offset), device_id_type=MESH_IDS)

    splits = 4
    half = proj_ref.shape[0] // splits

    def rows(h):
        return pl.ds(h * half, half)

    def relay_moves(h):
        moves = (
            remote(proj_ref.at[rows(h)], p_got.at[0, rows(h)], 0, h, 0, far),
            remote(cot_ref.at[rows(h)], cot_got.at[0, rows(h)], 1, h, 0, -far),
        )
        if h == 0:
            moves += (remote(sent_ref.at[0], ch_got.at[0], 2, 0, 0, -far),)
        return moves

    def local_moves(h):
        moves = (
            pltpu.make_async_copy(proj_ref.at[rows(h)], p_got.at[0, rows(h)], local_sem.at[0, h]),
            pltpu.make_async_copy(cot_ref.at[rows(h)], cot_got.at[0, rows(h)], local_sem.at[1, h]),
        )
        if h == 0:
            moves += (pltpu.make_async_copy(sent_ref.at[0], ch_got.at[0], local_sem.at[2, 0]),)
        return moves

    def chosen_move(t):
        return remote(sent_ref.at[t], ch_got.at[t], 2, 0, t, -far - t)

    def forwards(t, h):
        return (
            remote(p_got.at[0, rows(h)], p_got.at[t, rows(h)], 0, h, t, t),
            remote(cot_got.at[0, rows(h)], cot_got.at[t, rows(h)], 1, h, t, -t),
        )

    barrier = pltpu.get_barrier_semaphore()

    def greet(offset):
        pl.semaphore_signal(barrier, inc=1, device_id=target(offset), device_id_type=MESH_IDS)
        pl.semaphore_signal(barrier, inc=1, device_id=target(-offset), device_id_type=MESH_IDS)

    for t in range(1, span):
        greet(far + t)
        greet(t)

    @pl.when(r != 0)
    def _():
        greet(far)
        greet(far)
        pl.semaphore_wait(barrier, 4 * span)
        for h in range(splits):
            for c in relay_moves(h):
                c.start()

    @pl.when(r == 0)
    def _():
        pl.semaphore_wait(barrier, 4 * span - 4)
        for h in range(splits):
            for c in local_moves(h):
                c.start()

    for t in range(1, span):
        chosen_move(t).start()

    for h in range(splits):

        @pl.when(r != 0)
        def _():
            for c in relay_moves(h):
                c.wait_recv()

        @pl.when(r == 0)
        def _():
            for c in local_moves(h):
                c.wait()

        for t in range(1, span):
            for c in forwards(t, h):
                c.start()

    for t in range(span):
        if t > 0:
            for h in range(splits):
                for c in forwards(t, h):
                    c.wait_recv()
            chosen_move(t).wait_recv()
        part = jnp.dot(chosen_ref[t], p_got[t], preferred_element_type=jnp.float32)
        back = jnp.dot(ch_got[t], cot_got[t], preferred_element_type=jnp.float32)
        if t == 0:
            acc[0] = part
            acc[1] = back
        else:
            acc[0] += part
            acc[1] += back

    width = out_ref.shape[-1]
    for q in range(out_ref.shape[0]):
        columns = pl.ds(q * width, width)
        out_ref[q] = acc[0, :, columns].astype(out_ref.dtype)
        back_ref[q] = acc[1, :, columns].astype(back_ref.dtype)

    @pl.when(r != 0)
    def _():
        for h in range(splits):
            for c in relay_moves(h):
                c.wait_send()

    for t in range(1, span):
        chosen_move(t).wait_send()
        for h in range(splits):
            for c in forwards(t, h):
                c.wait_send()


def window(projected, cotangent, chosen, chosen_t, blk_sizes, rep_sizes, every, collective):
    pieces = math.prod(rep_sizes)
    span = chosen.shape[0]
    rows, width = projected.shape
    vmem = pl.BlockSpec(memory_space=pltpu.VMEM)
    moved = (2 * rows * width * 2 + rows * rows * 2) * span
    return pl.pallas_call(
        functools.partial(window_kernel, blk_sizes, rep_sizes, every),
        out_shape=(
            jax.ShapeDtypeStruct((pieces, rows, width // pieces), jnp.bfloat16),
            jax.ShapeDtypeStruct((pieces, rows, width // pieces), jnp.bfloat16),
        ),
        in_specs=[vmem, vmem, vmem, vmem],
        out_specs=(vmem, vmem),
        scratch_shapes=[
            pltpu.VMEM((span, rows, width), projected.dtype),
            pltpu.VMEM((span, rows, width), cotangent.dtype),
            pltpu.VMEM((span, rows, rows), chosen.dtype),
            pltpu.SemaphoreType.DMA((3, 4, span)),
            pltpu.SemaphoreType.DMA((3, 4, span)),
            pltpu.SemaphoreType.DMA((3, 4)),
            pltpu.VMEM((2, rows, width), jnp.float32),
        ],
        compiler_params=pltpu.CompilerParams(collective_id=collective, has_side_effects=True),
        cost_estimate=pl.CostEstimate(
            flops=4 * span * rows * rows * width, transcendentals=0, bytes_accessed=2 * moved
        ),
    )(projected, cotangent, chosen, chosen_t)


def tail_kernel(rep_sizes, blk_sizes, every, out_c, back_c, act_t, out_ref, weight_ref, full_ref,
                land_o, land_b, land_w, land_g, bg_s, term_s, tot_o, tot_b, tot_w, sends, recvs):
    rep_axes, blk_axes = every[len(blk_sizes) :], every[: len(blk_sizes)]
    groups = {"rep": (rep_axes, rep_sizes), "blk": (blk_axes, blk_sizes)}
    barrier = pltpu.get_barrier_semaphore()

    def position(name):
        axes, sizes = groups[name]
        me = 0
        for a, s in zip(axes, sizes):
            me = me * s + lax.axis_index(a)
        return me

    def target(name, d):
        axes, sizes = groups[name]
        coords = {}
        rest = d
        for a, s in reversed(list(zip(axes, sizes))):
            coords[a] = rest % s
            rest = rest // s
        return tuple(coords[a] if a in coords else lax.axis_index(a) for a in every)

    def count(name):
        return math.prod(groups[name][1])

    for name in ("rep", "blk"):
        me, n = position(name), count(name)

        def greet(o, carry, name=name, me=me, n=n):
            pl.semaphore_signal(barrier, inc=1, device_id=target(name, (me + o) % n), device_id_type=MESH_IDS)
            return carry

        lax.fori_loop(1, n, greet, 0)
    pl.semaphore_wait(barrier, count("rep") + count("blk") - 2)

    def run(plans):
        for k, name, source, land, total, out in plans:
            me, n = position(name), count(name)

            def send(o, carry, k=k, name=name, source=source, land=land, me=me, n=n):
                d = (me + o) % n
                pltpu.make_async_remote_copy(source(d), land.at[me], sends.at[k, o], recvs.at[k, me],
                                             device_id=target(name, d), device_id_type=MESH_IDS).start()
                return carry

            lax.fori_loop(1, n, send, 0)
            if total is not None:
                total[...] = source(me)[...].astype(jnp.float32)
            else:
                width = land.shape[-1]
                out[:, pl.ds(pl.multiple_of(me * width, width), width)] = source(me)[...]
        for k, name, source, land, total, out in plans:
            me, n = position(name), count(name)

            def finish(o, carry, k=k, name=name, source=source, land=land, total=total, out=out, me=me, n=n):
                d = (me + o) % n
                pltpu.make_async_remote_copy(source(d), land.at[me], sends.at[k, o], recvs.at[k, me],
                                             device_id=target(name, d), device_id_type=MESH_IDS).wait_send()
                sender = (me + n - o) % n
                pltpu.make_async_remote_copy(source(sender), land.at[sender], sends.at[k, o], recvs.at[k, sender],
                                             device_id=target(name, sender), device_id_type=MESH_IDS).wait_recv()
                if total is not None:
                    total[...] += land[sender].astype(jnp.float32)
                else:
                    width = land.shape[-1]
                    out[:, pl.ds(pl.multiple_of(sender * width, width), width)] = land[sender]
                return carry

            lax.fori_loop(1, n, finish, 0)

    run([
        (0, "rep", lambda d: out_c.at[d], land_o, tot_o, None),
        (1, "rep", lambda d: back_c.at[d], land_b, tot_b, None),
    ])
    out_ref[...] = tot_o[...].astype(out_ref.dtype)
    bg_s[...] = tot_b[...].astype(bg_s.dtype)
    term = jnp.dot(act_t[...], bg_s[...], preferred_element_type=jnp.float32)
    term_s[...] = term.reshape(term_s.shape)
    run([
        (2, "blk", lambda d: term_s.at[d], land_w, tot_w, None),
        (3, "rep", lambda d: bg_s, land_g, None, full_ref),
    ])
    weight_ref[...] = tot_w[...]


def tail(out_c, back_c, act_t, blk_sizes, rep_sizes, every, collective):
    reps, blks = math.prod(rep_sizes), math.prod(blk_sizes)
    _, rows, cols = back_c.shape
    vmem = pl.BlockSpec(memory_space=pltpu.VMEM)
    most = max(reps, blks)
    return pl.pallas_call(
        functools.partial(tail_kernel, rep_sizes, blk_sizes, every),
        out_shape=(
            jax.ShapeDtypeStruct((rows, cols), jnp.bfloat16),
            jax.ShapeDtypeStruct((act_t.shape[0] // blks, cols), jnp.float32),
            jax.ShapeDtypeStruct((rows, cols * reps), jnp.bfloat16),
        ),
        in_specs=[vmem, vmem, vmem],
        out_specs=(vmem, vmem, vmem),
        scratch_shapes=[
            pltpu.VMEM((reps, rows, cols), out_c.dtype),
            pltpu.VMEM((reps, rows, cols), back_c.dtype),
            pltpu.VMEM((blks, act_t.shape[0] // blks, cols), jnp.float32),
            pltpu.VMEM((reps, rows, cols), jnp.bfloat16),
            pltpu.VMEM((rows, cols), jnp.bfloat16),
            pltpu.VMEM((blks, act_t.shape[0] // blks, cols), jnp.float32),
            pltpu.VMEM((rows, cols), jnp.float32),
            pltpu.VMEM((rows, cols), jnp.float32),
            pltpu.VMEM((act_t.shape[0] // blks, cols), jnp.float32),
            pltpu.SemaphoreType.DMA((4, most)),
            pltpu.SemaphoreType.DMA((4, most)),
        ],
        compiler_params=pltpu.CompilerParams(collective_id=collective, has_side_effects=True),
        cost_estimate=pl.CostEstimate(
            flops=2 * act_t.shape[0] * rows * cols, transcendentals=0,
            bytes_accessed=3 * (2 * reps * rows * cols * 2 + act_t.shape[0] * cols * 4 + reps * rows * cols * 2),
        ),
    )(out_c, back_c, act_t)


def shards(hidden_pre, adj_vals, adj_cols, w_out, cotangent):
    row_count, feature_width = hidden_pre.shape
    blk_count = lax.axis_size(BLK)
    rep_count = lax.axis_size(REP)
    span = blk_count // rep_count
    blk_pos = lax.axis_index(BLK)
    rep_pos = lax.axis_index(REP)
    cols_here = feature_width // rep_count
    slots = adj_vals.shape[1]

    hidden_act = jnp.maximum(hidden_pre, 0)
    projected = jnp.dot(hidden_act, w_out, preferred_element_type=jnp.float32).astype(jnp.bfloat16)
    own_vals = adj_vals[0]
    own_cols = adj_cols[0]
    section = jnp.mod(blk_pos - own_cols, blk_count) - rep_pos * span

    picks = (section[None, :] == jnp.arange(span, dtype=section.dtype)[:, None]).astype(own_vals.dtype)
    chosen = jnp.einsum("tk,kab->tab", picks, own_vals, preferred_element_type=jnp.float32).astype(own_vals.dtype)
    chosen_t = jnp.einsum("tk,kab->tba", picks, own_vals, preferred_element_type=jnp.float32).astype(own_vals.dtype)
    blk_sizes = tuple(lax.axis_size(a) for a in BLK)
    rep_sizes = tuple(lax.axis_size(a) for a in REP)
    out_sum, back_sum = window(
        projected, cotangent, chosen, chosen_t, blk_sizes, rep_sizes, EVERY, 3
    )

    rows = projected.shape[0]
    out_part, grad_weight, back_full = tail(
        out_sum, back_sum, jnp.transpose(hidden_act), blk_sizes, rep_sizes, EVERY, 0
    )
    w_rows = lax.dynamic_slice_in_dim(w_out, rep_pos * cols_here, cols_here, 0)
    grad_in = lax.dot_general(
        back_full, w_rows, (((1,), (1,)), ((), ())), preferred_element_type=jnp.float32
    )
    pre_part = lax.dynamic_slice_in_dim(hidden_pre, rep_pos * cols_here, cols_here, 1)
    grad_pre = jnp.where(pre_part > 0, grad_in, 0.0).astype(jnp.bfloat16)
    return (out_part, grad_weight, grad_pre)


def solution(mesh):
    blk_count, rep_count = mesh.devices.shape
    fine = Mesh(mesh.devices.reshape(8, blk_count // 16, 2, rep_count // 2, 2), EVERY)
    placed = (P(BLK, None), P(BLK, REP, None, None), P(BLK, REP), P(), P(BLK, None))
    return jax.shard_map(
        shards,
        mesh=fine,
        in_specs=placed,
        out_specs=(P(BLK, REP), P(BLK, REP), P(BLK, REP)),
        check_vma=False,
    )
```

```python
import functools
import math

import jax
import jax.numpy as jnp
from jax import lax
from jax.experimental import pallas as pl
from jax.experimental.pallas import tpu as pltpu
from jax.sharding import Mesh
from jax.sharding import PartitionSpec as P

MESH_IDS = pl.DeviceIdType.MESH

BLK = ("by", "bx", "bz")
REP = ("rz", "rc")
EVERY = BLK + REP


def shifted_pairs(blk_count, rep_count, per_rep):
    pairs = []
    for b in range(blk_count):
        for r in range(rep_count):
            pairs.append((b * rep_count + r, ((b + per_rep * r) % blk_count) * rep_count + r))
    return pairs


def ring_pairs(count, steps):
    return [(source, (source + steps) % count) for source in range(count)]


def staged_scatter(value, axes, dim):
    sizes = [lax.axis_size(a) for a in axes]
    full = value.shape[dim]
    rest = full // math.prod(sizes)
    shape = value.shape[:dim] + tuple(sizes) + (rest,) + value.shape[dim + 1 :]
    moved = value.reshape(shape)
    order = list(range(dim)) + [dim + i for i in reversed(range(len(axes)))]
    order += list(range(dim + len(axes), len(shape)))
    moved = jnp.transpose(moved, order).reshape(value.shape)
    for a in reversed(axes):
        moved = lax.psum_scatter(moved, a, scatter_dimension=dim, tiled=True)
    return moved


def exchange_kernel(plans, every, *refs):
    count_of = [math.prod(sizes) for _, sizes, _ in plans]
    n = len(plans)
    srcs, outs = refs[:n], refs[n : 2 * n]
    landed, send_sems, recv_sems = refs[2 * n : 3 * n], refs[3 * n : 4 * n], refs[4 * n : 5 * n]
    totals = refs[5 * n : 6 * n]
    barrier = pltpu.get_barrier_semaphore()

    def position(group, sizes):
        me = 0
        for a, s in zip(group, sizes):
            me = me * s + lax.axis_index(a)
        return me

    def target(group, sizes, d):
        coords = {}
        rest = d
        for a, s in reversed(list(zip(group, sizes))):
            coords[a] = rest % s
            rest = rest // s
        return tuple(coords[a] if a in coords else lax.axis_index(a) for a in every)

    def copy(i, d, slot, o):
        group, sizes, mode = plans[i]
        broadcast = mode == "concat"
        return pltpu.make_async_remote_copy(
            src_ref=srcs[i] if broadcast else srcs[i].at[d],
            dst_ref=landed[i].at[slot],
            send_sem=send_sems[i].at[o],
            recv_sem=recv_sems[i].at[slot],
            device_id=target(group, sizes, d),
            device_id_type=MESH_IDS,
        )

    for i, (group, sizes, _) in enumerate(plans):
        me, count = position(group, sizes), count_of[i]

        def greet(o, carry, group=group, sizes=sizes, me=me, count=count):
            pl.semaphore_signal(barrier, inc=1, device_id=target(group, sizes, (me + o) % count),
                                device_id_type=MESH_IDS)
            return carry

        lax.fori_loop(1, count, greet, 0)
    pl.semaphore_wait(barrier, sum(count_of) - n)

    for i, (group, sizes, mode) in enumerate(plans):
        me, count = position(group, sizes), count_of[i]

        def send(o, carry, i=i, me=me, count=count):
            copy(i, (me + o) % count, me, o).start()
            return carry

        lax.fori_loop(1, count, send, 0)
        if mode == "concat":
            width = srcs[i].shape[-1]
            outs[i][:, pl.ds(pl.multiple_of(me * width, width), width)] = srcs[i][...]
        else:
            totals[i][...] = srcs[i][me].astype(jnp.float32)

    for i, (group, sizes, mode) in enumerate(plans):
        me, count = position(group, sizes), count_of[i]

        def finish(o, carry, i=i, me=me, count=count, mode=mode):
            copy(i, (me + o) % count, me, o).wait_send()
            sender = (me + count - o) % count
            copy(i, sender, sender, o).wait_recv()
            if mode == "concat":
                width = srcs[i].shape[-1]
                outs[i][:, pl.ds(pl.multiple_of(sender * width, width), width)] = landed[i][sender]
            else:
                totals[i][...] += landed[i][sender].astype(jnp.float32)
            return carry

        lax.fori_loop(1, count, finish, 0)
        if mode != "concat":
            outs[i][...] = totals[i][...].astype(outs[i].dtype)


def exchange_many(items, every, collective):
    plans, shapes, landings, totals, counts, total = [], [], [], [], [], 0
    for blocks, group, mode, dtype in items:
        sizes = tuple(lax.axis_size(a) for a in group)
        count = math.prod(sizes)
        if mode == "concat":
            slot_shape = blocks.shape
            shapes.append(jax.ShapeDtypeStruct(blocks.shape[:-1] + (count * blocks.shape[-1],), dtype))
        else:
            slot_shape = blocks.shape[1:]
            shapes.append(jax.ShapeDtypeStruct(slot_shape, dtype))
        plans.append((group, sizes, mode))
        counts.append(count)
        landings.append(pltpu.VMEM((count,) + slot_shape, blocks.dtype))
        totals.append(pltpu.VMEM(slot_shape, jnp.float32))
        total += count * math.prod(slot_shape) * blocks.dtype.itemsize
    vmem = pl.BlockSpec(memory_space=pltpu.VMEM)
    return pl.pallas_call(
        functools.partial(exchange_kernel, tuple(plans), every),
        out_shape=tuple(shapes),
        in_specs=[vmem] * len(items),
        out_specs=tuple([vmem] * len(items)),
        scratch_shapes=landings
        + [pltpu.SemaphoreType.DMA((c,)) for c in counts]
        + [pltpu.SemaphoreType.DMA((c,)) for c in counts]
        + totals,
        compiler_params=pltpu.CompilerParams(collective_id=collective, has_side_effects=True),
        cost_estimate=pl.CostEstimate(flops=0, transcendentals=0, bytes_accessed=3 * total),
    )(*[item[0] for item in items])


def window_kernel(blk_sizes, rep_sizes, every, proj_ref, cot_ref, chosen_ref, sent_ref, out_ref, back_ref,
                  p_got, cot_got, ch_got, send_sem, recv_sem, local_sem, acc, greeted=False):
    blk_count = math.prod(blk_sizes)
    span = chosen_ref.shape[0]
    blk_axes, rep_axes = every[: len(blk_sizes)], every[len(blk_sizes) :]
    b = 0
    for a, s in zip(blk_axes, blk_sizes):
        b = b * s + lax.axis_index(a)
    r = 0
    for a, s in zip(rep_axes, rep_sizes):
        r = r * s + lax.axis_index(a)
    far = span * r

    def target(offset):
        rest = (b + offset + blk_count) % blk_count
        coords = []
        for s in reversed(blk_sizes):
            coords.append(rest % s)
            rest = rest // s
        return tuple(reversed(coords)) + tuple(lax.axis_index(a) for a in rep_axes)

    def remote(src, dst, kind, h, t, offset):
        return pltpu.make_async_remote_copy(src, dst, send_sem.at[kind, h, t], recv_sem.at[kind, h, t],
                                            device_id=target(offset), device_id_type=MESH_IDS)

    splits = 4
    half = proj_ref.shape[0] // splits

    def rows(h):
        return pl.ds(h * half, half)

    def relay_moves(h):
        moves = (
            remote(proj_ref.at[rows(h)], p_got.at[0, rows(h)], 0, h, 0, far),
            remote(cot_ref.at[rows(h)], cot_got.at[0, rows(h)], 1, h, 0, -far),
        )
        if h == 0:
            moves += (remote(sent_ref.at[0], ch_got.at[0], 2, 0, 0, -far),)
        return moves

    def local_moves(h):
        moves = (
            pltpu.make_async_copy(proj_ref.at[rows(h)], p_got.at[0, rows(h)], local_sem.at[0, h]),
            pltpu.make_async_copy(cot_ref.at[rows(h)], cot_got.at[0, rows(h)], local_sem.at[1, h]),
        )
        if h == 0:
            moves += (pltpu.make_async_copy(sent_ref.at[0], ch_got.at[0], local_sem.at[2, 0]),)
        return moves

    def chosen_move(t):
        return remote(sent_ref.at[t], ch_got.at[t], 2, 0, t, -far - t)

    def forwards(t, h):
        return (
            remote(p_got.at[0, rows(h)], p_got.at[t, rows(h)], 0, h, t, t),
            remote(cot_got.at[0, rows(h)], cot_got.at[t, rows(h)], 1, h, t, -t),
        )

    barrier = pltpu.get_barrier_semaphore()

    def greet(offset):
        pl.semaphore_signal(barrier, inc=1, device_id=target(offset), device_id_type=MESH_IDS)
        pl.semaphore_signal(barrier, inc=1, device_id=target(-offset), device_id_type=MESH_IDS)

    if not greeted:
        for t in range(1, span):
            greet(far + t)
            greet(t)

    @pl.when(r != 0)
    def _():
        if not greeted:
            greet(far)
            greet(far)
            pl.semaphore_wait(barrier, 4 * span)
        for h in range(splits):
            for c in relay_moves(h):
                c.start()

    @pl.when(r == 0)
    def _():
        if not greeted:
            pl.semaphore_wait(barrier, 4 * span - 4)
        for h in range(splits):
            for c in local_moves(h):
                c.start()

    for t in range(1, span):
        chosen_move(t).start()

    for h in range(splits):

        @pl.when(r != 0)
        def _():
            for c in relay_moves(h):
                c.wait_recv()

        @pl.when(r == 0)
        def _():
            for c in local_moves(h):
                c.wait()

        for t in range(1, span):
            for c in forwards(t, h):
                c.start()

    for t in range(span):
        if t > 0:
            for h in range(splits):
                for c in forwards(t, h):
                    c.wait_recv()
            chosen_move(t).wait_recv()
        part = jnp.dot(chosen_ref[t], p_got[t], preferred_element_type=jnp.float32)
        back = jnp.dot(ch_got[t], cot_got[t], preferred_element_type=jnp.float32)
        if t == 0:
            acc[0] = part
            acc[1] = back
        else:
            acc[0] += part
            acc[1] += back

    width = out_ref.shape[-1]
    for q in range(out_ref.shape[0]):
        columns = pl.ds(q * width, width)
        out_ref[q] = acc[0, :, columns].astype(out_ref.dtype)
        back_ref[q] = acc[1, :, columns].astype(back_ref.dtype)

    @pl.when(r != 0)
    def _():
        for h in range(splits):
            for c in relay_moves(h):
                c.wait_send()

    for t in range(1, span):
        chosen_move(t).wait_send()
        for h in range(splits):
            for c in forwards(t, h):
                c.wait_send()


def window(projected, cotangent, chosen, chosen_t, blk_sizes, rep_sizes, every, collective):
    pieces = math.prod(rep_sizes)
    span = chosen.shape[0]
    rows, width = projected.shape
    vmem = pl.BlockSpec(memory_space=pltpu.VMEM)
    moved = (2 * rows * width * 2 + rows * rows * 2) * span
    return pl.pallas_call(
        functools.partial(window_kernel, blk_sizes, rep_sizes, every),
        out_shape=(
            jax.ShapeDtypeStruct((pieces, rows, width // pieces), jnp.bfloat16),
            jax.ShapeDtypeStruct((pieces, rows, width // pieces), jnp.bfloat16),
        ),
        in_specs=[vmem, vmem, vmem, vmem],
        out_specs=(vmem, vmem),
        scratch_shapes=[
            pltpu.VMEM((span, rows, width), projected.dtype),
            pltpu.VMEM((span, rows, width), cotangent.dtype),
            pltpu.VMEM((span, rows, rows), chosen.dtype),
            pltpu.SemaphoreType.DMA((3, 4, span)),
            pltpu.SemaphoreType.DMA((3, 4, span)),
            pltpu.SemaphoreType.DMA((3, 4)),
            pltpu.VMEM((2, rows, width), jnp.float32),
        ],
        compiler_params=pltpu.CompilerParams(collective_id=collective, has_side_effects=True),
        cost_estimate=pl.CostEstimate(
            flops=4 * span * rows * rows * width, transcendentals=0, bytes_accessed=2 * moved
        ),
    )(projected, cotangent, chosen, chosen_t)


def tail_kernel(rep_sizes, blk_sizes, every, out_c, back_c, act_t, out_ref, weight_ref, full_ref,
                land_o, land_b, land_w, land_g, bg_s, term_s, tot_o, tot_b, tot_w, sends, recvs, greeted=False):
    rep_axes, blk_axes = every[len(blk_sizes) :], every[: len(blk_sizes)]
    groups = {"rep": (rep_axes, rep_sizes), "blk": (blk_axes, blk_sizes)}
    barrier = pltpu.get_barrier_semaphore()

    def position(name):
        axes, sizes = groups[name]
        me = 0
        for a, s in zip(axes, sizes):
            me = me * s + lax.axis_index(a)
        return me

    def target(name, d):
        axes, sizes = groups[name]
        coords = {}
        rest = d
        for a, s in reversed(list(zip(axes, sizes))):
            coords[a] = rest % s
            rest = rest // s
        return tuple(coords[a] if a in coords else lax.axis_index(a) for a in every)

    def count(name):
        return math.prod(groups[name][1])

    for name in ("rep", "blk") if not greeted else ():
        me, n = position(name), count(name)

        def greet(o, carry, name=name, me=me, n=n):
            pl.semaphore_signal(barrier, inc=1, device_id=target(name, (me + o) % n), device_id_type=MESH_IDS)
            return carry

        lax.fori_loop(1, n, greet, 0)
    if not greeted:
        pl.semaphore_wait(barrier, count("rep") + count("blk") - 2)

    def run(plans):
        for k, name, source, land, total, out in plans:
            me, n = position(name), count(name)

            def send(o, carry, k=k, name=name, source=source, land=land, me=me, n=n):
                d = (me + o) % n
                pltpu.make_async_remote_copy(source(d), land.at[me], sends.at[k, o], recvs.at[k, me],
                                             device_id=target(name, d), device_id_type=MESH_IDS).start()
                return carry

            lax.fori_loop(1, n, send, 0)
            if total is not None:
                total[...] = source(me)[...].astype(jnp.float32)
            else:
                width = land.shape[-1]
                out[:, pl.ds(pl.multiple_of(me * width, width), width)] = source(me)[...]
        for k, name, source, land, total, out in plans:
            me, n = position(name), count(name)

            def finish(o, carry, k=k, name=name, source=source, land=land, total=total, out=out, me=me, n=n):
                d = (me + o) % n
                pltpu.make_async_remote_copy(source(d), land.at[me], sends.at[k, o], recvs.at[k, me],
                                             device_id=target(name, d), device_id_type=MESH_IDS).wait_send()
                sender = (me + n - o) % n
                pltpu.make_async_remote_copy(source(sender), land.at[sender], sends.at[k, o], recvs.at[k, sender],
                                             device_id=target(name, sender), device_id_type=MESH_IDS).wait_recv()
                if total is not None:
                    total[...] += land[sender].astype(jnp.float32)
                else:
                    width = land.shape[-1]
                    out[:, pl.ds(pl.multiple_of(sender * width, width), width)] = land[sender]
                return carry

            lax.fori_loop(1, n, finish, 0)

    run([
        (0, "rep", lambda d: out_c.at[d], land_o, tot_o, None),
        (1, "rep", lambda d: back_c.at[d], land_b, tot_b, None),
    ])
    out_ref[...] = tot_o[...].astype(out_ref.dtype)
    bg_s[...] = tot_b[...].astype(bg_s.dtype)
    term = jnp.dot(act_t[...], bg_s[...], preferred_element_type=jnp.float32)
    term_s[...] = term.reshape(term_s.shape)
    run([
        (2, "blk", lambda d: term_s.at[d], land_w, tot_w, None),
        (3, "rep", lambda d: bg_s, land_g, None, full_ref),
    ])
    weight_ref[...] = tot_w[...]


def tail(out_c, back_c, act_t, blk_sizes, rep_sizes, every, collective):
    reps, blks = math.prod(rep_sizes), math.prod(blk_sizes)
    _, rows, cols = back_c.shape
    vmem = pl.BlockSpec(memory_space=pltpu.VMEM)
    most = max(reps, blks)
    return pl.pallas_call(
        functools.partial(tail_kernel, rep_sizes, blk_sizes, every),
        out_shape=(
            jax.ShapeDtypeStruct((rows, cols), jnp.bfloat16),
            jax.ShapeDtypeStruct((act_t.shape[0] // blks, cols), jnp.float32),
            jax.ShapeDtypeStruct((rows, cols * reps), jnp.bfloat16),
        ),
        in_specs=[vmem, vmem, vmem],
        out_specs=(vmem, vmem, vmem),
        scratch_shapes=[
            pltpu.VMEM((reps, rows, cols), out_c.dtype),
            pltpu.VMEM((reps, rows, cols), back_c.dtype),
            pltpu.VMEM((blks, act_t.shape[0] // blks, cols), jnp.float32),
            pltpu.VMEM((reps, rows, cols), jnp.bfloat16),
            pltpu.VMEM((rows, cols), jnp.bfloat16),
            pltpu.VMEM((blks, act_t.shape[0] // blks, cols), jnp.float32),
            pltpu.VMEM((rows, cols), jnp.float32),
            pltpu.VMEM((rows, cols), jnp.float32),
            pltpu.VMEM((act_t.shape[0] // blks, cols), jnp.float32),
            pltpu.SemaphoreType.DMA((4, most)),
            pltpu.SemaphoreType.DMA((4, most)),
        ],
        compiler_params=pltpu.CompilerParams(collective_id=collective, has_side_effects=True),
        cost_estimate=pl.CostEstimate(
            flops=2 * act_t.shape[0] * rows * cols, transcendentals=0,
            bytes_accessed=3 * (2 * reps * rows * cols * 2 + act_t.shape[0] * cols * 4 + reps * rows * cols * 2),
        ),
    )(out_c, back_c, act_t)


def fused_kernel(blk_sizes, rep_sizes, every, proj_ref, cot_ref, chosen_ref, sent_ref, act_t, out_ref, weight_ref,
                 full_ref, out_c, back_c, p_got, cot_got, ch_got, send_sem, recv_sem, local_sem, acc, *tail_refs):
    barrier = pltpu.get_barrier_semaphore()
    for axes, sizes in ((every[: len(blk_sizes)], blk_sizes), (every[len(blk_sizes) :], rep_sizes)):
        n = math.prod(sizes)
        me = 0
        for a, s in zip(axes, sizes):
            me = me * s + lax.axis_index(a)

        def greet(o, carry, axes=axes, sizes=sizes, me=me, n=n):
            rest = (me + o) % n
            coords = {}
            for a, s in reversed(list(zip(axes, sizes))):
                coords[a] = rest % s
                rest = rest // s
            device = tuple(coords[a] if a in coords else lax.axis_index(a) for a in every)
            pl.semaphore_signal(barrier, inc=1, device_id=device, device_id_type=MESH_IDS)
            return carry

        lax.fori_loop(1, n, greet, 0)
    pl.semaphore_wait(barrier, math.prod(blk_sizes) + math.prod(rep_sizes) - 2)
    window_kernel(blk_sizes, rep_sizes, every, proj_ref, cot_ref, chosen_ref, sent_ref, out_c, back_c,
                  p_got, cot_got, ch_got, send_sem, recv_sem, local_sem, acc, greeted=True)
    tail_kernel(rep_sizes, blk_sizes, every, out_c, back_c, act_t, out_ref, weight_ref, full_ref, *tail_refs,
                greeted=True)


def fused(projected, cotangent, chosen, chosen_t, act_t, blk_sizes, rep_sizes, every, collective):
    reps, blks = math.prod(rep_sizes), math.prod(blk_sizes)
    span = chosen.shape[0]
    rows, width = projected.shape
    cols = width // reps
    vmem = pl.BlockSpec(memory_space=pltpu.VMEM)
    most = max(reps, blks)
    moved = (2 * rows * width * 2 + rows * rows * 2) * span + 3 * (reps * rows * cols * 6 + act_t.shape[0] * cols * 4)
    return pl.pallas_call(
        functools.partial(fused_kernel, blk_sizes, rep_sizes, every),
        out_shape=(
            jax.ShapeDtypeStruct((rows, cols), jnp.bfloat16),
            jax.ShapeDtypeStruct((act_t.shape[0] // blks, cols), jnp.float32),
            jax.ShapeDtypeStruct((rows, width), jnp.bfloat16),
        ),
        in_specs=[vmem] * 5,
        out_specs=(vmem, vmem, vmem),
        scratch_shapes=[
            pltpu.VMEM((reps, rows, cols), jnp.bfloat16),
            pltpu.VMEM((reps, rows, cols), jnp.bfloat16),
            pltpu.VMEM((span, rows, width), projected.dtype),
            pltpu.VMEM((span, rows, width), cotangent.dtype),
            pltpu.VMEM((span, rows, rows), chosen.dtype),
            pltpu.SemaphoreType.DMA((3, 4, span)),
            pltpu.SemaphoreType.DMA((3, 4, span)),
            pltpu.SemaphoreType.DMA((3, 4)),
            pltpu.VMEM((2, rows, width), jnp.float32),
            pltpu.VMEM((reps, rows, cols), jnp.bfloat16),
            pltpu.VMEM((reps, rows, cols), jnp.bfloat16),
            pltpu.VMEM((blks, act_t.shape[0] // blks, cols), jnp.float32),
            pltpu.VMEM((reps, rows, cols), jnp.bfloat16),
            pltpu.VMEM((rows, cols), jnp.bfloat16),
            pltpu.VMEM((blks, act_t.shape[0] // blks, cols), jnp.float32),
            pltpu.VMEM((rows, cols), jnp.float32),
            pltpu.VMEM((rows, cols), jnp.float32),
            pltpu.VMEM((act_t.shape[0] // blks, cols), jnp.float32),
            pltpu.SemaphoreType.DMA((4, most)),
            pltpu.SemaphoreType.DMA((4, most)),
        ],
        compiler_params=pltpu.CompilerParams(collective_id=collective, has_side_effects=True),
        cost_estimate=pl.CostEstimate(
            flops=4 * span * rows * rows * width + 2 * act_t.shape[0] * rows * cols,
            transcendentals=0,
            bytes_accessed=moved,
        ),
    )(projected, cotangent, chosen, chosen_t, act_t)


def shards(hidden_pre, adj_vals, adj_cols, w_out, cotangent):
    row_count, feature_width = hidden_pre.shape
    blk_count = lax.axis_size(BLK)
    rep_count = lax.axis_size(REP)
    span = blk_count // rep_count
    blk_pos = lax.axis_index(BLK)
    rep_pos = lax.axis_index(REP)
    cols_here = feature_width // rep_count
    slots = adj_vals.shape[1]

    hidden_act = jnp.maximum(hidden_pre, 0)
    projected = jnp.dot(hidden_act, w_out, preferred_element_type=jnp.float32).astype(jnp.bfloat16)
    own_vals = adj_vals[0]
    own_cols = adj_cols[0]
    section = jnp.mod(blk_pos - own_cols, blk_count) - rep_pos * span

    picks = (section[None, :] == jnp.arange(span, dtype=section.dtype)[:, None]).astype(own_vals.dtype)
    chosen = jnp.einsum("tk,kab->tab", picks, own_vals, preferred_element_type=jnp.float32).astype(own_vals.dtype)
    chosen_t = jnp.einsum("tk,kab->tba", picks, own_vals, preferred_element_type=jnp.float32).astype(own_vals.dtype)
    blk_sizes = tuple(lax.axis_size(a) for a in BLK)
    rep_sizes = tuple(lax.axis_size(a) for a in REP)
    out_part, grad_weight, back_full = fused(
        projected, cotangent, chosen, chosen_t, jnp.transpose(hidden_act), blk_sizes, rep_sizes, EVERY, 0
    )
    w_rows = lax.dynamic_slice_in_dim(w_out, rep_pos * cols_here, cols_here, 0)
    grad_in = lax.dot_general(
        back_full, w_rows, (((1,), (1,)), ((), ())), preferred_element_type=jnp.float32
    )
    pre_part = lax.dynamic_slice_in_dim(hidden_pre, rep_pos * cols_here, cols_here, 1)
    grad_pre = jnp.where(pre_part > 0, grad_in, 0.0).astype(jnp.bfloat16)
    return (out_part, grad_weight, grad_pre)


def solution(mesh):
    blk_count, rep_count = mesh.devices.shape
    fine = Mesh(mesh.devices.reshape(8, blk_count // 16, 2, rep_count // 2, 2), EVERY)
    placed = (P(BLK, None), P(BLK, REP, None, None), P(BLK, REP), P(), P(BLK, None))
    return jax.shard_map(
        shards,
        mesh=fine,
        in_specs=placed,
        out_specs=(P(BLK, REP), P(BLK, REP), P(BLK, REP)),
        check_vma=False,
    )
```

```python
import functools
import math

import jax
import jax.numpy as jnp
from jax import lax
from jax.experimental import pallas as pl
from jax.experimental.pallas import tpu as pltpu
from jax.sharding import Mesh
from jax.sharding import PartitionSpec as P

MESH_IDS = pl.DeviceIdType.MESH

BLK = ("by", "bx", "bz")
REP = ("rz", "rc")
EVERY = BLK + REP


def shifted_pairs(blk_count, rep_count, per_rep):
    pairs = []
    for b in range(blk_count):
        for r in range(rep_count):
            pairs.append((b * rep_count + r, ((b + per_rep * r) % blk_count) * rep_count + r))
    return pairs


def ring_pairs(count, steps):
    return [(source, (source + steps) % count) for source in range(count)]


def staged_scatter(value, axes, dim):
    sizes = [lax.axis_size(a) for a in axes]
    full = value.shape[dim]
    rest = full // math.prod(sizes)
    shape = value.shape[:dim] + tuple(sizes) + (rest,) + value.shape[dim + 1 :]
    moved = value.reshape(shape)
    order = list(range(dim)) + [dim + i for i in reversed(range(len(axes)))]
    order += list(range(dim + len(axes), len(shape)))
    moved = jnp.transpose(moved, order).reshape(value.shape)
    for a in reversed(axes):
        moved = lax.psum_scatter(moved, a, scatter_dimension=dim, tiled=True)
    return moved


def exchange_kernel(plans, every, *refs):
    count_of = [math.prod(sizes) for _, sizes, _ in plans]
    n = len(plans)
    srcs, outs = refs[:n], refs[n : 2 * n]
    landed, send_sems, recv_sems = refs[2 * n : 3 * n], refs[3 * n : 4 * n], refs[4 * n : 5 * n]
    totals = refs[5 * n : 6 * n]
    barrier = pltpu.get_barrier_semaphore()

    def position(group, sizes):
        me = 0
        for a, s in zip(group, sizes):
            me = me * s + lax.axis_index(a)
        return me

    def target(group, sizes, d):
        coords = {}
        rest = d
        for a, s in reversed(list(zip(group, sizes))):
            coords[a] = rest % s
            rest = rest // s
        return tuple(coords[a] if a in coords else lax.axis_index(a) for a in every)

    def copy(i, d, slot, o):
        group, sizes, mode = plans[i]
        broadcast = mode == "concat"
        return pltpu.make_async_remote_copy(
            src_ref=srcs[i] if broadcast else srcs[i].at[d],
            dst_ref=landed[i].at[slot],
            send_sem=send_sems[i].at[o],
            recv_sem=recv_sems[i].at[slot],
            device_id=target(group, sizes, d),
            device_id_type=MESH_IDS,
        )

    for i, (group, sizes, _) in enumerate(plans):
        me, count = position(group, sizes), count_of[i]

        def greet(o, carry, group=group, sizes=sizes, me=me, count=count):
            pl.semaphore_signal(barrier, inc=1, device_id=target(group, sizes, (me + o) % count),
                                device_id_type=MESH_IDS)
            return carry

        lax.fori_loop(1, count, greet, 0)
    pl.semaphore_wait(barrier, sum(count_of) - n)

    for i, (group, sizes, mode) in enumerate(plans):
        me, count = position(group, sizes), count_of[i]

        def send(o, carry, i=i, me=me, count=count):
            copy(i, (me + o) % count, me, o).start()
            return carry

        lax.fori_loop(1, count, send, 0)
        if mode == "concat":
            width = srcs[i].shape[-1]
            outs[i][:, pl.ds(pl.multiple_of(me * width, width), width)] = srcs[i][...]
        else:
            totals[i][...] = srcs[i][me].astype(jnp.float32)

    for i, (group, sizes, mode) in enumerate(plans):
        me, count = position(group, sizes), count_of[i]

        def finish(o, carry, i=i, me=me, count=count, mode=mode):
            copy(i, (me + o) % count, me, o).wait_send()
            sender = (me + count - o) % count
            copy(i, sender, sender, o).wait_recv()
            if mode == "concat":
                width = srcs[i].shape[-1]
                outs[i][:, pl.ds(pl.multiple_of(sender * width, width), width)] = landed[i][sender]
            else:
                totals[i][...] += landed[i][sender].astype(jnp.float32)
            return carry

        lax.fori_loop(1, count, finish, 0)
        if mode != "concat":
            outs[i][...] = totals[i][...].astype(outs[i].dtype)


def exchange_many(items, every, collective):
    plans, shapes, landings, totals, counts, total = [], [], [], [], [], 0
    for blocks, group, mode, dtype in items:
        sizes = tuple(lax.axis_size(a) for a in group)
        count = math.prod(sizes)
        if mode == "concat":
            slot_shape = blocks.shape
            shapes.append(jax.ShapeDtypeStruct(blocks.shape[:-1] + (count * blocks.shape[-1],), dtype))
        else:
            slot_shape = blocks.shape[1:]
            shapes.append(jax.ShapeDtypeStruct(slot_shape, dtype))
        plans.append((group, sizes, mode))
        counts.append(count)
        landings.append(pltpu.VMEM((count,) + slot_shape, blocks.dtype))
        totals.append(pltpu.VMEM(slot_shape, jnp.float32))
        total += count * math.prod(slot_shape) * blocks.dtype.itemsize
    vmem = pl.BlockSpec(memory_space=pltpu.VMEM)
    return pl.pallas_call(
        functools.partial(exchange_kernel, tuple(plans), every),
        out_shape=tuple(shapes),
        in_specs=[vmem] * len(items),
        out_specs=tuple([vmem] * len(items)),
        scratch_shapes=landings
        + [pltpu.SemaphoreType.DMA((c,)) for c in counts]
        + [pltpu.SemaphoreType.DMA((c,)) for c in counts]
        + totals,
        compiler_params=pltpu.CompilerParams(collective_id=collective, has_side_effects=True),
        cost_estimate=pl.CostEstimate(flops=0, transcendentals=0, bytes_accessed=3 * total),
    )(*[item[0] for item in items])


def window_kernel(blk_sizes, rep_sizes, every, proj_ref, cot_ref, chosen_ref, sent_ref, out_ref, back_ref,
                  p_got, cot_got, ch_got, send_sem, recv_sem, local_sem, acc, greeted=False):
    blk_count = math.prod(blk_sizes)
    span = chosen_ref.shape[0]
    blk_axes, rep_axes = every[: len(blk_sizes)], every[len(blk_sizes) :]
    b = 0
    for a, s in zip(blk_axes, blk_sizes):
        b = b * s + lax.axis_index(a)
    r = 0
    for a, s in zip(rep_axes, rep_sizes):
        r = r * s + lax.axis_index(a)
    far = span * r

    def target(offset):
        rest = (b + offset + blk_count) % blk_count
        coords = []
        for s in reversed(blk_sizes):
            coords.append(rest % s)
            rest = rest // s
        return tuple(reversed(coords)) + tuple(lax.axis_index(a) for a in rep_axes)

    def remote(src, dst, kind, h, t, offset):
        return pltpu.make_async_remote_copy(src, dst, send_sem.at[kind, h, t], recv_sem.at[kind, h, t],
                                            device_id=target(offset), device_id_type=MESH_IDS)

    splits = 4
    half = proj_ref.shape[0] // splits

    def rows(h):
        return pl.ds(h * half, half)

    def relay_moves(h):
        moves = (
            remote(proj_ref.at[rows(h)], p_got.at[0, rows(h)], 0, h, 0, far),
            remote(cot_ref.at[rows(h)], cot_got.at[0, rows(h)], 1, h, 0, -far),
        )
        if h == 0:
            moves += (remote(sent_ref.at[0], ch_got.at[0], 2, 0, 0, -far),)
        return moves

    def local_moves(h):
        moves = (
            pltpu.make_async_copy(proj_ref.at[rows(h)], p_got.at[0, rows(h)], local_sem.at[0, h]),
            pltpu.make_async_copy(cot_ref.at[rows(h)], cot_got.at[0, rows(h)], local_sem.at[1, h]),
        )
        if h == 0:
            moves += (pltpu.make_async_copy(sent_ref.at[0], ch_got.at[0], local_sem.at[2, 0]),)
        return moves

    def chosen_move(t):
        return remote(sent_ref.at[t], ch_got.at[t], 2, 0, t, -far - t)

    def forwards(t, h):
        return (
            remote(p_got.at[0, rows(h)], p_got.at[t, rows(h)], 0, h, t, t),
            remote(cot_got.at[0, rows(h)], cot_got.at[t, rows(h)], 1, h, t, -t),
        )

    barrier = pltpu.get_barrier_semaphore()

    def greet(offset):
        pl.semaphore_signal(barrier, inc=1, device_id=target(offset), device_id_type=MESH_IDS)
        pl.semaphore_signal(barrier, inc=1, device_id=target(-offset), device_id_type=MESH_IDS)

    if not greeted:
        for t in range(1, span):
            greet(far + t)
            greet(t)

    @pl.when(r != 0)
    def _():
        if not greeted:
            greet(far)
            greet(far)
            pl.semaphore_wait(barrier, 4 * span)
        for h in range(splits):
            for c in relay_moves(h):
                c.start()

    @pl.when(r == 0)
    def _():
        if not greeted:
            pl.semaphore_wait(barrier, 4 * span - 4)
        for h in range(splits):
            for c in local_moves(h):
                c.start()

    for t in range(1, span):
        chosen_move(t).start()

    for h in range(splits):

        @pl.when(r != 0)
        def _():
            for c in relay_moves(h):
                c.wait_recv()

        @pl.when(r == 0)
        def _():
            for c in local_moves(h):
                c.wait()

        for t in range(1, span):
            for c in forwards(t, h):
                c.start()

    for t in range(span):
        if t > 0:
            for h in range(splits):
                for c in forwards(t, h):
                    c.wait_recv()
            chosen_move(t).wait_recv()
        part = jnp.dot(chosen_ref[t], p_got[t], preferred_element_type=jnp.float32)
        back = jnp.dot(ch_got[t], cot_got[t], preferred_element_type=jnp.float32)
        if t == 0:
            acc[0] = part
            acc[1] = back
        else:
            acc[0] += part
            acc[1] += back

    width = out_ref.shape[-1]
    for q in range(out_ref.shape[0]):
        columns = pl.ds(q * width, width)
        out_ref[q] = acc[0, :, columns].astype(out_ref.dtype)
        back_ref[q] = acc[1, :, columns].astype(back_ref.dtype)

    @pl.when(r != 0)
    def _():
        for h in range(splits):
            for c in relay_moves(h):
                c.wait_send()

    for t in range(1, span):
        chosen_move(t).wait_send()
        for h in range(splits):
            for c in forwards(t, h):
                c.wait_send()


def window(projected, cotangent, chosen, chosen_t, blk_sizes, rep_sizes, every, collective):
    pieces = math.prod(rep_sizes)
    span = chosen.shape[0]
    rows, width = projected.shape
    vmem = pl.BlockSpec(memory_space=pltpu.VMEM)
    moved = (2 * rows * width * 2 + rows * rows * 2) * span
    return pl.pallas_call(
        functools.partial(window_kernel, blk_sizes, rep_sizes, every),
        out_shape=(
            jax.ShapeDtypeStruct((pieces, rows, width // pieces), jnp.bfloat16),
            jax.ShapeDtypeStruct((pieces, rows, width // pieces), jnp.bfloat16),
        ),
        in_specs=[vmem, vmem, vmem, vmem],
        out_specs=(vmem, vmem),
        scratch_shapes=[
            pltpu.VMEM((span, rows, width), projected.dtype),
            pltpu.VMEM((span, rows, width), cotangent.dtype),
            pltpu.VMEM((span, rows, rows), chosen.dtype),
            pltpu.SemaphoreType.DMA((3, 4, span)),
            pltpu.SemaphoreType.DMA((3, 4, span)),
            pltpu.SemaphoreType.DMA((3, 4)),
            pltpu.VMEM((2, rows, width), jnp.float32),
        ],
        compiler_params=pltpu.CompilerParams(collective_id=collective, has_side_effects=True),
        cost_estimate=pl.CostEstimate(
            flops=4 * span * rows * rows * width, transcendentals=0, bytes_accessed=2 * moved
        ),
    )(projected, cotangent, chosen, chosen_t)


def tail_kernel(rep_sizes, blk_sizes, every, out_c, back_c, act_t, out_ref, weight_ref, full_ref,
                land_o, land_b, land_w, land_g, bg_s, term_s, tot_o, tot_b, tot_w, sends, recvs, greeted=False):
    rep_axes, blk_axes = every[len(blk_sizes) :], every[: len(blk_sizes)]
    groups = {"rep": (rep_axes, rep_sizes), "blk": (blk_axes, blk_sizes)}
    barrier = pltpu.get_barrier_semaphore()

    def position(name):
        axes, sizes = groups[name]
        me = 0
        for a, s in zip(axes, sizes):
            me = me * s + lax.axis_index(a)
        return me

    def target(name, d):
        axes, sizes = groups[name]
        coords = {}
        rest = d
        for a, s in reversed(list(zip(axes, sizes))):
            coords[a] = rest % s
            rest = rest // s
        return tuple(coords[a] if a in coords else lax.axis_index(a) for a in every)

    def count(name):
        return math.prod(groups[name][1])

    for name in ("rep", "blk") if not greeted else ():
        me, n = position(name), count(name)

        def greet(o, carry, name=name, me=me, n=n):
            pl.semaphore_signal(barrier, inc=1, device_id=target(name, (me + o) % n), device_id_type=MESH_IDS)
            return carry

        lax.fori_loop(1, n, greet, 0)
    if not greeted:
        pl.semaphore_wait(barrier, count("rep") + count("blk") - 2)

    def run(plans):
        for k, name, source, land, total, out in plans:
            me, n = position(name), count(name)

            def send(o, carry, k=k, name=name, source=source, land=land, me=me, n=n):
                d = (me + o) % n
                pltpu.make_async_remote_copy(source(d), land.at[me], sends.at[k, o], recvs.at[k, me],
                                             device_id=target(name, d), device_id_type=MESH_IDS).start()
                return carry

            lax.fori_loop(1, n, send, 0)
            if total is not None:
                total[...] = source(me)[...].astype(jnp.float32)
            else:
                width = land.shape[-1]
                out[:, pl.ds(pl.multiple_of(me * width, width), width)] = source(me)[...]
        for k, name, source, land, total, out in plans:
            me, n = position(name), count(name)

            def finish(o, carry, k=k, name=name, source=source, land=land, total=total, out=out, me=me, n=n):
                d = (me + o) % n
                pltpu.make_async_remote_copy(source(d), land.at[me], sends.at[k, o], recvs.at[k, me],
                                             device_id=target(name, d), device_id_type=MESH_IDS).wait_send()
                sender = (me + n - o) % n
                pltpu.make_async_remote_copy(source(sender), land.at[sender], sends.at[k, o], recvs.at[k, sender],
                                             device_id=target(name, sender), device_id_type=MESH_IDS).wait_recv()
                if total is not None:
                    total[...] += land[sender].astype(jnp.float32)
                else:
                    width = land.shape[-1]
                    out[:, pl.ds(pl.multiple_of(sender * width, width), width)] = land[sender]
                return carry

            lax.fori_loop(1, n, finish, 0)

    run([
        (0, "rep", lambda d: out_c.at[d], land_o, tot_o, None),
        (1, "rep", lambda d: back_c.at[d], land_b, tot_b, None),
    ])
    out_ref[...] = tot_o[...].astype(out_ref.dtype)
    bg_s[...] = tot_b[...].astype(bg_s.dtype)
    term = jnp.dot(act_t[...], bg_s[...], preferred_element_type=jnp.float32)
    term_s[...] = term.reshape(term_s.shape)
    run([
        (2, "blk", lambda d: term_s.at[d], land_w, tot_w, None),
        (3, "rep", lambda d: bg_s, land_g, None, full_ref),
    ])
    weight_ref[...] = tot_w[...]


def tail(out_c, back_c, act_t, blk_sizes, rep_sizes, every, collective):
    reps, blks = math.prod(rep_sizes), math.prod(blk_sizes)
    _, rows, cols = back_c.shape
    vmem = pl.BlockSpec(memory_space=pltpu.VMEM)
    most = max(reps, blks)
    return pl.pallas_call(
        functools.partial(tail_kernel, rep_sizes, blk_sizes, every),
        out_shape=(
            jax.ShapeDtypeStruct((rows, cols), jnp.bfloat16),
            jax.ShapeDtypeStruct((act_t.shape[0] // blks, cols), jnp.float32),
            jax.ShapeDtypeStruct((rows, cols * reps), jnp.bfloat16),
        ),
        in_specs=[vmem, vmem, vmem],
        out_specs=(vmem, vmem, vmem),
        scratch_shapes=[
            pltpu.VMEM((reps, rows, cols), out_c.dtype),
            pltpu.VMEM((reps, rows, cols), back_c.dtype),
            pltpu.VMEM((blks, act_t.shape[0] // blks, cols), jnp.float32),
            pltpu.VMEM((reps, rows, cols), jnp.bfloat16),
            pltpu.VMEM((rows, cols), jnp.bfloat16),
            pltpu.VMEM((blks, act_t.shape[0] // blks, cols), jnp.float32),
            pltpu.VMEM((rows, cols), jnp.float32),
            pltpu.VMEM((rows, cols), jnp.float32),
            pltpu.VMEM((act_t.shape[0] // blks, cols), jnp.float32),
            pltpu.SemaphoreType.DMA((4, most)),
            pltpu.SemaphoreType.DMA((4, most)),
        ],
        compiler_params=pltpu.CompilerParams(collective_id=collective, has_side_effects=True),
        cost_estimate=pl.CostEstimate(
            flops=2 * act_t.shape[0] * rows * cols, transcendentals=0,
            bytes_accessed=3 * (2 * reps * rows * cols * 2 + act_t.shape[0] * cols * 4 + reps * rows * cols * 2),
        ),
    )(out_c, back_c, act_t)


def fused_kernel(blk_sizes, rep_sizes, every, proj_ref, cot_ref, chosen_ref, sent_ref, act_t, out_ref, weight_ref,
                 full_ref, out_c, back_c, p_got, cot_got, ch_got, send_sem, recv_sem, local_sem, acc, *tail_refs):
    barrier = pltpu.get_barrier_semaphore()
    for axes, sizes in ((every[: len(blk_sizes)], blk_sizes), (every[len(blk_sizes) :], rep_sizes)):
        n = math.prod(sizes)
        me = 0
        for a, s in zip(axes, sizes):
            me = me * s + lax.axis_index(a)

        def greet(o, carry, axes=axes, sizes=sizes, me=me, n=n):
            rest = (me + o) % n
            coords = {}
            for a, s in reversed(list(zip(axes, sizes))):
                coords[a] = rest % s
                rest = rest // s
            device = tuple(coords[a] if a in coords else lax.axis_index(a) for a in every)
            pl.semaphore_signal(barrier, inc=1, device_id=device, device_id_type=MESH_IDS)
            return carry

        lax.fori_loop(1, n, greet, 0)
    pl.semaphore_wait(barrier, math.prod(blk_sizes) + math.prod(rep_sizes) - 2)
    window_kernel(blk_sizes, rep_sizes, every, proj_ref, cot_ref, chosen_ref, sent_ref, out_c, back_c,
                  p_got, cot_got, ch_got, send_sem, recv_sem, local_sem, acc, greeted=True)
    tail_kernel(rep_sizes, blk_sizes, every, out_c, back_c, act_t, out_ref, weight_ref, full_ref, *tail_refs,
                greeted=True)


def fused(projected, cotangent, chosen, chosen_t, act_t, blk_sizes, rep_sizes, every, collective):
    reps, blks = math.prod(rep_sizes), math.prod(blk_sizes)
    span = chosen.shape[0]
    rows, width = projected.shape
    cols = width // reps
    vmem = pl.BlockSpec(memory_space=pltpu.VMEM)
    most = max(reps, blks)
    moved = (2 * rows * width * 2 + rows * rows * 2) * span + 3 * (reps * rows * cols * 6 + act_t.shape[0] * cols * 4)
    return pl.pallas_call(
        functools.partial(fused_kernel, blk_sizes, rep_sizes, every),
        out_shape=(
            jax.ShapeDtypeStruct((rows, cols), jnp.bfloat16),
            jax.ShapeDtypeStruct((act_t.shape[0] // blks, cols), jnp.float32),
            jax.ShapeDtypeStruct((rows, width), jnp.bfloat16),
        ),
        in_specs=[vmem] * 5,
        out_specs=(vmem, vmem, vmem),
        scratch_shapes=[
            pltpu.VMEM((reps, rows, cols), jnp.bfloat16),
            pltpu.VMEM((reps, rows, cols), jnp.bfloat16),
            pltpu.VMEM((span, rows, width), projected.dtype),
            pltpu.VMEM((span, rows, width), cotangent.dtype),
            pltpu.VMEM((span, rows, rows), chosen.dtype),
            pltpu.SemaphoreType.DMA((3, 4, span)),
            pltpu.SemaphoreType.DMA((3, 4, span)),
            pltpu.SemaphoreType.DMA((3, 4)),
            pltpu.VMEM((2, rows, width), jnp.float32),
            pltpu.VMEM((reps, rows, cols), jnp.bfloat16),
            pltpu.VMEM((reps, rows, cols), jnp.bfloat16),
            pltpu.VMEM((blks, act_t.shape[0] // blks, cols), jnp.float32),
            pltpu.VMEM((reps, rows, cols), jnp.bfloat16),
            pltpu.VMEM((rows, cols), jnp.bfloat16),
            pltpu.VMEM((blks, act_t.shape[0] // blks, cols), jnp.float32),
            pltpu.VMEM((rows, cols), jnp.float32),
            pltpu.VMEM((rows, cols), jnp.float32),
            pltpu.VMEM((act_t.shape[0] // blks, cols), jnp.float32),
            pltpu.SemaphoreType.DMA((4, most)),
            pltpu.SemaphoreType.DMA((4, most)),
        ],
        compiler_params=pltpu.CompilerParams(collective_id=collective, has_side_effects=True),
        cost_estimate=pl.CostEstimate(
            flops=4 * span * rows * rows * width + 2 * act_t.shape[0] * rows * cols,
            transcendentals=0,
            bytes_accessed=moved,
        ),
    )(projected, cotangent, chosen, chosen_t, act_t)


def shards(hidden_pre, adj_vals, adj_cols, w_out, cotangent):
    row_count, feature_width = hidden_pre.shape
    blk_count = lax.axis_size(BLK)
    rep_count = lax.axis_size(REP)
    span = blk_count // rep_count
    blk_pos = lax.axis_index(BLK)
    rep_pos = lax.axis_index(REP)
    cols_here = feature_width // rep_count
    slots = adj_vals.shape[1]

    hidden_act = jnp.maximum(hidden_pre, 0)
    projected = jnp.dot(hidden_act, w_out, preferred_element_type=jnp.float32).astype(jnp.bfloat16)
    own_vals = adj_vals[0]
    own_cols = adj_cols[0]
    section = jnp.mod(blk_pos - own_cols, blk_count) - rep_pos * span

    picks = (section[None, :] == jnp.arange(span, dtype=section.dtype)[:, None]).astype(own_vals.dtype)
    flipped = jnp.swapaxes(own_vals, 1, 2)
    chosen = sum(picks[:, k, None, None] * own_vals[k][None] for k in range(slots))
    chosen_t = sum(picks[:, k, None, None] * flipped[k][None] for k in range(slots))
    blk_sizes = tuple(lax.axis_size(a) for a in BLK)
    rep_sizes = tuple(lax.axis_size(a) for a in REP)
    out_part, grad_weight, back_full = fused(
        projected, cotangent, chosen, chosen_t, jnp.transpose(hidden_act), blk_sizes, rep_sizes, EVERY, 0
    )
    w_rows = lax.dynamic_slice_in_dim(w_out, rep_pos * cols_here, cols_here, 0)
    grad_in = lax.dot_general(
        back_full, w_rows, (((1,), (1,)), ((), ())), preferred_element_type=jnp.float32
    )
    pre_part = lax.dynamic_slice_in_dim(hidden_pre, rep_pos * cols_here, cols_here, 1)
    grad_pre = jnp.where(pre_part > 0, grad_in, 0.0).astype(jnp.bfloat16)
    return (out_part, grad_weight, grad_pre)


def solution(mesh):
    blk_count, rep_count = mesh.devices.shape
    fine = Mesh(mesh.devices.reshape(8, blk_count // 16, 2, rep_count // 2, 2), EVERY)
    placed = (P(BLK, None), P(BLK, REP, None, None), P(BLK, REP), P(), P(BLK, None))
    return jax.shard_map(
        shards,
        mesh=fine,
        in_specs=placed,
        out_specs=(P(BLK, REP), P(BLK, REP), P(BLK, REP)),
        check_vma=False,
    )
```

```python
import functools
import math

import jax
import jax.numpy as jnp
from jax import lax
from jax.experimental import pallas as pl
from jax.experimental.pallas import tpu as pltpu
from jax.sharding import Mesh
from jax.sharding import PartitionSpec as P

MESH_IDS = pl.DeviceIdType.MESH

BLK = ("by", "bx", "bz")
REP = ("rz", "rc")
EVERY = BLK + REP


def shifted_pairs(blk_count, rep_count, per_rep):
    pairs = []
    for b in range(blk_count):
        for r in range(rep_count):
            pairs.append((b * rep_count + r, ((b + per_rep * r) % blk_count) * rep_count + r))
    return pairs


def ring_pairs(count, steps):
    return [(source, (source + steps) % count) for source in range(count)]


def staged_scatter(value, axes, dim):
    sizes = [lax.axis_size(a) for a in axes]
    full = value.shape[dim]
    rest = full // math.prod(sizes)
    shape = value.shape[:dim] + tuple(sizes) + (rest,) + value.shape[dim + 1 :]
    moved = value.reshape(shape)
    order = list(range(dim)) + [dim + i for i in reversed(range(len(axes)))]
    order += list(range(dim + len(axes), len(shape)))
    moved = jnp.transpose(moved, order).reshape(value.shape)
    for a in reversed(axes):
        moved = lax.psum_scatter(moved, a, scatter_dimension=dim, tiled=True)
    return moved


def exchange_kernel(plans, every, *refs):
    count_of = [math.prod(sizes) for _, sizes, _ in plans]
    n = len(plans)
    srcs, outs = refs[:n], refs[n : 2 * n]
    landed, send_sems, recv_sems = refs[2 * n : 3 * n], refs[3 * n : 4 * n], refs[4 * n : 5 * n]
    totals = refs[5 * n : 6 * n]
    barrier = pltpu.get_barrier_semaphore()

    def position(group, sizes):
        me = 0
        for a, s in zip(group, sizes):
            me = me * s + lax.axis_index(a)
        return me

    def target(group, sizes, d):
        coords = {}
        rest = d
        for a, s in reversed(list(zip(group, sizes))):
            coords[a] = rest % s
            rest = rest // s
        return tuple(coords[a] if a in coords else lax.axis_index(a) for a in every)

    def copy(i, d, slot, o):
        group, sizes, mode = plans[i]
        broadcast = mode == "concat"
        return pltpu.make_async_remote_copy(
            src_ref=srcs[i] if broadcast else srcs[i].at[d],
            dst_ref=landed[i].at[slot],
            send_sem=send_sems[i].at[o],
            recv_sem=recv_sems[i].at[slot],
            device_id=target(group, sizes, d),
            device_id_type=MESH_IDS,
        )

    for i, (group, sizes, _) in enumerate(plans):
        me, count = position(group, sizes), count_of[i]

        def greet(o, carry, group=group, sizes=sizes, me=me, count=count):
            pl.semaphore_signal(barrier, inc=1, device_id=target(group, sizes, (me + o) % count),
                                device_id_type=MESH_IDS)
            return carry

        lax.fori_loop(1, count, greet, 0)
    pl.semaphore_wait(barrier, sum(count_of) - n)

    for i, (group, sizes, mode) in enumerate(plans):
        me, count = position(group, sizes), count_of[i]

        def send(o, carry, i=i, me=me, count=count):
            copy(i, (me + o) % count, me, o).start()
            return carry

        lax.fori_loop(1, count, send, 0)
        if mode == "concat":
            width = srcs[i].shape[-1]
            outs[i][:, pl.ds(pl.multiple_of(me * width, width), width)] = srcs[i][...]
        else:
            totals[i][...] = srcs[i][me].astype(jnp.float32)

    for i, (group, sizes, mode) in enumerate(plans):
        me, count = position(group, sizes), count_of[i]

        def finish(o, carry, i=i, me=me, count=count, mode=mode):
            copy(i, (me + o) % count, me, o).wait_send()
            sender = (me + count - o) % count
            copy(i, sender, sender, o).wait_recv()
            if mode == "concat":
                width = srcs[i].shape[-1]
                outs[i][:, pl.ds(pl.multiple_of(sender * width, width), width)] = landed[i][sender]
            else:
                totals[i][...] += landed[i][sender].astype(jnp.float32)
            return carry

        lax.fori_loop(1, count, finish, 0)
        if mode != "concat":
            outs[i][...] = totals[i][...].astype(outs[i].dtype)


def exchange_many(items, every, collective):
    plans, shapes, landings, totals, counts, total = [], [], [], [], [], 0
    for blocks, group, mode, dtype in items:
        sizes = tuple(lax.axis_size(a) for a in group)
        count = math.prod(sizes)
        if mode == "concat":
            slot_shape = blocks.shape
            shapes.append(jax.ShapeDtypeStruct(blocks.shape[:-1] + (count * blocks.shape[-1],), dtype))
        else:
            slot_shape = blocks.shape[1:]
            shapes.append(jax.ShapeDtypeStruct(slot_shape, dtype))
        plans.append((group, sizes, mode))
        counts.append(count)
        landings.append(pltpu.VMEM((count,) + slot_shape, blocks.dtype))
        totals.append(pltpu.VMEM(slot_shape, jnp.float32))
        total += count * math.prod(slot_shape) * blocks.dtype.itemsize
    vmem = pl.BlockSpec(memory_space=pltpu.VMEM)
    return pl.pallas_call(
        functools.partial(exchange_kernel, tuple(plans), every),
        out_shape=tuple(shapes),
        in_specs=[vmem] * len(items),
        out_specs=tuple([vmem] * len(items)),
        scratch_shapes=landings
        + [pltpu.SemaphoreType.DMA((c,)) for c in counts]
        + [pltpu.SemaphoreType.DMA((c,)) for c in counts]
        + totals,
        compiler_params=pltpu.CompilerParams(collective_id=collective, has_side_effects=True),
        cost_estimate=pl.CostEstimate(flops=0, transcendentals=0, bytes_accessed=3 * total),
    )(*[item[0] for item in items])


def window_kernel(blk_sizes, rep_sizes, every, proj_ref, cot_ref, chosen_ref, sent_ref, out_ref, back_ref,
                  p_got, cot_got, ch_got, send_sem, recv_sem, local_sem, acc, greeted=False):
    blk_count = math.prod(blk_sizes)
    span = chosen_ref.shape[0]
    blk_axes, rep_axes = every[: len(blk_sizes)], every[len(blk_sizes) :]
    b = 0
    for a, s in zip(blk_axes, blk_sizes):
        b = b * s + lax.axis_index(a)
    r = 0
    for a, s in zip(rep_axes, rep_sizes):
        r = r * s + lax.axis_index(a)
    far = span * r

    def target(offset):
        rest = (b + offset + blk_count) % blk_count
        coords = []
        for s in reversed(blk_sizes):
            coords.append(rest % s)
            rest = rest // s
        return tuple(reversed(coords)) + tuple(lax.axis_index(a) for a in rep_axes)

    def remote(src, dst, kind, h, t, offset):
        return pltpu.make_async_remote_copy(src, dst, send_sem.at[kind, h, t], recv_sem.at[kind, h, t],
                                            device_id=target(offset), device_id_type=MESH_IDS)

    splits = 4
    half = proj_ref.shape[0] // splits

    def rows(h):
        return pl.ds(h * half, half)

    def relay_moves(h):
        moves = (
            remote(proj_ref.at[rows(h)], p_got.at[0, rows(h)], 0, h, 0, far),
            remote(cot_ref.at[rows(h)], cot_got.at[0, rows(h)], 1, h, 0, -far),
        )
        if h == 0:
            moves += (remote(sent_ref.at[0], ch_got.at[0], 2, 0, 0, -far),)
        return moves

    def local_moves(h):
        moves = (
            pltpu.make_async_copy(proj_ref.at[rows(h)], p_got.at[0, rows(h)], local_sem.at[0, h]),
            pltpu.make_async_copy(cot_ref.at[rows(h)], cot_got.at[0, rows(h)], local_sem.at[1, h]),
        )
        if h == 0:
            moves += (pltpu.make_async_copy(sent_ref.at[0], ch_got.at[0], local_sem.at[2, 0]),)
        return moves

    def chosen_move(t):
        return remote(sent_ref.at[t], ch_got.at[t], 2, 0, t, -far - t)

    def forwards(t, h):
        return (
            remote(p_got.at[0, rows(h)], p_got.at[t, rows(h)], 0, h, t, t),
            remote(cot_got.at[0, rows(h)], cot_got.at[t, rows(h)], 1, h, t, -t),
        )

    barrier = pltpu.get_barrier_semaphore()

    def greet(offset):
        pl.semaphore_signal(barrier, inc=1, device_id=target(offset), device_id_type=MESH_IDS)
        pl.semaphore_signal(barrier, inc=1, device_id=target(-offset), device_id_type=MESH_IDS)

    if not greeted:
        for t in range(1, span):
            greet(far + t)
            greet(t)

    @pl.when(r != 0)
    def _():
        if not greeted:
            greet(far)
            greet(far)
            pl.semaphore_wait(barrier, 4 * span)
        for h in range(splits):
            for c in relay_moves(h):
                c.start()

    @pl.when(r == 0)
    def _():
        if not greeted:
            pl.semaphore_wait(barrier, 4 * span - 4)
        for h in range(splits):
            for c in local_moves(h):
                c.start()

    for t in range(1, span):
        chosen_move(t).start()

    for h in range(splits):

        @pl.when(r != 0)
        def _():
            for c in relay_moves(h):
                c.wait_recv()

        @pl.when(r == 0)
        def _():
            for c in local_moves(h):
                c.wait()

        for t in range(1, span):
            for c in forwards(t, h):
                c.start()

    for t in range(span):
        if t > 0:
            for h in range(splits):
                for c in forwards(t, h):
                    c.wait_recv()
            chosen_move(t).wait_recv()
        part = jnp.dot(chosen_ref[t], p_got[t], preferred_element_type=jnp.float32)
        back = jnp.dot(ch_got[t], cot_got[t], preferred_element_type=jnp.float32)
        if t == 0:
            acc[0] = part
            acc[1] = back
        else:
            acc[0] += part
            acc[1] += back

    width = out_ref.shape[-1]
    for q in range(out_ref.shape[0]):
        columns = pl.ds(q * width, width)
        out_ref[q] = acc[0, :, columns].astype(out_ref.dtype)
        back_ref[q] = acc[1, :, columns].astype(back_ref.dtype)

    @pl.when(r != 0)
    def _():
        for h in range(splits):
            for c in relay_moves(h):
                c.wait_send()

    for t in range(1, span):
        chosen_move(t).wait_send()
        for h in range(splits):
            for c in forwards(t, h):
                c.wait_send()


def window(projected, cotangent, chosen, chosen_t, blk_sizes, rep_sizes, every, collective):
    pieces = math.prod(rep_sizes)
    span = chosen.shape[0]
    rows, width = projected.shape
    vmem = pl.BlockSpec(memory_space=pltpu.VMEM)
    moved = (2 * rows * width * 2 + rows * rows * 2) * span
    return pl.pallas_call(
        functools.partial(window_kernel, blk_sizes, rep_sizes, every),
        out_shape=(
            jax.ShapeDtypeStruct((pieces, rows, width // pieces), jnp.bfloat16),
            jax.ShapeDtypeStruct((pieces, rows, width // pieces), jnp.bfloat16),
        ),
        in_specs=[vmem, vmem, vmem, vmem],
        out_specs=(vmem, vmem),
        scratch_shapes=[
            pltpu.VMEM((span, rows, width), projected.dtype),
            pltpu.VMEM((span, rows, width), cotangent.dtype),
            pltpu.VMEM((span, rows, rows), chosen.dtype),
            pltpu.SemaphoreType.DMA((3, 4, span)),
            pltpu.SemaphoreType.DMA((3, 4, span)),
            pltpu.SemaphoreType.DMA((3, 4)),
            pltpu.VMEM((2, rows, width), jnp.float32),
        ],
        compiler_params=pltpu.CompilerParams(collective_id=collective, has_side_effects=True),
        cost_estimate=pl.CostEstimate(
            flops=4 * span * rows * rows * width, transcendentals=0, bytes_accessed=2 * moved
        ),
    )(projected, cotangent, chosen, chosen_t)


def tail_kernel(rep_sizes, blk_sizes, every, out_c, back_c, act_t, out_ref, weight_ref, full_ref,
                land_o, land_b, land_w, land_g, bg_s, term_s, tot_o, tot_b, tot_w, sends, recvs, greeted=False):
    rep_axes, blk_axes = every[len(blk_sizes) :], every[: len(blk_sizes)]
    groups = {"rep": (rep_axes, rep_sizes), "blk": (blk_axes, blk_sizes)}
    barrier = pltpu.get_barrier_semaphore()

    def position(name):
        axes, sizes = groups[name]
        me = 0
        for a, s in zip(axes, sizes):
            me = me * s + lax.axis_index(a)
        return me

    def target(name, d):
        axes, sizes = groups[name]
        coords = {}
        rest = d
        for a, s in reversed(list(zip(axes, sizes))):
            coords[a] = rest % s
            rest = rest // s
        return tuple(coords[a] if a in coords else lax.axis_index(a) for a in every)

    def count(name):
        return math.prod(groups[name][1])

    for name in ("rep", "blk") if not greeted else ():
        me, n = position(name), count(name)

        def greet(o, carry, name=name, me=me, n=n):
            pl.semaphore_signal(barrier, inc=1, device_id=target(name, (me + o) % n), device_id_type=MESH_IDS)
            return carry

        lax.fori_loop(1, n, greet, 0)
    if not greeted:
        pl.semaphore_wait(barrier, count("rep") + count("blk") - 2)

    def run(plans):
        for k, name, source, land, total, out in plans:
            me, n = position(name), count(name)

            def send(o, carry, k=k, name=name, source=source, land=land, me=me, n=n):
                d = (me + o) % n
                pltpu.make_async_remote_copy(source(d), land.at[me], sends.at[k, o], recvs.at[k, me],
                                             device_id=target(name, d), device_id_type=MESH_IDS).start()
                return carry

            lax.fori_loop(1, n, send, 0)
            if total is not None:
                total[...] = source(me)[...].astype(jnp.float32)
            else:
                width = land.shape[-1]
                out[:, pl.ds(pl.multiple_of(me * width, width), width)] = source(me)[...]
        for k, name, source, land, total, out in plans:
            me, n = position(name), count(name)

            def finish(o, carry, k=k, name=name, source=source, land=land, total=total, out=out, me=me, n=n):
                d = (me + o) % n
                pltpu.make_async_remote_copy(source(d), land.at[me], sends.at[k, o], recvs.at[k, me],
                                             device_id=target(name, d), device_id_type=MESH_IDS).wait_send()
                sender = (me + n - o) % n
                pltpu.make_async_remote_copy(source(sender), land.at[sender], sends.at[k, o], recvs.at[k, sender],
                                             device_id=target(name, sender), device_id_type=MESH_IDS).wait_recv()
                if total is not None:
                    total[...] += land[sender].astype(jnp.float32)
                else:
                    width = land.shape[-1]
                    out[:, pl.ds(pl.multiple_of(sender * width, width), width)] = land[sender]
                return carry

            lax.fori_loop(1, n, finish, 0)

    run([
        (0, "rep", lambda d: out_c.at[d], land_o, tot_o, None),
        (1, "rep", lambda d: back_c.at[d], land_b, tot_b, None),
    ])
    out_ref[...] = tot_o[...].astype(out_ref.dtype)
    bg_s[...] = tot_b[...].astype(bg_s.dtype)
    term = lax.dot_general(act_t[...], bg_s[...], (((0,), (0,)), ((), ())), preferred_element_type=jnp.float32)
    term_s[...] = term.reshape(term_s.shape)
    run([
        (2, "blk", lambda d: term_s.at[d], land_w, tot_w, None),
        (3, "rep", lambda d: bg_s, land_g, None, full_ref),
    ])
    weight_ref[...] = tot_w[...]


def tail(out_c, back_c, act_t, blk_sizes, rep_sizes, every, collective):
    reps, blks = math.prod(rep_sizes), math.prod(blk_sizes)
    _, rows, cols = back_c.shape
    vmem = pl.BlockSpec(memory_space=pltpu.VMEM)
    most = max(reps, blks)
    return pl.pallas_call(
        functools.partial(tail_kernel, rep_sizes, blk_sizes, every),
        out_shape=(
            jax.ShapeDtypeStruct((rows, cols), jnp.bfloat16),
            jax.ShapeDtypeStruct((act_t.shape[0] // blks, cols), jnp.float32),
            jax.ShapeDtypeStruct((rows, cols * reps), jnp.bfloat16),
        ),
        in_specs=[vmem, vmem, vmem],
        out_specs=(vmem, vmem, vmem),
        scratch_shapes=[
            pltpu.VMEM((reps, rows, cols), out_c.dtype),
            pltpu.VMEM((reps, rows, cols), back_c.dtype),
            pltpu.VMEM((blks, act_t.shape[0] // blks, cols), jnp.float32),
            pltpu.VMEM((reps, rows, cols), jnp.bfloat16),
            pltpu.VMEM((rows, cols), jnp.bfloat16),
            pltpu.VMEM((blks, act_t.shape[0] // blks, cols), jnp.float32),
            pltpu.VMEM((rows, cols), jnp.float32),
            pltpu.VMEM((rows, cols), jnp.float32),
            pltpu.VMEM((act_t.shape[0] // blks, cols), jnp.float32),
            pltpu.SemaphoreType.DMA((4, most)),
            pltpu.SemaphoreType.DMA((4, most)),
        ],
        compiler_params=pltpu.CompilerParams(collective_id=collective, has_side_effects=True),
        cost_estimate=pl.CostEstimate(
            flops=2 * act_t.shape[0] * rows * cols, transcendentals=0,
            bytes_accessed=3 * (2 * reps * rows * cols * 2 + act_t.shape[0] * cols * 4 + reps * rows * cols * 2),
        ),
    )(out_c, back_c, act_t)


def fused_kernel(blk_sizes, rep_sizes, every, proj_ref, cot_ref, chosen_ref, sent_ref, act_t, out_ref, weight_ref,
                 full_ref, out_c, back_c, p_got, cot_got, ch_got, send_sem, recv_sem, local_sem, acc, *tail_refs):
    barrier = pltpu.get_barrier_semaphore()
    for axes, sizes in ((every[: len(blk_sizes)], blk_sizes), (every[len(blk_sizes) :], rep_sizes)):
        n = math.prod(sizes)
        me = 0
        for a, s in zip(axes, sizes):
            me = me * s + lax.axis_index(a)

        def greet(o, carry, axes=axes, sizes=sizes, me=me, n=n):
            rest = (me + o) % n
            coords = {}
            for a, s in reversed(list(zip(axes, sizes))):
                coords[a] = rest % s
                rest = rest // s
            device = tuple(coords[a] if a in coords else lax.axis_index(a) for a in every)
            pl.semaphore_signal(barrier, inc=1, device_id=device, device_id_type=MESH_IDS)
            return carry

        lax.fori_loop(1, n, greet, 0)
    pl.semaphore_wait(barrier, math.prod(blk_sizes) + math.prod(rep_sizes) - 2)
    window_kernel(blk_sizes, rep_sizes, every, proj_ref, cot_ref, chosen_ref, sent_ref, out_c, back_c,
                  p_got, cot_got, ch_got, send_sem, recv_sem, local_sem, acc, greeted=True)
    tail_kernel(rep_sizes, blk_sizes, every, out_c, back_c, act_t, out_ref, weight_ref, full_ref, *tail_refs,
                greeted=True)


def fused(projected, cotangent, chosen, chosen_t, act_t, blk_sizes, rep_sizes, every, collective):
    reps, blks = math.prod(rep_sizes), math.prod(blk_sizes)
    span = chosen.shape[0]
    rows, width = projected.shape
    cols = width // reps
    vmem = pl.BlockSpec(memory_space=pltpu.VMEM)
    most = max(reps, blks)
    moved = (2 * rows * width * 2 + rows * rows * 2) * span + 3 * (reps * rows * cols * 6 + act_t.shape[-1] * cols * 4)
    return pl.pallas_call(
        functools.partial(fused_kernel, blk_sizes, rep_sizes, every),
        out_shape=(
            jax.ShapeDtypeStruct((rows, cols), jnp.bfloat16),
            jax.ShapeDtypeStruct((act_t.shape[-1] // blks, cols), jnp.float32),
            jax.ShapeDtypeStruct((rows, width), jnp.bfloat16),
        ),
        in_specs=[vmem] * 5,
        out_specs=(vmem, vmem, vmem),
        scratch_shapes=[
            pltpu.VMEM((reps, rows, cols), jnp.bfloat16),
            pltpu.VMEM((reps, rows, cols), jnp.bfloat16),
            pltpu.VMEM((span, rows, width), projected.dtype),
            pltpu.VMEM((span, rows, width), cotangent.dtype),
            pltpu.VMEM((span, rows, rows), chosen.dtype),
            pltpu.SemaphoreType.DMA((3, 4, span)),
            pltpu.SemaphoreType.DMA((3, 4, span)),
            pltpu.SemaphoreType.DMA((3, 4)),
            pltpu.VMEM((2, rows, width), jnp.float32),
            pltpu.VMEM((reps, rows, cols), jnp.bfloat16),
            pltpu.VMEM((reps, rows, cols), jnp.bfloat16),
            pltpu.VMEM((blks, act_t.shape[-1] // blks, cols), jnp.float32),
            pltpu.VMEM((reps, rows, cols), jnp.bfloat16),
            pltpu.VMEM((rows, cols), jnp.bfloat16),
            pltpu.VMEM((blks, act_t.shape[-1] // blks, cols), jnp.float32),
            pltpu.VMEM((rows, cols), jnp.float32),
            pltpu.VMEM((rows, cols), jnp.float32),
            pltpu.VMEM((act_t.shape[-1] // blks, cols), jnp.float32),
            pltpu.SemaphoreType.DMA((4, most)),
            pltpu.SemaphoreType.DMA((4, most)),
        ],
        compiler_params=pltpu.CompilerParams(collective_id=collective, has_side_effects=True),
        cost_estimate=pl.CostEstimate(
            flops=4 * span * rows * rows * width + 2 * act_t.shape[-1] * rows * cols,
            transcendentals=0,
            bytes_accessed=moved,
        ),
    )(projected, cotangent, chosen, chosen_t, act_t)


def shards(hidden_pre, adj_vals, adj_cols, w_out, cotangent):
    row_count, feature_width = hidden_pre.shape
    blk_count = lax.axis_size(BLK)
    rep_count = lax.axis_size(REP)
    span = blk_count // rep_count
    blk_pos = lax.axis_index(BLK)
    rep_pos = lax.axis_index(REP)
    cols_here = feature_width // rep_count
    slots = adj_vals.shape[1]

    hidden_act = jnp.maximum(hidden_pre, 0)
    projected = jnp.dot(hidden_act, w_out, preferred_element_type=jnp.float32).astype(jnp.bfloat16)
    own_vals = adj_vals[0]
    own_cols = adj_cols[0]
    section = jnp.mod(blk_pos - own_cols, blk_count) - rep_pos * span

    picks = (section[None, :] == jnp.arange(span, dtype=section.dtype)[:, None]).astype(own_vals.dtype)
    chosen = jnp.einsum("tk,kab->tab", picks, own_vals, preferred_element_type=jnp.float32).astype(own_vals.dtype)
    chosen_t = jnp.einsum("tk,kab->tba", picks, own_vals, preferred_element_type=jnp.float32).astype(own_vals.dtype)
    blk_sizes = tuple(lax.axis_size(a) for a in BLK)
    rep_sizes = tuple(lax.axis_size(a) for a in REP)
    out_part, grad_weight, back_full = fused(
        projected, cotangent, chosen, chosen_t, hidden_act, blk_sizes, rep_sizes, EVERY, 0
    )
    w_rows = lax.dynamic_slice_in_dim(w_out, rep_pos * cols_here, cols_here, 0)
    grad_in = lax.dot_general(
        back_full, w_rows, (((1,), (1,)), ((), ())), preferred_element_type=jnp.float32
    )
    pre_part = lax.dynamic_slice_in_dim(hidden_pre, rep_pos * cols_here, cols_here, 1)
    grad_pre = jnp.where(pre_part > 0, grad_in, 0.0).astype(jnp.bfloat16)
    return (out_part, grad_weight, grad_pre)


def solution(mesh):
    blk_count, rep_count = mesh.devices.shape
    fine = Mesh(mesh.devices.reshape(8, blk_count // 16, 2, rep_count // 2, 2), EVERY)
    placed = (P(BLK, None), P(BLK, REP, None, None), P(BLK, REP), P(), P(BLK, None))
    return jax.shard_map(
        shards,
        mesh=fine,
        in_specs=placed,
        out_specs=(P(BLK, REP), P(BLK, REP), P(BLK, REP)),
        check_vma=False,
    )
```
